32 devices in a mesh: dp: 16 (over z, y, x), tensor: 2 (over core).
Axes of the slice: x: 2, y: 2, z: 4, core: 2. Of those that a mesh axis runs over, the one named last changes fastest.
Arguments:
- hidden_in: bfloat16 [2, 8192, 768], P(None, 'dp'), may hold values from -6 to 6
- positions: int32 [2, 8192], P(None, 'dp'), may hold values from 0 to 1999, as said below
- out_grad: bfloat16 [2, 8192, 768], P(None, 'dp'), may hold values from -6 to 6
- norm1_gain: float32 [768], replicated, may hold values from 0.5 to 1.5
- norm1_bias: float32 [768], replicated, may hold values from -3 to 3
- norm2_gain: float32 [768], replicated, may hold values from 0.5 to 1.5
- norm2_bias: float32 [768], replicated, may hold values from -3 to 3
- query_weight: bfloat16 [768, 768], P('dp', 'tensor'), may hold values from -0.21875 to 0.21875
- query_bias: float32 [768], P('tensor'), may hold values from -3 to 3
- keyval_weight: bfloat16 [768, 128], P('dp', 'tensor'), may hold values from -0.21875 to 0.21875
- keyval_bias: float32 [128], P('tensor'), may hold values from -3 to 3
- attn_out_weight: bfloat16 [768, 768], P('tensor', 'dp'), may hold values from -4 to 4
- attn_out_bias: float32 [768], replicated, may hold values from -2 to 2
- up_weight: bfloat16 [768, 3072], P('dp', 'tensor'), may hold values from -0.21875 to 0.21875
- up_bias: float32 [3072], P('tensor'), may hold values from -3 to 3
- down_weight: bfloat16 [3072, 768], P('tensor', 'dp'), may hold values from -0.109375 to 0.109375
- down_bias: float32 [768], replicated, may hold values from -2 to 2
Outputs:
- layer_out: bfloat16 [2, 8192, 768], P(None, 'dp')
- keyval_out: bfloat16 [2, 8192, 128], P(None, 'dp')
- input_grad: bfloat16 [2, 8192, 768], P(None, 'dp')
- grad_norm1_gain: float32 [768], replicated
- grad_norm1_bias: float32 [768], replicated
- grad_norm2_gain: float32 [768], replicated
- grad_norm2_bias: float32 [768], replicated
- grad_query_weight: float32 [768, 768], P('dp', 'tensor')
- grad_query_bias: float32 [768], P('tensor')
- grad_keyval_weight: float32 [768, 128], P('dp', 'tensor')
- grad_keyval_bias: float32 [128], P('tensor')
- grad_attn_out_weight: float32 [768, 768], P('tensor', 'dp')
- grad_attn_out_bias: float32 [768], replicated
- grad_up_weight: float32 [768, 3072], P('dp', 'tensor')
- grad_up_bias: float32 [3072], P('tensor')
- grad_down_weight: float32 [3072, 768], P('tensor', 'dp')
- grad_down_bias: float32 [768], replicated
The draws below stay inside these ranges and needn't reach their ends.
Inputs may be any that keep to these rules, and one draw needn't show every extreme that they name: In each micro-batch's stream of 8192 tokens, positions count 0, 1, 2, ... within a document and restart at 0 where a new document begins; the stream begins with a document; every document except the last of a stream has 200 to 2000 tokens, and every stream holds a document of exactly 2000 tokens.
All inputs are finite; a program needn't handle non-finite values.
Results may differ from the reference program's by a relative error of at most 0.015.
Values may be sent and summed in bfloat16 or wider, within the bound.
A program may use at most 128 MiB of HBM per device.

```python
import jax
import jax.numpy as jnp
from jax import lax

D = 768
HEADS = 12
HDIM = 64
ROT = 16
FF = 3072
TOK_DEV = 512
MB = 2
DOC_MAX = 2000
DOC_MIN = 200
REACH = 4
TOKENS = 8192
HQ = 768


def draw_positions(key, part):
    streams = []
    doc_count = TOKENS // DOC_MIN + 1
    for micro_step in range(MB):
        micro_key = jax.random.fold_in(key, micro_step + 11)
        lengths = jax.random.randint(jax.random.fold_in(micro_key, 1), (doc_count,), DOC_MIN, DOC_MAX + 1)
        longest = jax.random.randint(jax.random.fold_in(micro_key, 2), (), 0, TOKENS // DOC_MAX)
        lengths = jnp.where(jnp.arange(doc_count) == longest, DOC_MAX, lengths).astype(jnp.int32)
        starts = jnp.cumsum(lengths) - lengths
        token_ids = jnp.arange(TOKENS, dtype=jnp.int32)
        owners = jnp.searchsorted(starts, token_ids, side='right') - 1
        streams.append(token_ids - starts[owners])
    return jnp.stack(streams).astype(jnp.int32)


def block_scale(key, shape, split, least, top_value):
    factor_of = 1.0
    for axis_at, parts in split:
        draws = jax.random.uniform(jax.random.fold_in(jax.random.fold_in(key, 6), axis_at), (parts,), jnp.float32, least / len(split), top_value / len(split))
        factor_of = factor_of * jnp.repeat(jnp.exp(draws), shape[axis_at] // parts).reshape((-1,) + (1,) * (len(shape) - 1 - axis_at))
    return factor_of


def scatter_about(rng, extent, deviation, most, pieces=(), kind=jnp.bfloat16):
    loudness = block_scale(rng, extent, pieces, -0.22, 0.18) if pieces else 1.0
    entries = jax.random.normal(rng, extent, jnp.float32) * deviation * loudness
    return jnp.minimum(jnp.maximum(entries, -most), most).astype(kind)


def setup_inputs(seed: int = 0) -> dict:
    key_list = jax.random.split(jax.random.key(seed), 18)
    return {
        "hidden_in": scatter_about(key_list[0], (MB, TOKENS, D), 1.0, 6.0, ((1, 16),)),
        "positions": draw_positions(jax.random.fold_in(key_list[17], 71), 0),
        "out_grad": scatter_about(key_list[2], (MB, TOKENS, D), 1.0, 6.0, ((1, 16),)),
        "norm1_gain": jnp.clip(1.0 + 0.1 * jax.random.normal(key_list[3], (D,), jnp.float32), 0.5, 1.5),
        "norm1_bias": scatter_about(key_list[4], (D,), 0.5, 3.0, (), jnp.float32),
        "norm2_gain": jnp.clip(1.0 + 0.1 * jax.random.normal(key_list[5], (D,), jnp.float32), 0.5, 1.5),
        "norm2_bias": scatter_about(key_list[6], (D,), 0.5, 3.0, (), jnp.float32),
        "query_weight": scatter_about(key_list[7], (D, HQ), D ** -0.5, 0.21875, ((0, 16), (1, 2))),
        "query_bias": scatter_about(key_list[8], (HQ,), 0.5, 3.0, ((0, 2),), jnp.float32),
        "keyval_weight": scatter_about(key_list[9], (D, 2 * HDIM), D ** -0.5, 0.21875, ((0, 16), (1, 2))),
        "keyval_bias": scatter_about(key_list[10], (2 * HDIM,), 0.5, 3.0, ((0, 2),), jnp.float32),
        "attn_out_weight": scatter_about(key_list[11], (HQ, D), 2 ** -0.5, 4.0, ((0, 2), (1, 16))),
        "attn_out_bias": scatter_about(key_list[12], (D,), 0.3, 2.0, (), jnp.float32),
        "up_weight": scatter_about(key_list[13], (D, FF), D ** -0.5, 0.21875, ((0, 16), (1, 2))),
        "up_bias": scatter_about(key_list[14], (FF,), 0.5, 3.0, ((0, 2),), jnp.float32),
        "down_weight": scatter_about(key_list[15], (FF, D), FF ** -0.5, 0.109375, ((0, 2), (1, 16))),
        "down_bias": scatter_about(key_list[16], (D,), 0.3, 2.0, (), jnp.float32),
    }


@jax.custom_vjp
def low(v):
    return lax.optimization_barrier(v.astype(jnp.bfloat16)).astype(jnp.float32)

@jax.custom_vjp
def low_back(v):
    return v

def low_keep(v):
    return (low(v), None)

def low_pass(kept, grad):
    return (grad,)

def back_keep(v):
    return (v, None)

def back_low(kept, grad):
    return (low(grad),)
low.defvjp(low_keep, low_pass)
low_back.defvjp(back_keep, back_low)
epsilon = 1e-05
highest = lax.Precision.HIGHEST

def layer_norm(stream, norm_gain, norm_bias):
    average = lax.optimization_barrier(jnp.mean(stream, axis=-1, keepdims=True))
    centered = stream - average
    spread = lax.optimization_barrier(jnp.mean(centered * centered, axis=-1, keepdims=True))
    return centered * lax.rsqrt(spread + epsilon) * norm_gain + norm_bias

def rotary_tables(places):
    inverse = 10000.0 ** (-(jnp.arange(ROT // 2, dtype=jnp.float32) * 2.0) / ROT)
    angles = places.astype(jnp.float32)[:, None] * inverse[None, :]
    angles = jnp.concatenate([angles, angles], axis=-1)
    return (jnp.cos(angles), jnp.sin(angles))

def rotate(values, cos_table, sine_table):
    head_part = values[..., :ROT]
    first_half = head_part[..., :ROT // 2]
    second_half = head_part[..., ROT // 2:]
    turned = jnp.concatenate([-second_half, first_half], axis=-1)
    spun_part = head_part * cos_table[:, None, :] + turned * sine_table[:, None, :]
    return jnp.concatenate([spun_part, values[..., ROT:]], axis=-1)

def attention(queries, keyval, places):
    tokens = queries.shape[0]
    block_len = TOK_DEV
    window = (REACH + 1) * block_len
    block_count = tokens // block_len
    padded = jnp.concatenate([jnp.zeros((REACH * block_len, 2 * HDIM), keyval.dtype), keyval], axis=0)
    q_blocks = queries.reshape(block_count, block_len, HEADS, HDIM)
    p_blocks = places.reshape(block_count, block_len)
    starts = jnp.arange(block_count, dtype=jnp.int32) * block_len

    def one_block(inputs):
        q_block, p_block, block_start = inputs
        window_rows = lax.dynamic_slice_in_dim(padded, block_start, window, 0)
        key_rows = window_rows[:, :HDIM]
        value_rows = window_rows[:, HDIM:]
        scores = low_back(jnp.einsum('thd,kd->htk', q_block, key_rows, precision=highest))
        row_ids = jnp.arange(block_len, dtype=jnp.int32)
        col_ids = jnp.arange(window, dtype=jnp.int32)
        offsets = REACH * block_len + row_ids[:, None] - col_ids[None, :]
        visible = ((offsets >= 0) & (offsets <= p_block[:, None]))[None]
        masked = jnp.where(visible, scores, -1e+30)
        top_score = lax.optimization_barrier(jnp.max(masked, axis=-1, keepdims=True))
        weights_full = jnp.where(visible, jnp.exp(masked - top_score), 0.0)
        weights_full = weights_full / lax.optimization_barrier(jnp.sum(weights_full, axis=-1, keepdims=True))
        weights_low = low(weights_full)
        return jnp.einsum('htk,kd->thd', weights_low, value_rows, precision=highest)
    mixture = lax.map(jax.checkpoint(one_block), (q_blocks, p_blocks, starts))
    return mixture.reshape(tokens, HEADS, HDIM)

def block_forward(stream, places, params):
    n1g, n1b, n2g, n2b, wq, bq, wkv, bkv, wo, bo, wu, bu, wd, bd = params
    tokens = stream.shape[0]
    normed1 = low(layer_norm(stream, n1g, n1b))
    normed2 = low(layer_norm(stream, n2g, n2b))
    cos_table, sine_table = rotary_tables(places)
    query_lin = low_back(jnp.dot(normed1, wq, precision=highest) + bq)
    queries = low(rotate(query_lin.reshape(tokens, HEADS, HDIM), cos_table, sine_table) * HDIM ** (-0.5))
    keyval_lin = low_back(jnp.dot(normed1, wkv, precision=highest) + bkv)
    spun_keys = rotate(keyval_lin[:, None, :HDIM], cos_table, sine_table)[:, 0, :]
    keyval = low(jnp.concatenate([spun_keys, keyval_lin[:, HDIM:]], axis=-1))
    mixture = low(low_back(attention(queries, keyval, places).reshape(tokens, HQ)))
    up_lin = low_back(jnp.dot(normed2, wu, precision=highest) + bu)
    activated = low(jax.nn.gelu(up_lin, approximate=False))
    attn_branch = jnp.dot(mixture, wo, precision=highest) + bo
    ffn_branch = jnp.dot(activated, wd, precision=highest) + bd
    return (stream + attn_branch + ffn_branch, keyval)

def reference(hidden_in, positions, out_grad, norm1_gain, norm1_bias, norm2_gain, norm2_bias, query_weight, query_bias, keyval_weight, keyval_bias, attn_out_weight, attn_out_bias, up_weight, up_bias, down_weight, down_bias):
    params = tuple((item.astype(jnp.float32) for item in (norm1_gain, norm1_bias, norm2_gain, norm2_bias, query_weight, query_bias, keyval_weight, keyval_bias, attn_out_weight, attn_out_bias, up_weight, up_bias, down_weight, down_bias)))

    def forward_all(stream_all, *weights):
        layer_rows = []
        cache_rows = []
        for micro_step in range(MB):
            result, cache = block_forward(stream_all[micro_step], positions[micro_step], weights)
            layer_rows.append(result)
            cache_rows.append(cache)
        return (jnp.stack(layer_rows), jnp.stack(cache_rows))
    layer_out, pullback, keyval_out = jax.vjp(forward_all, hidden_in.astype(jnp.float32), *params, has_aux=True)
    gradients = pullback(out_grad.astype(jnp.float32))
    return (layer_out.astype(jnp.bfloat16), keyval_out.astype(jnp.bfloat16), gradients[0].astype(jnp.bfloat16), gradients[1], gradients[2], gradients[3], gradients[4], gradients[5], gradients[6], gradients[7], gradients[8], gradients[9], gradients[10], gradients[11], gradients[12], gradients[13], gradients[14])
```

```python
import functools

import jax
import jax.numpy as jnp
from jax import lax
from jax.experimental import pallas as pl
from jax.experimental.pallas import tpu as pltpu
from jax.sharding import PartitionSpec as P

HDIM = 64
ROT = 16
REACH = 4


epsilon = 1e-05


def shifted(value, axis, steps):
    count = lax.axis_size(axis)
    initial, last = (max(0, -steps), min(count, count - steps))
    return lax.ppermute(value, axis, [(source, source + steps) for source in range(initial, last)])


def norm_forward(stream):
    average = jnp.mean(stream, axis=-1, keepdims=True)
    centered = stream - average
    spread = jnp.mean(centered * centered, axis=-1, keepdims=True)
    scaling = lax.rsqrt(spread + epsilon)
    normed = centered * scaling
    return (normed, scaling)


def norm_backward(upstream, normed, scaling, norm_gain):
    weighted = upstream * norm_gain
    return scaling * (
        weighted
        - jnp.mean(weighted, axis=-1, keepdims=True)
        - normed * jnp.mean(weighted * normed, axis=-1, keepdims=True)
    )


def rotary_tables(places):
    inverse = 10000.0 ** (-(jnp.arange(ROT // 2, dtype=jnp.float32) * 2.0) / ROT)
    angles = places.astype(jnp.float32)[:, None] * inverse[None, :]
    angles = jnp.concatenate([angles, angles], axis=-1)
    return (jnp.cos(angles), jnp.sin(angles))


def rotate(values, cos_table, sine_table):
    head_part = values[..., :ROT]
    first_half = head_part[..., : ROT // 2]
    second_half = head_part[..., ROT // 2 :]
    turned = jnp.concatenate([-second_half, first_half], axis=-1)
    spun_part = head_part * cos_table[:, None, :] + turned * sine_table[:, None, :]
    return jnp.concatenate([spun_part, values[..., ROT:]], axis=-1)


def gelu_exact(values):
    return jax.nn.gelu(values, approximate=False)


MESH = pl.DeviceIdType.MESH


def grid_place():
    me = lax.axis_index("dp")
    return me // 4, (me // 2) % 2, me % 2


def place_id(z, y, x):
    return {"dp": z * 4 + y * 2 + x}


def barrier(peers):
    b=pltpu.get_barrier_semaphore()
    for p in peers:
        pl.semaphore_signal(b,inc=1,device_id=p,device_id_type=MESH)
    pl.semaphore_wait(b,len(peers))

def gather_kernel(chunks, in_ref, out_ref, zs, zr, s2s, s2r, s3s, s3r):
    z,y,x=grid_place()
    peers=[place_id((z+d)%4,y,x) for d in (1,2,3)]+[place_id(z,1-y,x),place_id(z,y,1-x)]
    barrier(peers)
    def rc(src,dst,ss,rs,d):
        return pltpu.make_async_remote_copy(src_ref=src,dst_ref=dst,send_sem=ss,recv_sem=rs,device_id=d,device_id_type=MESH)
    C={}
    def s1(k):
        c0,c1=chunks[k]; cs=pl.ds(c0,c1-c0)
        C[k,1]=[rc(in_ref.at[:,cs],out_ref.at[z,y,x,:,cs],zs.at[k,d-1],zr.at[k,d-1],place_id((z+d)%4,y,x)) for d in (1,2,3)]
        for c in C[k,1]: c.start()
    def s2(k):
        for c in C[k,1]: c.wait_recv()
        c0,c1=chunks[k]; cs=pl.ds(c0,c1-c0)
        r=out_ref.at[:,y,x,:,cs]
        C[k,2]=rc(r,r,s2s.at[k],s2r.at[k],place_id(z,y,1-x) if k%2==0 else place_id(z,1-y,x))
        C[k,2].start()
    def s3(k):
        C[k,2].wait_recv()
        c0,c1=chunks[k]; cs=pl.ds(c0,c1-c0)
        if k%2==0:
            r=out_ref.at[:,y,:,:,cs]; d=place_id(z,1-y,x)
        else:
            r=out_ref.at[:,:,x,:,cs]; d=place_id(z,y,1-x)
        C[k,3]=rc(r,r,s3s.at[k],s3r.at[k],d)
        C[k,3].start()
    out_ref[z,y,x]=in_ref[...]
    n=len(chunks)
    for k in range(n): s1(k)
    for t in range(n+1):
        if t<n: s2(t)
        if t>=1: s3(t-1)
    for k in range(n):
        C[k,3].wait_recv()
    for k in range(n):
        for c in C[k,1]: c.wait_send()
        C[k,2].wait_send(); C[k,3].wait_send()

def gather(shard, chunks):
    rows,cols=shard.shape
    n=len(chunks)
    D=pltpu.SemaphoreType.DMA
    return pl.pallas_call(functools.partial(gather_kernel,chunks),
        out_shape=jax.ShapeDtypeStruct((4,2,2,rows,cols),shard.dtype),
        in_specs=[pl.BlockSpec(memory_space=pltpu.VMEM)],
        out_specs=pl.BlockSpec(memory_space=pltpu.VMEM),
        scratch_shapes=[D((n,3)),D((n,3)),D((n,)),D((n,)),D((n,)),D((n,))],
        compiler_params=pltpu.CompilerParams(collective_id=0,has_side_effects=True,vmem_limit_bytes=40<<20),
        name="gather_w")(shard)

def rs_kernel(chunks, g_ref, out_ref, r1, r2, r3, s1s,s1r,s2s,s2r,zs,zr):
    z,y,x=grid_place()
    peers=[place_id((z+d)%4,y,x) for d in (1,2,3)]+[place_id(z,1-y,x),place_id(z,y,1-x)]
    barrier(peers)
    def rc(src,dst,ss,rs,d):
        return pltpu.make_async_remote_copy(src_ref=src,dst_ref=dst,send_sem=ss,recv_sem=rs,device_id=d,device_id_type=MESH)
    C={}
    def cs_of(k):
        c0,c1=chunks[k]; return pl.ds(c0,c1-c0)
    def a(k):
        cs=cs_of(k)
        if k%2==0: src=g_ref.at[:,:,1-x,:,cs]; d=place_id(z,y,1-x)
        else: src=g_ref.at[:,1-y,:,:,cs]; d=place_id(z,1-y,x)
        C[k,1]=rc(src,r1.at[:,:,:,cs],s1s.at[k],s1r.at[k],d); C[k,1].start()
    def b(k):
        C[k,1].wait_recv()
        cs=cs_of(k)
        def body(i,_):
            zz=i//2; yy=i%2
            mine=g_ref[zz,yy,x,:,cs] if k%2==0 else g_ref[zz,y,yy,:,cs]
            r1[zz,yy,:,cs]=r1[zz,yy,:,cs]+mine
            return 0
        lax.fori_loop(0,8,body,0)
        o=y if k%2==0 else x
        d=place_id(z,1-y,x) if k%2==0 else place_id(z,y,1-x)
        C[k,2]=rc(r1.at[:,1-o,:,cs],r2.at[:,:,cs],s2s.at[k],s2r.at[k],d); C[k,2].start()
    def c(k):
        C[k,2].wait_recv()
        cs=cs_of(k)
        o=y if k%2==0 else x
        def body(i,_):
            r2[i,:,cs]=r2[i,:,cs]+r1[i,o,:,cs]
            return 0
        lax.fori_loop(0,4,body,0)
        C[k,3]=[rc(r2.at[(z+d)%4,:,cs],r3.at[d-1,:,cs],zs.at[k,d-1],zr.at[k,d-1],place_id((z+d)%4,y,x)) for d in (1,2,3)]
        for q in C[k,3]: q.start()
    def e(k):
        cs=cs_of(k)
        for q in C[k,3]: q.wait_recv()
        out_ref[:,cs]=(r2[z,:,cs].astype(jnp.float32)+r3[0,:,cs].astype(jnp.float32))+(r3[1,:,cs].astype(jnp.float32)+r3[2,:,cs].astype(jnp.float32))
    n=len(chunks)
    for k in range(n): a(k)
    for t in range(n+2):
        if t<n: b(t)
        if 0<=t-1<n: c(t-1)
        if 0<=t-2<n: e(t-2)
    for k in range(n):
        C[k,1].wait_send(); C[k,2].wait_send()
        for q in C[k,3]: q.wait_send()

def rscat(g, chunks):
    _,_,_,rows,cols=g.shape
    n=len(chunks)
    D=pltpu.SemaphoreType.DMA
    V=pltpu.VMEM
    return pl.pallas_call(functools.partial(rs_kernel,chunks),
        out_shape=jax.ShapeDtypeStruct((rows,cols),jnp.float32),
        in_specs=[pl.BlockSpec(memory_space=pltpu.VMEM)],
        out_specs=pl.BlockSpec(memory_space=pltpu.VMEM),
        scratch_shapes=[V((4,2,rows,cols),jnp.bfloat16),V((4,rows,cols),jnp.bfloat16),V((3,rows,cols),jnp.bfloat16),
            D((n,)),D((n,)),D((n,)),D((n,)),D((n,3)),D((n,3))],
        compiler_params=pltpu.CompilerParams(collective_id=1,has_side_effects=True,vmem_limit_bytes=40<<20),
        name="rscat_g")(g)

def column_chunks(columns, parts):
    width = columns // 128
    edges = [round(i * width / parts) * 128 for i in range(parts + 1)]
    return [(edges[i], edges[i + 1]) for i in range(parts)]


def pack_columns(query_part, keyval_part, out_part, up_part, down_part):
    packed = jnp.concatenate([query_part, out_part, up_part, down_part, keyval_part], axis=1)
    pad = -packed.shape[1] % 128
    return jnp.pad(packed, ((0, 0), (0, pad)))


def unpack_columns(packed, widths):
    pieces = []
    at = 0
    for width in widths:
        pieces.append(packed[:, at : at + width])
        at += width
    query_part, out_part, up_part, down_part, keyval_part = pieces
    return query_part, keyval_part, out_part, up_part, down_part


def gather_rows(shard):
    count = lax.axis_size("dp")
    if count == 16 and shard.shape[0] % 16 == 0:
        gathered = gather(shard, column_chunks(shard.shape[1], 8))
        return gathered.reshape(count * shard.shape[0], shard.shape[1])
    return lax.all_gather(shard, "dp", axis=0, tiled=True)


def scatter_rows(partial):
    count = lax.axis_size("dp")
    rows = partial.shape[0] // count
    if count == 16 and rows % 16 == 0:
        return rscat(partial.reshape(4, 2, 2, rows, partial.shape[1]), column_chunks(partial.shape[1], 8))
    return lax.psum_scatter(partial, "dp", scatter_dimension=0, tiled=True).astype(jnp.float32)


def fetch_weights(shard_weights):
    query_w, keyval_w, out_w, up_w, down_w = shard_weights
    packed = pack_columns(query_w, keyval_w, out_w.T, up_w, down_w.T)
    widths = (query_w.shape[1], out_w.shape[0], up_w.shape[1], down_w.shape[0], keyval_w.shape[1])
    full = gather_rows(packed)
    w_query, w_keyval, w_out, w_up, w_down = unpack_columns(full, widths)
    return (w_query, w_keyval, w_out.T, w_up, w_down.T)


def score_block(queries, key_rows, places, reach_step):
    tokens_here = queries.shape[1]
    scores = jnp.einsum("htd,kd->htk", queries, key_rows, preferred_element_type=jnp.float32)
    row_ids = jnp.arange(tokens_here, dtype=jnp.int32)
    offsets = reach_step * tokens_here + row_ids[:, None] - row_ids[None, :]
    visible = (offsets >= 0) & (offsets <= places[:, None])
    return (scores, visible[None])


def attend_forward(queries, blocks, places):
    heads_here, tokens_here = (queries.shape[0], queries.shape[1])
    top_score = jnp.full((heads_here, tokens_here), -1e30, jnp.float32)
    totals = jnp.zeros((heads_here, tokens_here), jnp.float32)
    for reach_step, kv_block in enumerate(blocks):
        scores, visible = score_block(queries, kv_block[:, :HDIM], places, reach_step)
        masked = jnp.where(visible, scores, -1e30)
        new_top = jnp.maximum(top_score, jnp.max(masked, axis=-1))
        totals = totals * jnp.exp(top_score - new_top) + jnp.sum(
            jnp.where(visible, jnp.exp(masked - new_top[..., None]), 0.0), axis=-1
        )
        top_score = new_top
    log_sum = top_score + jnp.log(totals)
    mixture = jnp.zeros((heads_here, tokens_here, HDIM), jnp.float32)
    for reach_step, kv_block in enumerate(blocks):
        scores, visible = score_block(queries, kv_block[:, :HDIM], places, reach_step)
        weights_low = jnp.where(visible, jnp.exp(scores - log_sum[..., None]), 0.0).astype(
            jnp.bfloat16
        )
        mixture = mixture + jnp.einsum(
            "htk,kd->htd", weights_low, kv_block[:, HDIM:], preferred_element_type=jnp.float32
        )
    return (mixture, log_sum)


def attend_backward(queries, blocks, places, log_sum, grad_mixture, row_dots):
    grad_queries = jnp.zeros(queries.shape, jnp.float32)
    key_terms = []
    for reach_step, kv_block in enumerate(blocks):
        key_rows = kv_block[:, :HDIM]
        value_rows = kv_block[:, HDIM:]
        scores, visible = score_block(queries, key_rows, places, reach_step)
        weights_full = jnp.where(visible, jnp.exp(scores - log_sum[..., None]), 0.0)
        weights_low = weights_full.astype(jnp.bfloat16)
        grad_weights = jnp.einsum(
            "htd,kd->htk", grad_mixture, value_rows, preferred_element_type=jnp.float32
        )
        grad_scores = (weights_full * (grad_weights - row_dots[..., None])).astype(jnp.bfloat16)
        grad_queries = grad_queries + jnp.einsum(
            "htk,kd->htd", grad_scores, key_rows, preferred_element_type=jnp.float32
        )
        grad_keys = jnp.einsum(
            "htk,htd->kd", grad_scores, queries, preferred_element_type=jnp.float32
        )
        grad_values = jnp.einsum(
            "htk,htd->kd", weights_low, grad_mixture, preferred_element_type=jnp.float32
        )
        key_terms.append(jnp.concatenate([grad_keys, grad_values], axis=-1))
    return (grad_queries, key_terms)


def on_device(
    hidden_in,
    positions,
    out_grad,
    norm1_gain,
    norm1_bias,
    norm2_gain,
    norm2_bias,
    query_weight,
    query_bias,
    keyval_weight,
    keyval_bias,
    attn_out_weight,
    attn_out_bias,
    up_weight,
    up_bias,
    down_weight,
    down_bias,
):
    micro_count = hidden_in.shape[0]
    tokens_here = hidden_in.shape[1]
    width = hidden_in.shape[2]
    dp_count = lax.axis_size("dp")
    first_core = lax.axis_index("tensor") == 0
    heads_here = query_bias.shape[0] // HDIM
    query_scale = HDIM ** (-0.5)
    shard_weights = (query_weight, keyval_weight, attn_out_weight, up_weight, down_weight)
    grad_query_w = jnp.zeros((width, query_weight.shape[1]), jnp.float32)
    grad_keyval_w = jnp.zeros((width, keyval_weight.shape[1]), jnp.float32)
    grad_out_w = jnp.zeros(
        (attn_out_weight.shape[0], attn_out_weight.shape[1] * dp_count), jnp.float32
    )
    grad_up_w = jnp.zeros((width, up_weight.shape[1]), jnp.float32)
    grad_down_w = jnp.zeros((down_weight.shape[0], down_weight.shape[1] * dp_count), jnp.float32)
    grad_n1_gain = jnp.zeros((width,), jnp.float32)
    grad_n1_bias = jnp.zeros((width,), jnp.float32)
    grad_n2_gain = jnp.zeros((width,), jnp.float32)
    grad_n2_bias = jnp.zeros((width,), jnp.float32)
    grad_row_sum = jnp.zeros((width,), jnp.float32)
    grad_query_b = jnp.zeros(query_bias.shape, jnp.float32)
    grad_keyval_b = jnp.zeros(keyval_bias.shape, jnp.float32)
    grad_up_b = jnp.zeros(up_bias.shape, jnp.float32)
    layer_rows = []
    cache_rows = []
    input_rows = []
    gathered = fetch_weights(shard_weights)
    for micro_step in range(micro_count):
        w_query, w_keyval, w_out, w_up, w_down = gathered
        stream = hidden_in[micro_step].astype(jnp.float32)
        places = positions[micro_step]
        normed, scaling = norm_forward(stream)
        low_first = (normed * norm1_gain + norm1_bias).astype(jnp.bfloat16)
        low_second = (normed * norm2_gain + norm2_bias).astype(jnp.bfloat16)
        cos_table, sine_table = rotary_tables(places)
        query_lin = jnp.dot(low_first, w_query, preferred_element_type=jnp.float32) + query_bias
        queries = (
            rotate(query_lin.reshape(tokens_here, heads_here, HDIM), cos_table, sine_table)
            * query_scale
        ).astype(jnp.bfloat16)
        query_heads = jnp.transpose(queries, (1, 0, 2))
        half_lin = jnp.dot(low_first, w_keyval, preferred_element_type=jnp.float32) + keyval_bias
        spun_half = rotate(half_lin[:, None, :], cos_table, sine_table)[:, 0, :]
        half_low = jnp.where(first_core, spun_half, half_lin).astype(jnp.bfloat16)
        keyval = lax.all_gather(half_low, "tensor", axis=1, tiled=True)
        blocks = [keyval] + [
            shifted(keyval, "dp", reach_step) for reach_step in range(1, REACH + 1)
        ]
        mixture, log_sum = attend_forward(query_heads, blocks, places)
        mixture_low = (
            jnp.transpose(mixture, (1, 0, 2))
            .reshape(tokens_here, heads_here * HDIM)
            .astype(jnp.bfloat16)
        )
        up_lin = jnp.dot(low_second, w_up, preferred_element_type=jnp.float32) + up_bias
        active_low = gelu_exact(up_lin).astype(jnp.bfloat16)
        branch_part = jnp.dot(mixture_low, w_out, preferred_element_type=jnp.float32) + jnp.dot(
            active_low, w_down, preferred_element_type=jnp.float32
        )
        branches = lax.psum(branch_part.astype(jnp.bfloat16), "tensor").astype(jnp.float32)
        layer_rows.append((stream + branches + attn_out_bias + down_bias).astype(jnp.bfloat16))
        cache_rows.append(keyval)
        grad_low = out_grad[micro_step]
        grad_rows = grad_low.astype(jnp.float32)
        grad_row_sum = grad_row_sum + jnp.sum(grad_rows, axis=0)
        grad_out_w = grad_out_w + jnp.einsum(
            "th,td->hd", mixture_low, grad_low, preferred_element_type=jnp.float32
        )
        grad_down_w = grad_down_w + jnp.einsum(
            "tf,td->fd", active_low, grad_low, preferred_element_type=jnp.float32
        )
        grad_active = jnp.einsum("td,fd->tf", grad_low, w_down, preferred_element_type=jnp.float32)
        gelu_values, gelu_pull = jax.vjp(gelu_exact, up_lin)
        grad_up_low = gelu_pull(grad_active)[0].astype(jnp.bfloat16)
        grad_up_b = grad_up_b + jnp.sum(grad_up_low.astype(jnp.float32), axis=0)
        grad_up_w = grad_up_w + jnp.einsum(
            "td,tf->df", low_second, grad_up_low, preferred_element_type=jnp.float32
        )
        second_part = jnp.einsum("tf,df->td", grad_up_low, w_up, preferred_element_type=jnp.float32)
        grad_mix_low = jnp.einsum(
            "td,hd->th", grad_low, w_out, preferred_element_type=jnp.float32
        ).astype(jnp.bfloat16)
        grad_mixture = jnp.transpose(grad_mix_low.reshape(tokens_here, heads_here, HDIM), (1, 0, 2))
        row_dots = jnp.sum(grad_mixture.astype(jnp.float32) * mixture, axis=-1)
        grad_queries, key_terms = attend_backward(
            query_heads, blocks, places, log_sum, grad_mixture, row_dots
        )
        keyval_grad = key_terms[0]
        for reach_step in range(1, REACH + 1):
            keyval_grad = keyval_grad + shifted(
                key_terms[reach_step].astype(jnp.bfloat16), "dp", -reach_step
            ).astype(jnp.float32)
        half_grad = lax.psum_scatter(
            keyval_grad.astype(jnp.bfloat16), "tensor", scatter_dimension=1, tiled=True
        ).astype(jnp.float32)
        unspun_half = rotate(half_grad[:, None, :], cos_table, -sine_table)[:, 0, :]
        half_grad_low = jnp.where(first_core, unspun_half, half_grad).astype(jnp.bfloat16)
        grad_keyval_b = grad_keyval_b + jnp.sum(half_grad_low.astype(jnp.float32), axis=0)
        grad_keyval_w = grad_keyval_w + jnp.einsum(
            "td,tk->dk", low_first, half_grad_low, preferred_element_type=jnp.float32
        )
        query_rows = jnp.transpose(grad_queries, (1, 0, 2)) * query_scale
        grad_query_low = (
            rotate(query_rows, cos_table, -sine_table)
            .reshape(tokens_here, heads_here * HDIM)
            .astype(jnp.bfloat16)
        )
        grad_query_b = grad_query_b + jnp.sum(grad_query_low.astype(jnp.float32), axis=0)
        grad_query_w = grad_query_w + jnp.einsum(
            "td,tq->dq", low_first, grad_query_low, preferred_element_type=jnp.float32
        )
        first_part = jnp.einsum(
            "tq,dq->td", grad_query_low, w_query, preferred_element_type=jnp.float32
        ) + jnp.einsum("tk,dk->td", half_grad_low, w_keyval, preferred_element_type=jnp.float32)
        grad_first, grad_second = (
            lax.psum(first_part.astype(jnp.bfloat16), "tensor").astype(jnp.float32),
            lax.psum(second_part.astype(jnp.bfloat16), "tensor").astype(jnp.float32),
        )
        grad_n1_gain = grad_n1_gain + jnp.sum(grad_first * normed, axis=0)
        grad_n1_bias = grad_n1_bias + jnp.sum(grad_first, axis=0)
        grad_n2_gain = grad_n2_gain + jnp.sum(grad_second * normed, axis=0)
        grad_n2_bias = grad_n2_bias + jnp.sum(grad_second, axis=0)
        input_total = (
            grad_rows
            + norm_backward(grad_first, normed, scaling, norm1_gain)
            + norm_backward(grad_second, normed, scaling, norm2_gain)
        )
        input_rows.append(input_total.astype(jnp.bfloat16))
    packed_grads = pack_columns(
        grad_query_w, grad_keyval_w, grad_out_w.T, grad_up_w, grad_down_w.T
    ).astype(jnp.bfloat16)
    own_grads = scatter_rows(packed_grads)
    summed_query, summed_keyval, summed_out, summed_up, summed_down = unpack_columns(
        own_grads,
        (
            query_weight.shape[1],
            attn_out_weight.shape[0],
            up_weight.shape[1],
            down_weight.shape[0],
            keyval_weight.shape[1],
        ),
    )
    summed_out = summed_out.T
    summed_down = summed_down.T
    vector_sums = lax.psum(
        (
            grad_n1_gain,
            grad_n1_bias,
            grad_n2_gain,
            grad_n2_bias,
            grad_row_sum,
            grad_query_b,
            grad_keyval_b,
            grad_up_b,
        ),
        "dp",
    )
    (
        sum_n1_gain,
        sum_n1_bias,
        sum_n2_gain,
        sum_n2_bias,
        sum_rows,
        sum_query_b,
        sum_keyval_b,
        sum_up_b,
    ) = vector_sums
    return (
        jnp.stack(layer_rows),
        jnp.stack(cache_rows),
        jnp.stack(input_rows),
        sum_n1_gain,
        sum_n1_bias,
        sum_n2_gain,
        sum_n2_bias,
        summed_query,
        sum_query_b,
        summed_keyval,
        sum_keyval_b,
        summed_out,
        sum_rows,
        summed_up,
        sum_up_b,
        summed_down,
        sum_rows,
    )


def solution(mesh):
    return jax.shard_map(
        on_device,
        mesh=mesh,
        in_specs=(
            P(None, "dp", None),
            P(None, "dp"),
            P(None, "dp", None),
            P(),
            P(),
            P(),
            P(),
            P("dp", "tensor"),
            P("tensor"),
            P("dp", "tensor"),
            P("tensor"),
            P("tensor", "dp"),
            P(),
            P("dp", "tensor"),
            P("tensor"),
            P("tensor", "dp"),
            P(),
        ),
        out_specs=(
            P(None, "dp", None),
            P(None, "dp", None),
            P(None, "dp", None),
            P(),
            P(),
            P(),
            P(),
            P("dp", "tensor"),
            P("tensor"),
            P("dp", "tensor"),
            P("tensor"),
            P("tensor", "dp"),
            P(),
            P("dp", "tensor"),
            P("tensor"),
            P("tensor", "dp"),
            P(),
        ),
        check_vma=False,
    )
```

```python
import functools
import jax
import jax.numpy as jnp
from jax import lax
from jax.experimental import pallas as pl
from jax.experimental.pallas import tpu as pltpu
from jax.sharding import PartitionSpec as P

HDIM = 64
ROT = 16
REACH = 4
epsilon = 1e-05
MESH = pl.DeviceIdType.MESH
LOW = -1e30
F32 = jnp.float32
BF16 = jnp.bfloat16


def shifted(value, axis, steps):
    count = lax.axis_size(axis)
    initial, last = (max(0, -steps), min(count, count - steps))
    return lax.ppermute(value, axis, [(source, source + steps) for source in range(initial, last)])


def norm_forward(stream):
    average = jnp.mean(stream, axis=-1, keepdims=True)
    centered = stream - average
    spread = jnp.mean(centered * centered, axis=-1, keepdims=True)
    scaling = lax.rsqrt(spread + epsilon)
    normed = centered * scaling
    return (normed, scaling)


def norm_backward(upstream, normed, scaling, norm_gain):
    weighted = upstream * norm_gain
    return scaling * (
        weighted
        - jnp.mean(weighted, axis=-1, keepdims=True)
        - normed * jnp.mean(weighted * normed, axis=-1, keepdims=True)
    )


def rotary_tables(places):
    inverse = 10000.0 ** (-(jnp.arange(ROT // 2, dtype=jnp.float32) * 2.0) / ROT)
    angles = places.astype(jnp.float32)[:, None] * inverse[None, :]
    angles = jnp.concatenate([angles, angles], axis=-1)
    return (jnp.cos(angles), jnp.sin(angles))


def rotate(values, cos_table, sine_table):
    head_part = values[..., :ROT]
    first_half = head_part[..., : ROT // 2]
    second_half = head_part[..., ROT // 2 :]
    turned = jnp.concatenate([-second_half, first_half], axis=-1)
    spun_part = head_part * cos_table[:, None, :] + turned * sine_table[:, None, :]
    return jnp.concatenate([spun_part, values[..., ROT:]], axis=-1)


def gelu_exact(values):
    return jax.nn.gelu(values, approximate=False)


def fetch_weights(shard_weights):
    return (
        lax.all_gather(shard_weights[0], "dp", axis=0, tiled=True),
        lax.all_gather(shard_weights[1], "dp", axis=0, tiled=True),
        lax.all_gather(shard_weights[2], "dp", axis=1, tiled=True),
        lax.all_gather(shard_weights[3], "dp", axis=0, tiled=True),
        lax.all_gather(shard_weights[4], "dp", axis=1, tiled=True),
    )


def score_block(queries, key_rows, places, reach_step):
    tokens_here = queries.shape[1]
    scores = jnp.einsum("htd,kd->htk", queries, key_rows, preferred_element_type=jnp.float32)
    row_ids = jnp.arange(tokens_here, dtype=jnp.int32)
    offsets = reach_step * tokens_here + row_ids[:, None] - row_ids[None, :]
    visible = (offsets >= 0) & (offsets <= places[:, None])
    return (scores, visible[None])


def attend_forward(queries, blocks, places):
    heads_here, tokens_here = (queries.shape[0], queries.shape[1])
    top_score = jnp.full((heads_here, tokens_here), -1e30, jnp.float32)
    totals = jnp.zeros((heads_here, tokens_here), jnp.float32)
    for reach_step, kv_block in enumerate(blocks):
        scores, visible = score_block(queries, kv_block[:, :HDIM], places, reach_step)
        masked = jnp.where(visible, scores, -1e30)
        new_top = jnp.maximum(top_score, jnp.max(masked, axis=-1))
        totals = totals * jnp.exp(top_score - new_top) + jnp.sum(
            jnp.where(visible, jnp.exp(masked - new_top[..., None]), 0.0), axis=-1
        )
        top_score = new_top
    log_sum = top_score + jnp.log(totals)
    mixture = jnp.zeros((heads_here, tokens_here, HDIM), jnp.float32)
    for reach_step, kv_block in enumerate(blocks):
        scores, visible = score_block(queries, kv_block[:, :HDIM], places, reach_step)
        weights_low = jnp.where(visible, jnp.exp(scores - log_sum[..., None]), 0.0).astype(
            jnp.bfloat16
        )
        mixture = mixture + jnp.einsum(
            "htk,kd->htd", weights_low, kv_block[:, HDIM:], preferred_element_type=jnp.float32
        )
    return (mixture, log_sum)


def attend_backward(queries, blocks, places, log_sum, grad_mixture, row_dots):
    grad_queries = jnp.zeros(queries.shape, jnp.float32)
    key_terms = []
    for reach_step, kv_block in enumerate(blocks):
        key_rows = kv_block[:, :HDIM]
        value_rows = kv_block[:, HDIM:]
        scores, visible = score_block(queries, key_rows, places, reach_step)
        weights_full = jnp.where(visible, jnp.exp(scores - log_sum[..., None]), 0.0)
        weights_low = weights_full.astype(jnp.bfloat16)
        grad_weights = jnp.einsum(
            "htd,kd->htk", grad_mixture, value_rows, preferred_element_type=jnp.float32
        )
        grad_scores = (weights_full * (grad_weights - row_dots[..., None])).astype(jnp.bfloat16)
        grad_queries = grad_queries + jnp.einsum(
            "htk,kd->htd", grad_scores, key_rows, preferred_element_type=jnp.float32
        )
        grad_keys = jnp.einsum(
            "htk,htd->kd", grad_scores, queries, preferred_element_type=jnp.float32
        )
        grad_values = jnp.einsum(
            "htk,htd->kd", weights_low, grad_mixture, preferred_element_type=jnp.float32
        )
        key_terms.append(jnp.concatenate([grad_keys, grad_values], axis=-1))
    return (grad_queries, key_terms)


def plain_layer(
    hidden_in,
    positions,
    out_grad,
    norm1_gain,
    norm1_bias,
    norm2_gain,
    norm2_bias,
    query_weight,
    query_bias,
    keyval_weight,
    keyval_bias,
    attn_out_weight,
    attn_out_bias,
    up_weight,
    up_bias,
    down_weight,
    down_bias,
):
    micro_count = hidden_in.shape[0]
    tokens_here = hidden_in.shape[1]
    width = hidden_in.shape[2]
    dp_count = lax.axis_size("dp")
    first_core = lax.axis_index("tensor") == 0
    heads_here = query_bias.shape[0] // HDIM
    query_scale = HDIM ** (-0.5)
    shard_weights = (query_weight, keyval_weight, attn_out_weight, up_weight, down_weight)
    gathered = None
    grad_query_w = jnp.zeros((width, query_weight.shape[1]), jnp.float32)
    grad_keyval_w = jnp.zeros((width, keyval_weight.shape[1]), jnp.float32)
    grad_out_w = jnp.zeros(
        (attn_out_weight.shape[0], attn_out_weight.shape[1] * dp_count), jnp.float32
    )
    grad_up_w = jnp.zeros((width, up_weight.shape[1]), jnp.float32)
    grad_down_w = jnp.zeros((down_weight.shape[0], down_weight.shape[1] * dp_count), jnp.float32)
    grad_n1_gain = jnp.zeros((width,), jnp.float32)
    grad_n1_bias = jnp.zeros((width,), jnp.float32)
    grad_n2_gain = jnp.zeros((width,), jnp.float32)
    grad_n2_bias = jnp.zeros((width,), jnp.float32)
    grad_row_sum = jnp.zeros((width,), jnp.float32)
    grad_query_b = jnp.zeros(query_bias.shape, jnp.float32)
    grad_keyval_b = jnp.zeros(keyval_bias.shape, jnp.float32)
    grad_up_b = jnp.zeros(up_bias.shape, jnp.float32)
    layer_rows = []
    cache_rows = []
    input_rows = []
    for micro_step in range(micro_count):
        gathered = fetch_weights(shard_weights)
        w_query, w_keyval, w_out, w_up, w_down = gathered
        stream = hidden_in[micro_step].astype(jnp.float32)
        places = positions[micro_step]
        normed, scaling = norm_forward(stream)
        low_first = (normed * norm1_gain + norm1_bias).astype(jnp.bfloat16)
        low_second = (normed * norm2_gain + norm2_bias).astype(jnp.bfloat16)
        cos_table, sine_table = rotary_tables(places)
        query_lin = jnp.dot(low_first, w_query, preferred_element_type=jnp.float32) + query_bias
        queries = (
            rotate(query_lin.reshape(tokens_here, heads_here, HDIM), cos_table, sine_table)
            * query_scale
        ).astype(jnp.bfloat16)
        query_heads = jnp.transpose(queries, (1, 0, 2))
        half_lin = jnp.dot(low_first, w_keyval, preferred_element_type=jnp.float32) + keyval_bias
        spun_half = rotate(half_lin[:, None, :], cos_table, sine_table)[:, 0, :]
        half_low = jnp.where(first_core, spun_half, half_lin).astype(jnp.bfloat16)
        keyval = lax.all_gather(half_low, "tensor", axis=1, tiled=True)
        blocks = [keyval] + [
            shifted(keyval, "dp", reach_step) for reach_step in range(1, REACH + 1)
        ]
        mixture, log_sum = attend_forward(query_heads, blocks, places)
        mixture_low = (
            jnp.transpose(mixture, (1, 0, 2))
            .reshape(tokens_here, heads_here * HDIM)
            .astype(jnp.bfloat16)
        )
        up_lin = jnp.dot(low_second, w_up, preferred_element_type=jnp.float32) + up_bias
        active_low = gelu_exact(up_lin).astype(jnp.bfloat16)
        branch_part = jnp.dot(mixture_low, w_out, preferred_element_type=jnp.float32) + jnp.dot(
            active_low, w_down, preferred_element_type=jnp.float32
        )
        branches = lax.psum(branch_part.astype(jnp.bfloat16), "tensor").astype(jnp.float32)
        layer_rows.append((stream + branches + attn_out_bias + down_bias).astype(jnp.bfloat16))
        cache_rows.append(keyval)
        grad_low = out_grad[micro_step]
        grad_rows = grad_low.astype(jnp.float32)
        grad_row_sum = grad_row_sum + jnp.sum(grad_rows, axis=0)
        grad_out_w = grad_out_w + jnp.einsum(
            "th,td->hd", mixture_low, grad_low, preferred_element_type=jnp.float32
        )
        grad_down_w = grad_down_w + jnp.einsum(
            "tf,td->fd", active_low, grad_low, preferred_element_type=jnp.float32
        )
        grad_active = jnp.einsum("td,fd->tf", grad_low, w_down, preferred_element_type=jnp.float32)
        gelu_values, gelu_pull = jax.vjp(gelu_exact, up_lin)
        grad_up_low = gelu_pull(grad_active)[0].astype(jnp.bfloat16)
        grad_up_b = grad_up_b + jnp.sum(grad_up_low.astype(jnp.float32), axis=0)
        grad_up_w = grad_up_w + jnp.einsum(
            "td,tf->df", low_second, grad_up_low, preferred_element_type=jnp.float32
        )
        second_part = jnp.einsum("tf,df->td", grad_up_low, w_up, preferred_element_type=jnp.float32)
        grad_mix_low = jnp.einsum(
            "td,hd->th", grad_low, w_out, preferred_element_type=jnp.float32
        ).astype(jnp.bfloat16)
        grad_mixture = jnp.transpose(grad_mix_low.reshape(tokens_here, heads_here, HDIM), (1, 0, 2))
        row_dots = jnp.sum(grad_mixture.astype(jnp.float32) * mixture, axis=-1)
        grad_queries, key_terms = attend_backward(
            query_heads, blocks, places, log_sum, grad_mixture, row_dots
        )
        keyval_grad = key_terms[0]
        for reach_step in range(1, REACH + 1):
            keyval_grad = keyval_grad + shifted(
                key_terms[reach_step].astype(jnp.bfloat16), "dp", -reach_step
            ).astype(jnp.float32)
        half_grad = lax.psum_scatter(
            keyval_grad.astype(jnp.bfloat16), "tensor", scatter_dimension=1, tiled=True
        ).astype(jnp.float32)
        unspun_half = rotate(half_grad[:, None, :], cos_table, -sine_table)[:, 0, :]
        half_grad_low = jnp.where(first_core, unspun_half, half_grad).astype(jnp.bfloat16)
        grad_keyval_b = grad_keyval_b + jnp.sum(half_grad_low.astype(jnp.float32), axis=0)
        grad_keyval_w = grad_keyval_w + jnp.einsum(
            "td,tk->dk", low_first, half_grad_low, preferred_element_type=jnp.float32
        )
        query_rows = jnp.transpose(grad_queries, (1, 0, 2)) * query_scale
        grad_query_low = (
            rotate(query_rows, cos_table, -sine_table)
            .reshape(tokens_here, heads_here * HDIM)
            .astype(jnp.bfloat16)
        )
        grad_query_b = grad_query_b + jnp.sum(grad_query_low.astype(jnp.float32), axis=0)
        grad_query_w = grad_query_w + jnp.einsum(
            "td,tq->dq", low_first, grad_query_low, preferred_element_type=jnp.float32
        )
        first_part = jnp.einsum(
            "tq,dq->td", grad_query_low, w_query, preferred_element_type=jnp.float32
        ) + jnp.einsum("tk,dk->td", half_grad_low, w_keyval, preferred_element_type=jnp.float32)
        grad_first, grad_second = (
            lax.psum(first_part.astype(jnp.bfloat16), "tensor").astype(jnp.float32),
            lax.psum(second_part.astype(jnp.bfloat16), "tensor").astype(jnp.float32),
        )
        grad_n1_gain = grad_n1_gain + jnp.sum(grad_first * normed, axis=0)
        grad_n1_bias = grad_n1_bias + jnp.sum(grad_first, axis=0)
        grad_n2_gain = grad_n2_gain + jnp.sum(grad_second * normed, axis=0)
        grad_n2_bias = grad_n2_bias + jnp.sum(grad_second, axis=0)
        input_total = (
            grad_rows
            + norm_backward(grad_first, normed, scaling, norm1_gain)
            + norm_backward(grad_second, normed, scaling, norm2_gain)
        )
        input_rows.append(input_total.astype(jnp.bfloat16))
    summed_query, summed_keyval, summed_out, summed_up, summed_down = (
        lax.psum_scatter(grad_query_w, "dp", scatter_dimension=0, tiled=True),
        lax.psum_scatter(grad_keyval_w, "dp", scatter_dimension=0, tiled=True),
        lax.psum_scatter(grad_out_w, "dp", scatter_dimension=1, tiled=True),
        lax.psum_scatter(grad_up_w, "dp", scatter_dimension=0, tiled=True),
        lax.psum_scatter(grad_down_w, "dp", scatter_dimension=1, tiled=True),
    )
    vector_sums = lax.psum(
        (
            grad_n1_gain,
            grad_n1_bias,
            grad_n2_gain,
            grad_n2_bias,
            grad_row_sum,
            grad_query_b,
            grad_keyval_b,
            grad_up_b,
        ),
        "dp",
    )
    (
        sum_n1_gain,
        sum_n1_bias,
        sum_n2_gain,
        sum_n2_bias,
        sum_rows,
        sum_query_b,
        sum_keyval_b,
        sum_up_b,
    ) = vector_sums
    return (
        jnp.stack(layer_rows),
        jnp.stack(cache_rows),
        jnp.stack(input_rows),
        sum_n1_gain,
        sum_n1_bias,
        sum_n2_gain,
        sum_n2_bias,
        summed_query,
        sum_query_b,
        summed_keyval,
        sum_keyval_b,
        summed_out,
        sum_rows,
        summed_up,
        sum_up_b,
        summed_down,
        sum_rows,
    )


def nn(a, b):
    return jnp.dot(a, b, preferred_element_type=F32)


def nt(a, b):
    return lax.dot_general(a, b, (((1,), (1,)), ((), ())), preferred_element_type=F32)


def chunk_list(q_cols, kv_cols, ff_cols, pieces):
    sizes = [q_cols, kv_cols, q_cols] + [ff_cols // pieces] * (2 * pieces)
    at = 0
    out = []
    for size in sizes:
        out.append((at, size))
        at += size
    return out


def attend_tiles(n, half):
    own = REACH * n
    out = [(own + a, half, a, n - a, True) for a in range(0, n, half)]
    out += [(own - j * n, n, 0, n, False) for j in range(1, REACH)]
    out += [(a, half, 0, min(n, a + half), False) for a in range(0, n, half)]
    return out


def spin(rows, cos, sine):
    h = ROT // 2
    a, b, rest = rows[..., :h, :], rows[..., h:ROT, :], rows[..., ROT:, :]
    return jnp.concatenate([a * cos - b * sine, b * cos + a * sine, rest], axis=-2)


def fused_kernel(
    chunks, pieces,
    x, dy, shard, kvw, kvb, g1, b1, g2, b2, bq, bu, bo, cos, sine, start,
    layer_out, keyval_out, input_grad, grads_out, vec_out,
    W, G, kvx, kvbx, n1T, n2, n2T, dyT, wqT, qT, doT, oT, o_nat, lse, dvec, kvwin, kvTwin,
    m_s, l_s, acc, gbuf, dubuf, dqT, dkv, hs, hr, kvs, kvr, yp, yr, d2p, d2r,
    r1, r2, r3, vec, vrx, vb, vry, vz, dql, dkl,
    gzs, gzr, g2s, g2r, g3s, g3r, a1s, a1r, a2s, a2r, azs, azr,
    hfs, hfr, hbs, hbr, xs, xr, vs, vr,
):
    T, D = x.shape
    M, W_rows, KV = kvwin.shape
    n = T // M
    heads = qT.shape[0] // M
    hq = heads * HDIM
    own = REACH * n
    piece = gbuf.shape[2]
    scale = HDIM ** (-0.5)
    me = lax.axis_index("dp")
    core = lax.axis_index("tensor")
    count = lax.axis_size("dp")
    z, y, xx = me // 4, (me // 2) % 2, me % 2
    shard_rows = shard.shape[0]
    n_chunks = len(chunks)

    def at(zz, yy, xo):
        return {"dp": zz * 4 + yy * 2 + xo}

    z_ids = [at((z + d) % 4, y, xx) for d in (1, 2, 3)]
    y_id, x_id = at(z, 1 - y, xx), at(z, y, 1 - xx)
    t_id = {"tensor": 1 - core}

    def send(src, dst, ss, rs, to):
        return pltpu.make_async_remote_copy(
            src_ref=src, dst_ref=dst, send_sem=ss, recv_sem=rs, device_id=to, device_id_type=MESH
        )

    bar = pltpu.get_barrier_semaphore()
    peers = z_ids + [y_id, x_id, t_id]
    peers += [{"dp": (me + s) % count} for s in range(1, REACH + 1)]
    peers += [{"dp": (me + count - s) % count} for s in range(1, REACH + 1)]
    for p in peers:
        pl.semaphore_signal(bar, inc=1, device_id=p, device_id_type=MESH)
    pl.semaphore_wait(bar, len(peers))

    def cols(k):
        return pl.ds(chunks[k][0], chunks[k][1])

    def gather1(k):
        return [
            send(W.at[z, y, xx, :, cols(k)], W.at[z, y, xx, :, cols(k)], gzs.at[k, j], gzr.at[k, j], z_ids[j])
            for j in range(3)
        ]

    def gather2(k):
        r = W.at[:, y, xx, :, cols(k)]
        return send(r, r, g2s.at[k], g2r.at[k], x_id if k % 2 == 0 else y_id)

    def gather3(k):
        r = W.at[:, y, :, :, cols(k)] if k % 2 == 0 else W.at[:, :, xx, :, cols(k)]
        return send(r, r, g3s.at[k], g3r.at[k], y_id if k % 2 == 0 else x_id)

    def start1(k):
        for c in gather1(k):
            c.start()

    def step2(k):
        for c in gather1(k):
            c.wait_recv()
        gather2(k).start()

    def step3(k):
        gather2(k).wait_recv()
        gather3(k).start()

    def arrived(k):
        gather3(k).wait_recv()

    def weight(k):
        c0, cn = chunks[k]
        return W[:, :, :, :, c0 : c0 + cn].reshape(D, cn)

    def red1(k):
        if k % 2 == 0:
            return send(G.at[:, :, 1 - xx, :, cols(k)], r1.at[:, :, :, cols(k)], a1s.at[k], a1r.at[k], x_id)
        return send(G.at[:, 1 - y, :, :, cols(k)], r1.at[:, :, :, cols(k)], a1s.at[k], a1r.at[k], y_id)

    def red2(k):
        o = y if k % 2 == 0 else xx
        return send(r1.at[:, 1 - o, :, cols(k)], r2.at[:, :, cols(k)], a2s.at[k], a2r.at[k], y_id if k % 2 == 0 else x_id)

    def red3(k):
        return [
            send(r2.at[(z + j + 1) % 4, :, cols(k)], r3.at[j, :, cols(k)], azs.at[k, j], azr.at[k, j], z_ids[j])
            for j in range(3)
        ]

    def step_a(k):
        red1(k).start()

    def step_b(k):
        red1(k).wait_recv()

        def add(i, _):
            zz, yy = i // 2, i % 2
            mine = G[zz, yy, xx, :, cols(k)] if k % 2 == 0 else G[zz, y, yy, :, cols(k)]
            r1[zz, yy, :, cols(k)] = r1[zz, yy, :, cols(k)] + mine
            return 0

        lax.fori_loop(0, 8, add, 0)
        red2(k).start()

    def step_c(k):
        red2(k).wait_recv()
        o = y if k % 2 == 0 else xx

        def add(i, _):
            r2[i, :, cols(k)] = r2[i, :, cols(k)] + r1[i, o, :, cols(k)]
            return 0

        lax.fori_loop(0, 4, add, 0)
        for c in red3(k):
            c.start()

    def step_e(k):
        for c in red3(k):
            c.wait_recv()
        total = r2[z, :, cols(k)].astype(F32)
        for j in range(3):
            total = total + r3[j, :, cols(k)].astype(F32)
        grads_out[:, cols(k)] = total

    kv_copy = send(kvw, kvx, xs.at[0], xr.at[0], t_id)
    kvb_copy = send(kvb, kvbx, xs.at[1], xr.at[1], t_id)
    kv_copy.start()
    kvb_copy.start()
    W[z, y, xx] = shard[...]
    start1(0)
    kv_copy.wait_recv()
    kv0 = chunks[1][0]
    W[z, y, xx, :, kv0 : kv0 + KV] = kvw[...] + kvx[...]
    start1(1)
    start1(2)

    R = 256
    vec[...] = jnp.zeros_like(vec)

    def xhat_of(rows):
        v = x[rows, :].astype(F32)
        c = v - jnp.mean(v, axis=-1, keepdims=True)
        rstd = lax.rsqrt(jnp.mean(c * c, axis=-1, keepdims=True) + epsilon)
        return v, c * rstd, rstd

    def norm_tile(i, _):
        rows = pl.ds(pl.multiple_of(i * R, R), R)
        _, xh, _ = xhat_of(rows)
        n1v = (xh * g1[...] + b1[...]).astype(BF16)
        n2v = (xh * g2[...] + b2[...]).astype(BF16)
        n2[rows, :] = n2v
        n1T[:, rows] = n1v.T
        n2T[:, rows] = n2v.T
        d = dy[rows, :]
        dyT[:, rows] = d.T
        vec[4:5, :] += jnp.sum(d.astype(F32), axis=0, keepdims=True)
        return 0

    lax.fori_loop(0, T // R // 2, norm_tile, 0)
    step2(0)
    step2(1)
    start1(3)
    lax.fori_loop(T // R // 2, T // R, norm_tile, 0)
    step3(0)
    step3(1)
    step2(2)
    start1(4)
    kvb_copy.wait_recv()
    bkv = jnp.transpose(kvb[...] + kvbx[...])[:, 0:1]
    arrived(0)
    wqT[...] = weight(0).T
    arrived(1)
    wkvT = weight(1).T
    for m in range(M):
        ms = slice(m * n, (m + 1) * n)
        lin = nn(wkvT, n1T[:, ms]) + bkv
        low = spin(lin, cos[:, ms], sine[:, ms]).astype(BF16)
        kvTwin[m, :, own : own + n] = low
        natural = low.T
        kvwin[m, own : own + n, :] = natural
        keyval_out[m] = natural

    def halo(s):
        return send(
            kvwin.at[:, pl.ds(own, n), :], kvwin.at[:, pl.ds((REACH - s) * n, n), :],
            hfs.at[s - 1], hfr.at[s - 1], {"dp": (me + s) % count},
        )

    for s in range(1, REACH + 1):
        @pl.when(me + s < count)
        def _(s=s):
            halo(s).start()

    step3(2)
    step2(3)
    start1(5)
    for m in range(M):
        ms = slice(m * n, (m + 1) * n)
        lin = nn(wqT[...], n1T[:, ms]) + bq[...]
        turned = spin(lin.reshape(heads, HDIM, n), cos[:, ms], sine[:, ms]) * scale
        qT[m * heads : (m + 1) * heads] = turned.astype(BF16)
    arrived(2)
    step3(3)
    step2(4)
    start1(6)
    wo = weight(2).T
    for m in range(M):
        ms = slice(m * n, (m + 1) * n)
        doT[m * heads : (m + 1) * heads] = nn(wo, dyT[:, ms]).astype(BF16).reshape(heads, HDIM, n)

    for s in range(1, REACH + 1):
        blk = slice((REACH - s) * n, (REACH - s + 1) * n)

        @pl.when(me >= s)
        def _(s=s):
            halo(s).wait_recv()

        @pl.when(me < s)
        def _(blk=blk):
            kvwin[:, blk, :] = jnp.zeros((M, n, KV), BF16)

        for m in range(M):
            kvTwin[m, :, blk] = kvwin[m, blk, :].T

    tiles = attend_tiles(n, n // 2)

    def visible(w0, kn, q0, qn, first, causal):
        key = lax.broadcasted_iota(jnp.int32, (kn, 1), 0) + w0
        seen = key >= first
        if causal:
            query = lax.broadcasted_iota(jnp.int32, (1, qn), 1) + (q0 + own)
            seen = seen & (key <= query)
        return seen

    def forward(i, _):
        m = i // heads
        q = jnp.concatenate([qT[i], jnp.zeros((KV - HDIM, n), BF16)], axis=0)
        first = start[m]
        m_s[...] = jnp.full_like(m_s, LOW)
        l_s[...] = jnp.zeros_like(l_s)
        acc[...] = jnp.zeros_like(acc)
        for w0, kn, q0, qn, causal in tiles:
            qs = slice(q0, q0 + qn)
            sc = nn(kvwin[m, w0 : w0 + kn, :], q[:, qs])
            sc = jnp.where(visible(w0, kn, q0, qn, first[:, qs], causal), sc, LOW)
            before = m_s[:, qs]
            top = jnp.maximum(before, jnp.max(sc, axis=0, keepdims=True))
            p = jnp.exp(sc - top)
            shrink = jnp.exp(before - top)
            l_s[:, qs] = l_s[:, qs] * shrink + jnp.sum(p, axis=0, keepdims=True)
            m_s[:, qs] = top
            acc[:, qs] = acc[:, qs] * shrink + nn(kvTwin[m, HDIM:KV, w0 : w0 + kn], p.astype(BF16))
        o = acc[...] / l_s[...]
        oT[i] = o.astype(BF16)
        lse[i] = m_s[...] + jnp.log(l_s[...])
        dvec[i] = jnp.sum(doT[i].astype(F32) * o, axis=0, keepdims=True)
        gather_steps(i)
        return 0

    plan = [
        (lambda: (step3(4), step2(5), start1(7))),
        (lambda: None),
        (lambda: (step3(5), step2(6), start1(8))),
        (lambda: None),
        (lambda: (step3(6), step2(7))),
        (lambda: None),
        (lambda: (step3(7), step2(8))),
        (lambda: None),
        (lambda: step3(8)),
    ]

    def gather_steps(i):
        for j, act in enumerate(plan):
            if j % 2 == 0:
                pl.when(i == j + 1)(lambda act=act: (act(), None)[1])

    lax.fori_loop(0, M * heads, forward, 0)

    for m in range(M):
        o_nat[m * n : (m + 1) * n, :] = oT[m * heads : (m + 1) * heads].reshape(hq, n).T

    def put_grad(k, leftT, right):
        c0, cn = chunks[k]

        def half(i, _):
            rows = pl.ds(pl.multiple_of(i * (D // 2), 128), D // 2)
            part = nn(leftT[rows, :], right[...]).astype(BF16)
            G[pl.ds(i * 2, 2), :, :, :, c0 : c0 + cn] = part.reshape(2, 2, 2, shard_rows, cn)
            return 0

        lax.fori_loop(0, 2, half, 0)
        step_a(k)

    put_grad(2, dyT, o_nat)

    for c in range(pieces):
        ku, kd = 3 + 2 * c, 4 + 2 * c
        arrived(ku)
        arrived(kd)
        (u0, _), (d0, _) = chunks[ku], chunks[kd]

        def rows_tile(i, _, c=c, u0=u0, d0=d0):
            rows = pl.ds(pl.multiple_of(i * R, R), R)
            u = nn(n2[rows, :], W[:, :, :, :, u0 : u0 + piece].reshape(D, piece)) + bu[c]
            phi = 0.5 * (1.0 + lax.erf(u * 0.7071067811865476))
            slope = phi + u * (jnp.exp(-0.5 * u * u) * 0.3989422804014327)
            gbuf[c, rows, :] = (u * phi).astype(BF16)
            dg = nn(dy[rows, :], W[:, :, :, :, d0 : d0 + piece].reshape(D, piece))
            du = (slope * dg).astype(BF16)
            dubuf[c, rows, :] = du
            return 0

        lax.fori_loop(0, T // R, rows_tile, 0)
        put_grad(ku, n2T, dubuf.at[c])
        put_grad(kd, dyT, gbuf.at[c])

    def branch_tile(i, _):
        rows = pl.ds(pl.multiple_of(i * R, R), R)
        total = nt(o_nat[rows, :], weight(2))
        back = jnp.zeros((R, D), F32)
        for c in range(pieces):
            total = total + nt(gbuf[c, rows, :], weight(4 + 2 * c))
            back = back + nt(dubuf[c, rows, :], weight(3 + 2 * c))
        yp[rows, :] = total.astype(BF16)
        d2p[rows, :] = back.astype(BF16)
        return 0

    step_b(2)
    lax.fori_loop(0, T // R, branch_tile, 0)
    y_copy = send(yp, yr, xs.at[2], xr.at[2], t_id)
    d2_copy = send(d2p, d2r, xs.at[3], xr.at[3], t_id)
    y_copy.start()
    d2_copy.start()
    for c in range(pieces):
        part = jnp.sum(dubuf[c].astype(F32), axis=0, keepdims=True)
        done = 0
        while done < piece:
            flat = c * piece + done
            row, col = flat // D, flat % D
            width = min(piece - done, D - col)
            vec[6 + row : 7 + row, col : col + width] = part[:, done : done + width]
            done += width

    dkv[...] = jnp.zeros_like(dkv)

    def backward(i, _):
        m = i // heads
        zero = jnp.zeros((HDIM, n), BF16)
        q = jnp.concatenate([qT[i], zero], axis=0)
        do = jnp.concatenate([zero, doT[i]], axis=0)
        qdo = jnp.concatenate([qT[i], doT[i]], axis=0).T
        first, ls, dots = start[m], lse[i], dvec[i]
        dqT[i] = jnp.zeros((HDIM, n), F32)
        for w0, kn, q0, qn, causal in tiles:
            qs = slice(q0, q0 + qn)
            rows = kvwin[m, w0 : w0 + kn, :]
            sc = nn(rows, q[:, qs])
            sc = jnp.where(visible(w0, kn, q0, qn, first[:, qs], causal), sc, LOW)
            p = jnp.exp(sc - ls[:, qs])
            dp = nn(rows, do[:, qs])
            ds = (p * (dp - dots[:, qs])).astype(BF16)
            for_k = nn(ds, qdo[qs])
            for_v = nn(p.astype(BF16), qdo[qs])
            lane = lax.broadcasted_iota(jnp.int32, for_k.shape, 1)
            dkv[m, w0 : w0 + kn, :] += jnp.where(lane < HDIM, for_k, for_v)
            dqT[i, :, qs] += nn(kvTwin[m, 0:HDIM, w0 : w0 + kn], ds)
        reduce_steps(i)
        return 0

    def back_copy(s, m):
        return send(
            hs.at[s - 1, m], hr.at[s - 1, m], hbs.at[s - 1, m], hbr.at[s - 1, m],
            {"dp": (me + count - s) % count},
        )

    def return_halo(m):
        for s in range(1, REACH + 1):
            hs[s - 1, m] = dkv[m, (REACH - s) * n : (REACH - s + 1) * n, :].astype(BF16)

            @pl.when(me >= s)
            def _(s=s):
                back_copy(s, m).start()

    red_plan = {
        0: lambda: step_b(3),
        1: lambda: (step_c(2), step_b(4)),
        3: lambda: (step_c(3), step_c(4), step_b(5)),
        5: lambda: (step_e(2), step_e(3), step_b(6), step_c(5), return_halo(0)),
        7: lambda: (step_e(4), step_b(7), step_c(6)),
        9: lambda: (step_e(5), step_b(8), step_c(7)),
        11: lambda: (step_e(6), step_c(8)),
    }

    def reduce_steps(i):
        for j, act in red_plan.items():
            pl.when(i == j)(lambda act=act: (act(), None)[1])

    lax.fori_loop(0, M * heads, backward, 0)
    for m in range(1, M):
        return_halo(m)

    for m in range(M):
        ms = slice(m * n, (m + 1) * n)
        rows = dqT[m * heads : (m + 1) * heads] * scale
        low = spin(rows, cos[:, ms], -sine[:, ms]).astype(BF16)
        dql[ms, :] = low.reshape(hq, n).T
    put_grad(0, n1T, dql)
    vec[5:6, 0:hq] = jnp.sum(dql[...].astype(F32), axis=0, keepdims=True)

    y_copy.wait_recv()

    def out_tile(i, _):
        rows = pl.ds(pl.multiple_of(i * R, R), R)
        both = (yp[rows, :].astype(F32) + yr[rows, :].astype(F32)) + bo[...]
        layer_out[rows, :] = (x[rows, :].astype(F32) + both).astype(BF16)
        return 0

    lax.fori_loop(0, T // R, out_tile, 0)

    y_copy.wait_send()
    d1p, d1r = yp, n2

    for m in range(M):
        for s in range(1, REACH + 1):
            @pl.when(me + s < count)
            def _(s=s, m=m):
                back_copy(s, m).wait_recv()
                dkv[m, own : own + n, :] += hr[s - 1, m].astype(F32)
        kvs[m] = dkv[m, own : own + n, :].astype(BF16)
    kv_grad = send(kvs, kvr, xs.at[4], xr.at[4], t_id)
    kv_grad.start()
    step_b(0)
    kv_grad.wait_recv()
    half_row = lax.broadcasted_iota(jnp.int32, (KV, 1), 0) // HDIM
    for m in range(M):
        ms = slice(m * n, (m + 1) * n)
        both = (dkv[m, own : own + n, :] + kvr[m].astype(F32)).T
        low = spin(both, cos[:, ms], -sine[:, ms])
        low = jnp.where(half_row == core, low, 0.0).astype(BF16)
        dkl[ms, :] = low.T
    put_grad(1, n1T, dkl)
    vec[5:6, hq : hq + KV] = jnp.sum(dkl[...].astype(F32), axis=0, keepdims=True)
    step_c(0)

    def first_tile(i, _):
        rows = pl.ds(pl.multiple_of(i * R, R), R)
        d1p[rows, :] = (nt(dql[rows, :], weight(0)) + nt(dkl[rows, :], weight(1))).astype(BF16)
        return 0

    lax.fori_loop(0, T // R, first_tile, 0)
    d1_copy = send(d1p, d1r, xs.at[5], xr.at[5], t_id)
    d1_copy.start()
    step_b(1)
    step_e(7)
    step_e(8)
    d2_copy.wait_recv()
    d1_copy.wait_recv()
    step_c(1)
    step_e(0)

    def last_tile(i, _):
        rows = pl.ds(pl.multiple_of(i * R, R), R)
        _, xh, rstd = xhat_of(rows)
        dn1 = d1p[rows, :].astype(F32) + d1r[rows, :].astype(F32)
        dn2 = d2p[rows, :].astype(F32) + d2r[rows, :].astype(F32)
        vec[0:1, :] += jnp.sum(dn1 * xh, axis=0, keepdims=True)
        vec[1:2, :] += jnp.sum(dn1, axis=0, keepdims=True)
        vec[2:3, :] += jnp.sum(dn2 * xh, axis=0, keepdims=True)
        vec[3:4, :] += jnp.sum(dn2, axis=0, keepdims=True)
        a = dn1 * g1[...] + dn2 * g2[...]
        back = a - jnp.mean(a, axis=-1, keepdims=True) - xh * jnp.mean(a * xh, axis=-1, keepdims=True)
        input_grad[rows, :] = (dy[rows, :].astype(F32) + rstd * back).astype(BF16)
        return 0

    lax.fori_loop(0, T // R, last_tile, 0)

    v1 = send(vec, vrx, vs.at[0], vr.at[0], x_id)
    v1.start()
    v1.wait_recv()
    vb[...] = vec[...] + vrx[...]
    v2 = send(vb, vry, vs.at[1], vr.at[1], y_id)
    v2.start()
    step_e(1)
    v2.wait_recv()
    vz[z] = vb[...] + vry[...]
    v3 = [send(vz.at[z], vz.at[z], vs.at[2 + j], vr.at[2 + j], z_ids[j]) for j in range(3)]
    for c in v3:
        c.start()
    for c in v3:
        c.wait_recv()
    vec_out[...] = (vz[0] + vz[1]) + (vz[2] + vz[3])

    for k in range(n_chunks):
        for c in gather1(k):
            c.wait_send()
        gather2(k).wait_send()
        gather3(k).wait_send()
        red1(k).wait_send()
        red2(k).wait_send()
        for c in red3(k):
            c.wait_send()
    for s in range(1, REACH + 1):
        @pl.when(me + s < count)
        def _(s=s):
            halo(s).wait_send()

        @pl.when(me >= s)
        def _(s=s):
            for m in range(M):
                back_copy(s, m).wait_send()
    for c in [kv_copy, kvb_copy, d2_copy, kv_grad, d1_copy, v1, v2] + v3:
        c.wait_send()


def fused_layer(x, dy, shard, kvw, kvb, g1, b1, g2, b2, bq, bu, bo, cos, sine, start, pieces):
    T, D = x.shape
    M, n = start.shape[0], start.shape[2]
    hq = bq.shape[0]
    heads = hq // HDIM
    KV = kvw.shape[1]
    F = bu.shape[0] * bu.shape[2]
    piece = F // pieces
    rows, C = shard.shape
    chunks = chunk_list(hq, KV, F, pieces)
    k = len(chunks)
    Wn = (REACH + 1) * n
    V = pltpu.VMEM
    S = pltpu.SemaphoreType.DMA
    sds = jax.ShapeDtypeStruct
    vm = pl.BlockSpec(memory_space=pltpu.VMEM)
    mh = M * heads
    scratch = [
        V((4, 2, 2, rows, C), BF16), V((4, 2, 2, rows, C), BF16),
        V((rows, KV), BF16), V((8, KV), F32),
        V((D, T), BF16), V((T, D), BF16), V((D, T), BF16), V((D, T), BF16),
        V((hq, D), BF16), V((mh, HDIM, n), BF16), V((mh, HDIM, n), BF16), V((mh, HDIM, n), BF16),
        V((T, hq), BF16), V((mh, 1, n), F32), V((mh, 1, n), F32),
        V((M, Wn, KV), BF16), V((M, KV, Wn), BF16),
        V((1, n), F32), V((1, n), F32), V((HDIM, n), F32),
        V((pieces, T, piece), BF16), V((pieces, T, piece), BF16),
        V((mh, HDIM, n), F32), V((M, Wn, KV), F32),
        V((REACH, M, n, KV), BF16), V((REACH, M, n, KV), BF16),
        V((M, n, KV), BF16), V((M, n, KV), BF16),
        V((T, D), BF16), V((T, D), BF16), V((T, D), BF16), V((T, D), BF16),
        V((4, 2, rows, C), BF16), V((4, rows, C), BF16), V((3, rows, C), BF16),
        V((8, D), F32), V((8, D), F32), V((8, D), F32), V((8, D), F32), V((4, 8, D), F32),
        V((T, hq), BF16), V((T, KV), BF16),
        S((k, 3)), S((k, 3)), S((k,)), S((k,)), S((k,)), S((k,)),
        S((k,)), S((k,)), S((k,)), S((k,)), S((k, 3)), S((k, 3)),
        S((REACH,)), S((REACH,)), S((REACH, M)), S((REACH, M)), S((6,)), S((6,)), S((5,)), S((5,)),
    ]
    return pl.pallas_call(
        functools.partial(fused_kernel, chunks, pieces),
        out_shape=(
            sds((T, D), BF16), sds((M, n, KV), BF16), sds((T, D), BF16), sds((rows, C), F32), sds((8, D), F32),
        ),
        in_specs=[vm] * 15,
        out_specs=(vm,) * 5,
        scratch_shapes=scratch,
        compiler_params=pltpu.CompilerParams(
            collective_id=0, has_side_effects=True, vmem_limit_bytes=62 << 20
        ),
        name="fused_layer",
    )(x, dy, shard, kvw, kvb, g1, b1, g2, b2, bq, bu, bo, cos, sine, start)


PIECES = 3


def fits_fused(hidden_in, query_weight):
    rows = query_weight.shape[0]
    return lax.axis_size("dp") == 16 and rows % 16 == 0 and hidden_in.shape[1] % 256 == 0


def pack_columns(query_part, keyval_part, out_part, up_part, down_part, pieces):
    columns = [query_part, keyval_part, out_part]
    piece = up_part.shape[1] // pieces
    for c in range(pieces):
        columns.append(up_part[:, c * piece : (c + 1) * piece])
        columns.append(down_part[:, c * piece : (c + 1) * piece])
    return jnp.concatenate(columns, axis=1)


def fused_device(
    hidden_in,
    positions,
    out_grad,
    norm1_gain,
    norm1_bias,
    norm2_gain,
    norm2_bias,
    query_weight,
    query_bias,
    keyval_weight,
    keyval_bias,
    attn_out_weight,
    attn_out_bias,
    up_weight,
    up_bias,
    down_weight,
    down_bias,
):
    micro, tokens, width = hidden_in.shape
    core = lax.axis_index("tensor")
    hq = query_bias.shape[0]
    ff = up_bias.shape[0]
    piece = ff // PIECES
    half = keyval_bias.shape[0]

    def own_half(block):
        zero = jnp.zeros_like(block)
        return jnp.where(
            core == 0,
            jnp.concatenate([block, zero], axis=1),
            jnp.concatenate([zero, block], axis=1),
        )

    keyval_own = own_half(keyval_weight)
    bias_own = jnp.broadcast_to(own_half(keyval_bias[None, :]), (8, 2 * half))
    shard = pack_columns(
        query_weight, keyval_own, attn_out_weight.T, up_weight, down_weight.T, PIECES
    )
    flat = positions.reshape(1, micro * tokens).astype(jnp.float32)
    inverse = 10000.0 ** (-(jnp.arange(ROT // 2, dtype=jnp.float32) * 2.0) / ROT)
    angles = inverse[:, None] * flat
    row_ids = jnp.arange(tokens, dtype=jnp.int32)[None, :]
    first = (REACH * tokens + row_ids - positions)[:, None, :]
    layer_out, keyval_out, input_grad, grads, vec = fused_layer(
        hidden_in.reshape(micro * tokens, width),
        out_grad.reshape(micro * tokens, width),
        shard,
        keyval_own,
        bias_own,
        norm1_gain[None, :],
        norm1_bias[None, :],
        norm2_gain[None, :],
        norm2_bias[None, :],
        query_bias[:, None],
        up_bias.reshape(PIECES, 1, piece),
        (attn_out_bias + down_bias)[None, :],
        jnp.cos(angles),
        jnp.sin(angles),
        first,
        PIECES,
    )
    chunks = chunk_list(hq, 2 * half, ff, PIECES)

    def columns(k):
        return grads[:, chunks[k][0] : chunks[k][0] + chunks[k][1]]

    def own_columns(block):
        return jnp.where(core == 0, block[..., :half], block[..., half:])

    grad_up = jnp.concatenate([columns(3 + 2 * c) for c in range(PIECES)], axis=1)
    grad_down = jnp.concatenate([columns(4 + 2 * c) for c in range(PIECES)], axis=1).T
    return (
        layer_out.reshape(hidden_in.shape),
        keyval_out,
        input_grad.reshape(hidden_in.shape),
        vec[0],
        vec[1],
        vec[2],
        vec[3],
        columns(0),
        vec[5, :hq],
        own_columns(columns(1)),
        own_columns(vec[5, hq : hq + 2 * half]),
        columns(2).T,
        vec[4],
        grad_up,
        vec[6:8].reshape(-1)[:ff],
        grad_down,
        vec[4],
    )


def on_device(*arguments):
    if fits_fused(arguments[0], arguments[7]):
        return fused_device(*arguments)
    return plain_layer(*arguments)


def solution(mesh):
    return jax.shard_map(
        on_device,
        mesh=mesh,
        in_specs=(
            P(None, "dp", None),
            P(None, "dp"),
            P(None, "dp", None),
            P(),
            P(),
            P(),
            P(),
            P("dp", "tensor"),
            P("tensor"),
            P("dp", "tensor"),
            P("tensor"),
            P("tensor", "dp"),
            P(),
            P("dp", "tensor"),
            P("tensor"),
            P("tensor", "dp"),
            P(),
        ),
        out_specs=(
            P(None, "dp", None),
            P(None, "dp", None),
            P(None, "dp", None),
            P(),
            P(),
            P(),
            P(),
            P("dp", "tensor"),
            P("tensor"),
            P("dp", "tensor"),
            P("tensor"),
            P("tensor", "dp"),
            P(),
            P("dp", "tensor"),
            P("tensor"),
            P("tensor", "dp"),
            P(),
        ),
        check_vma=False,
    )
```

```python
import functools
import jax
import jax.numpy as jnp
from jax import lax
from jax.experimental import pallas as pl
from jax.experimental.pallas import tpu as pltpu
from jax.sharding import PartitionSpec as P

HDIM = 64
ROT = 16
REACH = 4
epsilon = 1e-05
MESH = pl.DeviceIdType.MESH
LOW = -1e30
F32 = jnp.float32
BF16 = jnp.bfloat16


def shifted(value, axis, steps):
    count = lax.axis_size(axis)
    initial, last = (max(0, -steps), min(count, count - steps))
    return lax.ppermute(value, axis, [(source, source + steps) for source in range(initial, last)])


def norm_forward(stream):
    average = jnp.mean(stream, axis=-1, keepdims=True)
    centered = stream - average
    spread = jnp.mean(centered * centered, axis=-1, keepdims=True)
    scaling = lax.rsqrt(spread + epsilon)
    normed = centered * scaling
    return (normed, scaling)


def norm_backward(upstream, normed, scaling, norm_gain):
    weighted = upstream * norm_gain
    return scaling * (
        weighted
        - jnp.mean(weighted, axis=-1, keepdims=True)
        - normed * jnp.mean(weighted * normed, axis=-1, keepdims=True)
    )


def rotary_tables(places):
    inverse = 10000.0 ** (-(jnp.arange(ROT // 2, dtype=jnp.float32) * 2.0) / ROT)
    angles = places.astype(jnp.float32)[:, None] * inverse[None, :]
    angles = jnp.concatenate([angles, angles], axis=-1)
    return (jnp.cos(angles), jnp.sin(angles))


def rotate(values, cos_table, sine_table):
    head_part = values[..., :ROT]
    first_half = head_part[..., : ROT // 2]
    second_half = head_part[..., ROT // 2 :]
    turned = jnp.concatenate([-second_half, first_half], axis=-1)
    spun_part = head_part * cos_table[:, None, :] + turned * sine_table[:, None, :]
    return jnp.concatenate([spun_part, values[..., ROT:]], axis=-1)


def gelu_exact(values):
    return jax.nn.gelu(values, approximate=False)


def fetch_weights(shard_weights):
    return (
        lax.all_gather(shard_weights[0], "dp", axis=0, tiled=True),
        lax.all_gather(shard_weights[1], "dp", axis=0, tiled=True),
        lax.all_gather(shard_weights[2], "dp", axis=1, tiled=True),
        lax.all_gather(shard_weights[3], "dp", axis=0, tiled=True),
        lax.all_gather(shard_weights[4], "dp", axis=1, tiled=True),
    )


def score_block(queries, key_rows, places, reach_step):
    tokens_here = queries.shape[1]
    scores = jnp.einsum("htd,kd->htk", queries, key_rows, preferred_element_type=jnp.float32)
    row_ids = jnp.arange(tokens_here, dtype=jnp.int32)
    offsets = reach_step * tokens_here + row_ids[:, None] - row_ids[None, :]
    visible = (offsets >= 0) & (offsets <= places[:, None])
    return (scores, visible[None])


def attend_forward(queries, blocks, places):
    heads_here, tokens_here = (queries.shape[0], queries.shape[1])
    top_score = jnp.full((heads_here, tokens_here), -1e30, jnp.float32)
    totals = jnp.zeros((heads_here, tokens_here), jnp.float32)
    for reach_step, kv_block in enumerate(blocks):
        scores, visible = score_block(queries, kv_block[:, :HDIM], places, reach_step)
        masked = jnp.where(visible, scores, -1e30)
        new_top = jnp.maximum(top_score, jnp.max(masked, axis=-1))
        totals = totals * jnp.exp(top_score - new_top) + jnp.sum(
            jnp.where(visible, jnp.exp(masked - new_top[..., None]), 0.0), axis=-1
        )
        top_score = new_top
    log_sum = top_score + jnp.log(totals)
    mixture = jnp.zeros((heads_here, tokens_here, HDIM), jnp.float32)
    for reach_step, kv_block in enumerate(blocks):
        scores, visible = score_block(queries, kv_block[:, :HDIM], places, reach_step)
        weights_low = jnp.where(visible, jnp.exp(scores - log_sum[..., None]), 0.0).astype(
            jnp.bfloat16
        )
        mixture = mixture + jnp.einsum(
            "htk,kd->htd", weights_low, kv_block[:, HDIM:], preferred_element_type=jnp.float32
        )
    return (mixture, log_sum)


def attend_backward(queries, blocks, places, log_sum, grad_mixture, row_dots):
    grad_queries = jnp.zeros(queries.shape, jnp.float32)
    key_terms = []
    for reach_step, kv_block in enumerate(blocks):
        key_rows = kv_block[:, :HDIM]
        value_rows = kv_block[:, HDIM:]
        scores, visible = score_block(queries, key_rows, places, reach_step)
        weights_full = jnp.where(visible, jnp.exp(scores - log_sum[..., None]), 0.0)
        weights_low = weights_full.astype(jnp.bfloat16)
        grad_weights = jnp.einsum(
            "htd,kd->htk", grad_mixture, value_rows, preferred_element_type=jnp.float32
        )
        grad_scores = (weights_full * (grad_weights - row_dots[..., None])).astype(jnp.bfloat16)
        grad_queries = grad_queries + jnp.einsum(
            "htk,kd->htd", grad_scores, key_rows, preferred_element_type=jnp.float32
        )
        grad_keys = jnp.einsum(
            "htk,htd->kd", grad_scores, queries, preferred_element_type=jnp.float32
        )
        grad_values = jnp.einsum(
            "htk,htd->kd", weights_low, grad_mixture, preferred_element_type=jnp.float32
        )
        key_terms.append(jnp.concatenate([grad_keys, grad_values], axis=-1))
    return (grad_queries, key_terms)


def plain_layer(
    hidden_in,
    positions,
    out_grad,
    norm1_gain,
    norm1_bias,
    norm2_gain,
    norm2_bias,
    query_weight,
    query_bias,
    keyval_weight,
    keyval_bias,
    attn_out_weight,
    attn_out_bias,
    up_weight,
    up_bias,
    down_weight,
    down_bias,
):
    micro_count = hidden_in.shape[0]
    tokens_here = hidden_in.shape[1]
    width = hidden_in.shape[2]
    dp_count = lax.axis_size("dp")
    first_core = lax.axis_index("tensor") == 0
    heads_here = query_bias.shape[0] // HDIM
    query_scale = HDIM ** (-0.5)
    shard_weights = (query_weight, keyval_weight, attn_out_weight, up_weight, down_weight)
    gathered = None
    grad_query_w = jnp.zeros((width, query_weight.shape[1]), jnp.float32)
    grad_keyval_w = jnp.zeros((width, keyval_weight.shape[1]), jnp.float32)
    grad_out_w = jnp.zeros(
        (attn_out_weight.shape[0], attn_out_weight.shape[1] * dp_count), jnp.float32
    )
    grad_up_w = jnp.zeros((width, up_weight.shape[1]), jnp.float32)
    grad_down_w = jnp.zeros((down_weight.shape[0], down_weight.shape[1] * dp_count), jnp.float32)
    grad_n1_gain = jnp.zeros((width,), jnp.float32)
    grad_n1_bias = jnp.zeros((width,), jnp.float32)
    grad_n2_gain = jnp.zeros((width,), jnp.float32)
    grad_n2_bias = jnp.zeros((width,), jnp.float32)
    grad_row_sum = jnp.zeros((width,), jnp.float32)
    grad_query_b = jnp.zeros(query_bias.shape, jnp.float32)
    grad_keyval_b = jnp.zeros(keyval_bias.shape, jnp.float32)
    grad_up_b = jnp.zeros(up_bias.shape, jnp.float32)
    layer_rows = []
    cache_rows = []
    input_rows = []
    for micro_step in range(micro_count):
        gathered = fetch_weights(shard_weights)
        w_query, w_keyval, w_out, w_up, w_down = gathered
        stream = hidden_in[micro_step].astype(jnp.float32)
        places = positions[micro_step]
        normed, scaling = norm_forward(stream)
        low_first = (normed * norm1_gain + norm1_bias).astype(jnp.bfloat16)
        low_second = (normed * norm2_gain + norm2_bias).astype(jnp.bfloat16)
        cos_table, sine_table = rotary_tables(places)
        query_lin = jnp.dot(low_first, w_query, preferred_element_type=jnp.float32) + query_bias
        queries = (
            rotate(query_lin.reshape(tokens_here, heads_here, HDIM), cos_table, sine_table)
            * query_scale
        ).astype(jnp.bfloat16)
        query_heads = jnp.transpose(queries, (1, 0, 2))
        half_lin = jnp.dot(low_first, w_keyval, preferred_element_type=jnp.float32) + keyval_bias
        spun_half = rotate(half_lin[:, None, :], cos_table, sine_table)[:, 0, :]
        half_low = jnp.where(first_core, spun_half, half_lin).astype(jnp.bfloat16)
        keyval = lax.all_gather(half_low, "tensor", axis=1, tiled=True)
        blocks = [keyval] + [
            shifted(keyval, "dp", reach_step) for reach_step in range(1, REACH + 1)
        ]
        mixture, log_sum = attend_forward(query_heads, blocks, places)
        mixture_low = (
            jnp.transpose(mixture, (1, 0, 2))
            .reshape(tokens_here, heads_here * HDIM)
            .astype(jnp.bfloat16)
        )
        up_lin = jnp.dot(low_second, w_up, preferred_element_type=jnp.float32) + up_bias
        active_low = gelu_exact(up_lin).astype(jnp.bfloat16)
        branch_part = jnp.dot(mixture_low, w_out, preferred_element_type=jnp.float32) + jnp.dot(
            active_low, w_down, preferred_element_type=jnp.float32
        )
        branches = lax.psum(branch_part.astype(jnp.bfloat16), "tensor").astype(jnp.float32)
        layer_rows.append((stream + branches + attn_out_bias + down_bias).astype(jnp.bfloat16))
        cache_rows.append(keyval)
        grad_low = out_grad[micro_step]
        grad_rows = grad_low.astype(jnp.float32)
        grad_row_sum = grad_row_sum + jnp.sum(grad_rows, axis=0)
        grad_out_w = grad_out_w + jnp.einsum(
            "th,td->hd", mixture_low, grad_low, preferred_element_type=jnp.float32
        )
        grad_down_w = grad_down_w + jnp.einsum(
            "tf,td->fd", active_low, grad_low, preferred_element_type=jnp.float32
        )
        grad_active = jnp.einsum("td,fd->tf", grad_low, w_down, preferred_element_type=jnp.float32)
        gelu_values, gelu_pull = jax.vjp(gelu_exact, up_lin)
        grad_up_low = gelu_pull(grad_active)[0].astype(jnp.bfloat16)
        grad_up_b = grad_up_b + jnp.sum(grad_up_low.astype(jnp.float32), axis=0)
        grad_up_w = grad_up_w + jnp.einsum(
            "td,tf->df", low_second, grad_up_low, preferred_element_type=jnp.float32
        )
        second_part = jnp.einsum("tf,df->td", grad_up_low, w_up, preferred_element_type=jnp.float32)
        grad_mix_low = jnp.einsum(
            "td,hd->th", grad_low, w_out, preferred_element_type=jnp.float32
        ).astype(jnp.bfloat16)
        grad_mixture = jnp.transpose(grad_mix_low.reshape(tokens_here, heads_here, HDIM), (1, 0, 2))
        row_dots = jnp.sum(grad_mixture.astype(jnp.float32) * mixture, axis=-1)
        grad_queries, key_terms = attend_backward(
            query_heads, blocks, places, log_sum, grad_mixture, row_dots
        )
        keyval_grad = key_terms[0]
        for reach_step in range(1, REACH + 1):
            keyval_grad = keyval_grad + shifted(
                key_terms[reach_step].astype(jnp.bfloat16), "dp", -reach_step
            ).astype(jnp.float32)
        half_grad = lax.psum_scatter(
            keyval_grad.astype(jnp.bfloat16), "tensor", scatter_dimension=1, tiled=True
        ).astype(jnp.float32)
        unspun_half = rotate(half_grad[:, None, :], cos_table, -sine_table)[:, 0, :]
        half_grad_low = jnp.where(first_core, unspun_half, half_grad).astype(jnp.bfloat16)
        grad_keyval_b = grad_keyval_b + jnp.sum(half_grad_low.astype(jnp.float32), axis=0)
        grad_keyval_w = grad_keyval_w + jnp.einsum(
            "td,tk->dk", low_first, half_grad_low, preferred_element_type=jnp.float32
        )
        query_rows = jnp.transpose(grad_queries, (1, 0, 2)) * query_scale
        grad_query_low = (
            rotate(query_rows, cos_table, -sine_table)
            .reshape(tokens_here, heads_here * HDIM)
            .astype(jnp.bfloat16)
        )
        grad_query_b = grad_query_b + jnp.sum(grad_query_low.astype(jnp.float32), axis=0)
        grad_query_w = grad_query_w + jnp.einsum(
            "td,tq->dq", low_first, grad_query_low, preferred_element_type=jnp.float32
        )
        first_part = jnp.einsum(
            "tq,dq->td", grad_query_low, w_query, preferred_element_type=jnp.float32
        ) + jnp.einsum("tk,dk->td", half_grad_low, w_keyval, preferred_element_type=jnp.float32)
        grad_first, grad_second = (
            lax.psum(first_part.astype(jnp.bfloat16), "tensor").astype(jnp.float32),
            lax.psum(second_part.astype(jnp.bfloat16), "tensor").astype(jnp.float32),
        )
        grad_n1_gain = grad_n1_gain + jnp.sum(grad_first * normed, axis=0)
        grad_n1_bias = grad_n1_bias + jnp.sum(grad_first, axis=0)
        grad_n2_gain = grad_n2_gain + jnp.sum(grad_second * normed, axis=0)
        grad_n2_bias = grad_n2_bias + jnp.sum(grad_second, axis=0)
        input_total = (
            grad_rows
            + norm_backward(grad_first, normed, scaling, norm1_gain)
            + norm_backward(grad_second, normed, scaling, norm2_gain)
        )
        input_rows.append(input_total.astype(jnp.bfloat16))
    summed_query, summed_keyval, summed_out, summed_up, summed_down = (
        lax.psum_scatter(grad_query_w, "dp", scatter_dimension=0, tiled=True),
        lax.psum_scatter(grad_keyval_w, "dp", scatter_dimension=0, tiled=True),
        lax.psum_scatter(grad_out_w, "dp", scatter_dimension=1, tiled=True),
        lax.psum_scatter(grad_up_w, "dp", scatter_dimension=0, tiled=True),
        lax.psum_scatter(grad_down_w, "dp", scatter_dimension=1, tiled=True),
    )
    vector_sums = lax.psum(
        (
            grad_n1_gain,
            grad_n1_bias,
            grad_n2_gain,
            grad_n2_bias,
            grad_row_sum,
            grad_query_b,
            grad_keyval_b,
            grad_up_b,
        ),
        "dp",
    )
    (
        sum_n1_gain,
        sum_n1_bias,
        sum_n2_gain,
        sum_n2_bias,
        sum_rows,
        sum_query_b,
        sum_keyval_b,
        sum_up_b,
    ) = vector_sums
    return (
        jnp.stack(layer_rows),
        jnp.stack(cache_rows),
        jnp.stack(input_rows),
        sum_n1_gain,
        sum_n1_bias,
        sum_n2_gain,
        sum_n2_bias,
        summed_query,
        sum_query_b,
        summed_keyval,
        sum_keyval_b,
        summed_out,
        sum_rows,
        summed_up,
        sum_up_b,
        summed_down,
        sum_rows,
    )


def nn(a, b):
    return jnp.dot(a, b, preferred_element_type=F32)


def nt(a, b):
    return lax.dot_general(a, b, (((1,), (1,)), ((), ())), preferred_element_type=F32)


def chunk_list(q_cols, kv_cols, ff_cols, pieces):
    sizes = [kv_cols, q_cols, q_cols] + [ff_cols // pieces] * (2 * pieces)
    at = 0
    out = []
    for size in sizes:
        out.append((at, size))
        at += size
    return out


def near_tiles(n, half):
    own = REACH * n
    return [(own + a, half, a, n - a, True) for a in range(0, n, half)]


def far_tiles(n, half):
    own = REACH * n
    out = [(own - j * n, n, 0, n, False) for j in range(1, REACH)]
    return out + [(a, half, 0, min(n, a + half), False) for a in range(0, n, half)]


def spin(rows, cos, sine):
    h = ROT // 2
    a, b, rest = rows[..., :h, :], rows[..., h:ROT, :], rows[..., ROT:, :]
    return jnp.concatenate([a * cos - b * sine, b * cos + a * sine, rest], axis=-2)


def fused_kernel(
    chunks, pieces,
    x, dy, positions, g1, b1, g2, b2, w_query, b_query, w_keyval, b_keyval, w_out, b_out, w_up, b_up, w_down, b_down,
    layer_out, keyval_out, input_grad, grads_out, vec_out,
    W, G, n1T, n2, n2T, dyT, wqT, qT, doT, oT, o_nat, lse, dvec, kvwin, kvTwin, low_kv,
    cos, sine, start, m_s, l_s, acc, gbuf, dubuf, dqT, dkv, dkvT, turned, hs, hr, hx, hxr, kvo, yp, yr, d2p, d2r,
    r1, r2, r3, vec, vp, vz, dql, dkl,
    gzs, gzr, g2s, g2r, g3s, g3r, a1s, a1r, a2s, a2r, azs, azr,
    hfs, hfr, hbs, hbr, fws, fwr, xs, xr, ts, tr, vs, vr,
):
    T, D = x.shape
    M, W_rows, KV = kvwin.shape
    n = T // M
    heads = qT.shape[0] // M
    hq = heads * HDIM
    own = REACH * n
    piece = dubuf.shape[2]
    scale = HDIM ** (-0.5)
    me = lax.axis_index("dp")
    core = lax.axis_index("tensor")
    count = lax.axis_size("dp")
    z, y, xx = me // 4, (me // 2) % 2, me % 2
    shard_rows = w_query.shape[0]
    n_chunks = len(chunks)
    kKV, kQ, kO = 0, 1, 2
    kUp = [3 + 2 * c for c in range(pieces)]
    kDown = [4 + 2 * c for c in range(pieces)]
    mine = pl.ds(pl.multiple_of(core * HDIM, HDIM), HDIM)
    other = pl.ds(pl.multiple_of((1 - core) * HDIM, HDIM), HDIM)

    def at(zz, yy, xo):
        return {"dp": zz * 4 + yy * 2 + xo}

    z_ids = [at((z + d) % 4, y, xx) for d in (1, 2, 3)]
    y_id, x_id, d_id = at(z, 1 - y, xx), at(z, y, 1 - xx), at(z, 1 - y, 1 - xx)
    t_id = {"tensor": 1 - core}

    def send(src, dst, ss, rs, to):
        return pltpu.make_async_remote_copy(
            src_ref=src, dst_ref=dst, send_sem=ss, recv_sem=rs, device_id=to, device_id_type=MESH
        )

    bar = pltpu.get_barrier_semaphore()
    peers = z_ids + [y_id, x_id, d_id, t_id]
    peers += [{"dp": (me + s) % count} for s in range(1, REACH + 1)]
    peers += [{"dp": (me + count - s) % count} for s in range(1, REACH + 1)]
    for p in peers:
        pl.semaphore_signal(bar, inc=1, device_id=p, device_id_type=MESH)
    pl.semaphore_wait(bar, len(peers))

    def cols(k):
        return pl.ds(chunks[k][0], chunks[k][1])

    def halves(k):
        c0, cn = chunks[k]
        if cn < 256:
            return pl.ds(c0, cn), None
        first = cn // 256 * 128
        return pl.ds(c0, first), pl.ds(c0 + first, cn - first)

    def gather_z(k):
        r = W.at[z, y, xx, :, cols(k)]
        return [send(r, r, gzs.at[k, j], gzr.at[k, j], z_ids[j]) for j in range(3)]

    def gather_col(k):
        r = W.at[:, y, xx, :, cols(k)]
        return [send(r, r, g2s.at[k, 0], g2r.at[k, 0], x_id), send(r, r, g2s.at[k, 1], g2r.at[k, 1], y_id)]

    def gather_far(k):
        first, second = halves(k)
        r = W.at[:, y, 1 - xx, :, first]
        out = [send(r, r, g3s.at[k, 0], g3r.at[k, 0], y_id)]
        if second is not None:
            r = W.at[:, 1 - y, xx, :, second]
            out.append(send(r, r, g3s.at[k, 1], g3r.at[k, 1], x_id))
        return out

    def start1(k):
        for c in gather_z(k):
            c.start()

    def step2(k):
        for c in gather_z(k):
            c.wait_recv()
        for c in gather_col(k):
            c.start()

    def step3(k):
        for c in gather_col(k):
            c.wait_recv()
        for c in gather_far(k):
            c.start()

    def arrived(k):
        for c in gather_far(k):
            c.wait_recv()

    def weight(k):
        c0, cn = chunks[k]
        return W[:, :, :, :, c0 : c0 + cn].reshape(D, cn)

    def red1(k):
        first, second = halves(k)
        out = [send(G.at[:, :, 1 - xx, :, first], r1.at[:, :, :, first], a1s.at[k, 0], a1r.at[k, 0], x_id)]
        if second is not None:
            out.append(send(G.at[:, 1 - y, :, :, second], r1.at[:, :, :, second], a1s.at[k, 1], a1r.at[k, 1], y_id))
        return out

    def red2(k):
        first, second = halves(k)
        out = [send(r1.at[:, 1 - y, :, first], r2.at[:, :, first], a2s.at[k, 0], a2r.at[k, 0], y_id)]
        if second is not None:
            out.append(send(r1.at[:, 1 - xx, :, second], r2.at[:, :, second], a2s.at[k, 1], a2r.at[k, 1], x_id))
        return out

    def red3(k):
        return [
            send(r2.at[(z + j + 1) % 4, :, cols(k)], r3.at[j, :, cols(k)], azs.at[k, j], azr.at[k, j], z_ids[j])
            for j in range(3)
        ]

    def step_a(k):
        for c in red1(k):
            c.start()

    def step_b(k):
        first, second = halves(k)
        for c in red1(k):
            c.wait_recv()

        def add(i, _):
            zz, o = i // 2, i % 2
            r1[zz, o, :, first] = r1[zz, o, :, first] + G[zz, o, xx, :, first]
            if second is not None:
                r1[zz, o, :, second] = r1[zz, o, :, second] + G[zz, y, o, :, second]
            return 0

        lax.fori_loop(0, 8, add, 0)
        for c in red2(k):
            c.start()

    def step_c(k):
        first, second = halves(k)
        for c in red2(k):
            c.wait_recv()

        def add(i, _):
            r2[i, :, first] = r2[i, :, first] + r1[i, y, :, first]
            if second is not None:
                r2[i, :, second] = r2[i, :, second] + r1[i, xx, :, second]
            return 0

        lax.fori_loop(0, 4, add, 0)
        for c in red3(k):
            c.start()

    def step_e(k):
        for c in red3(k):
            c.wait_recv()
        total = r2[z, :, cols(k)].astype(F32)
        for j in range(3):
            total = total + r3[j, :, cols(k)].astype(F32)
        grads_out[:, cols(k)] = total

    def place(k, block):
        c0 = chunks[k][0]
        W[z, y, xx, :, c0 : c0 + block.shape[1]] = block

    place(kKV, jnp.concatenate([w_keyval[...], jnp.zeros((shard_rows, HDIM), BF16)], axis=1))
    start1(kKV)
    place(kQ, w_query[...])
    start1(kQ)
    place(kO, w_out[...])
    for c in range(pieces):
        place(kUp[c], w_up[:, c * piece : (c + 1) * piece])
        place(kDown[c], w_down[:, c * piece : (c + 1) * piece])

    R = 256
    vec[...] = jnp.zeros_like(vec)

    def row(ref):
        return ref[...].reshape(1, ref.shape[0])

    g1v, b1v, g2v, b2v = row(g1), row(b1), row(g2), row(b2)

    def xhat_of(rows):
        v = x[rows, :].astype(F32)
        c = v - jnp.mean(v, axis=-1, keepdims=True)
        rstd = lax.rsqrt(jnp.mean(c * c, axis=-1, keepdims=True) + epsilon)
        return v, c * rstd, rstd

    def norm_tile(i, _):
        rows = pl.ds(pl.multiple_of(i * R, R), R)
        _, xh, _ = xhat_of(rows)
        n1v = (xh * g1v + b1v).astype(BF16)
        n2v = (xh * g2v + b2v).astype(BF16)
        n2[rows, :] = n2v
        n1T[:, rows] = n1v.T
        n2T[:, rows] = n2v.T
        d = dy[rows, :]
        dyT[:, rows] = d.T
        vec[4:5, :] += jnp.sum(d.astype(F32), axis=0, keepdims=True)
        return 0

    lax.fori_loop(0, T // R, norm_tile, 0)
    step2(kKV)
    h = ROT // 2
    index = lax.broadcasted_iota(jnp.int32, (h, 1), 0)
    inverse = jnp.zeros((h, 1), F32)
    for i in range(h):
        inverse = jnp.where(index == i, 10000.0 ** (-(2.0 * i) / ROT), inverse)
    for m in range(M):
        ms = slice(m * n, (m + 1) * n)
        place_row = positions[m : m + 1, :]
        angle = inverse * place_row.astype(F32)
        cos[:, ms] = jnp.cos(angle)
        sine[:, ms] = jnp.sin(angle)
        start[m] = lax.broadcasted_iota(jnp.int32, (1, n), 1) + own - place_row

    def keyval_spin(rows, m, sign):
        ms = slice(m * n, (m + 1) * n)
        return spin(rows, jnp.where(core == 0, cos[:, ms], 1.0), jnp.where(core == 0, sign * sine[:, ms], 0.0))

    def column(ref):
        size = ref.shape[0]
        return jnp.broadcast_to(ref[...].reshape(1, size), (8, size)).T[:, 0:1]

    step3(kKV)
    step2(kQ)
    arrived(kKV)
    wkvT = weight(kKV).T[0:HDIM]
    bkv = column(b_keyval)
    for m in range(M):
        ms = slice(m * n, (m + 1) * n)
        low_kv[m] = keyval_spin(nn(wkvT, n1T[:, ms]) + bkv, m, 1.0).astype(BF16)
    kvTwin[:, mine, own : own + n] = low_kv[...]

    def block(s):
        return pl.ds((REACH - s) * n, n)

    def halo(s):
        return send(
            low_kv, kvTwin.at[:, mine, block(s)], hfs.at[s - 1], hfr.at[s - 1], {"dp": (me + s) % count}
        )

    def across(s):
        part = kvTwin.at[:, mine, block(s)]
        return send(part, part, fws.at[s], fwr.at[s], t_id)

    for s in range(1, REACH + 1):
        @pl.when(me + s < count)
        def _(s=s):
            halo(s).start()
    across(0).start()

    start1(kO)
    start1(kUp[0])
    step3(kQ)
    across(0).wait_recv()
    for m in range(M):
        natural = kvTwin[m, :, own : own + n].T
        kvwin[m, own : own + n, :] = natural
        keyval_out[m] = natural
    arrived(kQ)
    wqT[...] = weight(kQ).T
    bq = column(b_query)
    for m in range(M):
        ms = slice(m * n, (m + 1) * n)
        lin = nn(wqT[...], n1T[:, ms]) + bq
        spun = spin(lin.reshape(heads, HDIM, n), cos[:, ms], sine[:, ms]) * scale
        qT[m * heads : (m + 1) * heads] = spun.astype(BF16)
    near, far = near_tiles(n, n // 2), far_tiles(n, n // 2)
    tops, totals, sums = lse, dvec, dqT

    def visible(w0, kn, q0, qn, first, causal):
        key = lax.broadcasted_iota(jnp.int32, (kn, 1), 0) + w0
        seen = key >= first
        if causal:
            query = lax.broadcasted_iota(jnp.int32, (1, qn), 1) + (q0 + own)
            seen = seen & (key <= query)
        return seen

    def padded_query(i):
        return jnp.concatenate([qT[i], jnp.zeros((KV - HDIM, n), BF16)], axis=0)

    def forward_near(i, _):
        m = i // heads
        q = padded_query(i)
        first = start[m]
        m_s[...] = jnp.full_like(m_s, LOW)
        l_s[...] = jnp.zeros_like(l_s)
        acc[...] = jnp.zeros_like(acc)
        forward_tiles(m, q, first, near)
        tops[i], totals[i], sums[i] = m_s[...], l_s[...], acc[...]
        return 0

    def forward_tiles(m, q, first, tiles):
        for w0, kn, q0, qn, causal in tiles:
            qs = slice(q0, q0 + qn)
            sc = nn(kvwin[m, w0 : w0 + kn, :], q[:, qs])
            sc = jnp.where(visible(w0, kn, q0, qn, first[:, qs], causal), sc, LOW)
            before = m_s[:, qs]
            top = jnp.maximum(before, jnp.max(sc, axis=0, keepdims=True))
            p = jnp.exp(sc - top)
            shrink = jnp.exp(before - top)
            l_s[:, qs] = l_s[:, qs] * shrink + jnp.sum(p, axis=0, keepdims=True)
            m_s[:, qs] = top
            acc[:, qs] = acc[:, qs] * shrink + nn(kvTwin[m, HDIM:KV, w0 : w0 + kn], p.astype(BF16))

    def forward_far(i, _):
        m = i // heads
        q = padded_query(i)
        m_s[...], l_s[...], acc[...] = tops[i], totals[i], sums[i]
        forward_tiles(m, q, start[m], far)
        o = acc[...] / l_s[...]
        oT[i] = o.astype(BF16)
        sums[i] = o
        lse[i] = m_s[...] + jnp.log(l_s[...])
        scheduled(far_plan, i)
        return 0

    def scheduled(plan, i):
        for j, act in plan.items():
            pl.when(i == j)(lambda act=act: (act(), None)[1])

    def near_step(i, _):
        forward_near(i, 0)
        scheduled(near_plan, i)
        return 0

    near_plan = {
        0: lambda: step2(kO),
        4: lambda: start1(kDown[0]),
        8: lambda: (step2(kUp[0]), step3(kO)),
    }
    lax.fori_loop(0, M * heads, near_step, 0)
    for s in range(1, REACH + 1):
        @pl.when(me >= s)
        def _(s=s):
            halo(s).wait_recv()
            across(s).start()

        @pl.when(me < s)
        def _(s=s):
            kvTwin[:, :, block(s)] = jnp.zeros((M, KV, n), BF16)

    step2(kDown[0])
    start1(kUp[1])
    for s in range(1, REACH + 1):
        @pl.when(me >= s)
        def _(s=s):
            across(s).wait_recv()

        for m in range(M):
            kvwin[m, block(s), :] = kvTwin[m, :, block(s)].T

    far_plan = {
        0: lambda: (step3(kUp[0]), start1(kDown[1])),
        2: lambda: step3(kDown[0]),
        4: lambda: (step2(kUp[1]), start1(kUp[2])),
        7: lambda: (step2(kDown[1]), start1(kDown[2])),
        9: lambda: step3(kUp[1]),
    }
    lax.fori_loop(0, M * heads, forward_far, 0)

    arrived(kO)
    wo = weight(kO).T
    for m in range(M):
        ms = slice(m * n, (m + 1) * n)
        doT[m * heads : (m + 1) * heads] = nn(wo, dyT[:, ms]).astype(BF16).reshape(heads, HDIM, n)

    def mix_dots(i, _):
        dvec[i] = jnp.sum(doT[i].astype(F32) * sums[i], axis=0, keepdims=True)
        return 0

    lax.fori_loop(0, M * heads, mix_dots, 0)
    for m in range(M):
        o_nat[m * n : (m + 1) * n, :] = oT[m * heads : (m + 1) * heads].reshape(hq, n).T

    def put_grad(k, leftT, right):
        c0, cn = chunks[k]

        def half(i, _):
            rows = pl.ds(pl.multiple_of(i * (D // 2), 128), D // 2)
            part = nn(leftT[rows, :], right[...]).astype(BF16)
            G[pl.ds(i * 2, 2), :, :, :, c0 : c0 + cn] = part.reshape(2, 2, 2, shard_rows, cn)
            return 0

        lax.fori_loop(0, 2, half, 0)
        step_a(k)

    put_grad(kO, dyT, o_nat)
    step3(kDown[1])
    step2(kUp[2])

    def feed_forward(c):
        ku, kd = kUp[c], kDown[c]
        arrived(ku)
        arrived(kd)
        (u0, _), (d0, _) = chunks[ku], chunks[kd]
        up_bias = b_up[c * piece : (c + 1) * piece].reshape(1, piece)

        def rows_tile(i, _):
            rows = pl.ds(pl.multiple_of(i * R, R), R)
            u = nn(n2[rows, :], W[:, :, :, :, u0 : u0 + piece].reshape(D, piece)) + up_bias
            phi = 0.5 * (1.0 + lax.erf(u * 0.7071067811865476))
            slope = phi + u * (jnp.exp(-0.5 * u * u) * 0.3989422804014327)
            gbuf[rows, c * piece : (c + 1) * piece] = (u * phi).astype(BF16)
            dg = nn(dy[rows, :], W[:, :, :, :, d0 : d0 + piece].reshape(D, piece))
            dubuf[c, rows, :] = (slope * dg).astype(BF16)
            return 0

        lax.fori_loop(0, T // R, rows_tile, 0)
        put_grad(ku, n2T, dubuf.at[c])
        put_grad(kd, dyT, gbuf.at[:, c * piece : (c + 1) * piece])

    def branch_tile(i, _):
        rows = pl.ds(pl.multiple_of(i * R, R), R)
        total = nt(o_nat[rows, :], weight(kO))
        back = jnp.zeros((R, D), F32)
        for c in range(pieces):
            total = total + nt(gbuf[rows, c * piece : (c + 1) * piece], weight(kDown[c]))
            back = back + nt(dubuf[c, rows, :], weight(kUp[c]))
        yp[rows, :] = total.astype(BF16)
        d2p[rows, :] = back.astype(BF16)
        return 0

    y_copy = send(yp, yr, xs.at[0], xr.at[0], t_id)
    d2_copy = send(d2p, d2r, xs.at[1], xr.at[1], t_id)

    def branches():
        lax.fori_loop(0, T // R, branch_tile, 0)
        y_copy.start()
        d2_copy.start()
        for c in range(pieces):
            part = jnp.sum(dubuf[c].astype(F32), axis=0, keepdims=True)
            done = 0
            while done < piece:
                flat = c * piece + done
                line, col = flat // D, flat % D
                width = min(piece - done, D - col)
                vec[6 + line : 7 + line, col : col + width] = part[:, done : done + width]
                done += width

    feed_forward(0)
    step2(kDown[2])

    dkv[...] = jnp.zeros_like(dkv)

    def backward_tiles(i, tiles):
        m = i // heads
        zero = jnp.zeros((HDIM, n), BF16)
        q = jnp.concatenate([qT[i], zero], axis=0)
        do = jnp.concatenate([zero, doT[i]], axis=0)
        qdo = jnp.concatenate([qT[i], doT[i]], axis=0).T
        first, ls, dots = start[m], lse[i], dvec[i]
        for w0, kn, q0, qn, causal in tiles:
            qs = slice(q0, q0 + qn)
            rows = kvwin[m, w0 : w0 + kn, :]
            sc = nn(rows, q[:, qs])
            sc = jnp.where(visible(w0, kn, q0, qn, first[:, qs], causal), sc, LOW)
            p = jnp.exp(sc - ls[:, qs])
            dp = nn(rows, do[:, qs])
            ds = (p * (dp - dots[:, qs])).astype(BF16)
            for_k = nn(ds, qdo[qs])
            for_v = nn(p.astype(BF16), qdo[qs])
            lane = lax.broadcasted_iota(jnp.int32, for_k.shape, 1)
            dkv[m, w0 : w0 + kn, :] += jnp.where(lane < HDIM, for_k, for_v)
            dqT[i, :, qs] += nn(kvTwin[m, 0:HDIM, w0 : w0 + kn], ds)

    def backward_far(i, _):
        scheduled(feed_plan, i)
        dqT[i] = jnp.zeros((HDIM, n), F32)
        backward_tiles(i, far)
        scheduled(back_far_plan, i)
        return 0

    def backward_near(i, _):
        backward_tiles(i, near)
        scheduled(back_near_plan, i)
        return 0

    def back_copy(s, m):
        return send(
            hs.at[s - 1, m], hr.at[s - 1, m], hbs.at[s - 1, m], hbr.at[s - 1, m],
            {"dp": (me + count - s) % count},
        )

    def half_copy(m):
        part = pl.ds(0, own)
        return send(hx.at[m, :, part], hxr.at[m, :, part], xs.at[2 + m], xr.at[2 + m], t_id)

    def own_copy(m):
        part = pl.ds(own, n)
        return send(hx.at[m, :, part], hxr.at[m, :, part], xs.at[2 + M + m], xr.at[2 + M + m], t_id)

    def split(m, j):
        js = slice(j * n, (j + 1) * n)
        turned[...] = dkv[m, js, :].T
        dkvT[m, :, js] = turned[mine, :]
        hx[m, :, js] = turned[other, :].astype(BF16)

    def give_half(m):
        for j in range(REACH):
            split(m, j)
        half_copy(m).start()

    def return_halo(m):
        half_copy(m).wait_recv()
        for j in range(REACH):
            js = slice(j * n, (j + 1) * n)
            hs[REACH - j - 1, m] = (dkvT[m, :, js] + hxr[m, :, js].astype(F32)).astype(BF16)
        for s in range(1, REACH + 1):
            @pl.when(me >= s)
            def _(s=s):
                back_copy(s, m).start()

    def give_own(m):
        split(m, REACH)
        own_copy(m).start()

    feed_plan = {
        3: lambda: feed_forward(1),
        6: lambda: (feed_forward(2), branches()),
    }
    back_far_plan = {
        0: lambda: (step3(kUp[2]), step_b(kO)),
        1: lambda: (step3(kDown[2]), step_b(kUp[0])),
        2: lambda: (step_b(kDown[0]), step_c(kO)),
        3: lambda: (step_c(kUp[0]), step_c(kDown[0])),
        4: lambda: step_e(kO),
        5: lambda: (give_half(0), step_b(kUp[1]), step_e(kUp[0])),
        6: lambda: (step_b(kDown[1]), step_c(kUp[1]), step_e(kDown[0])),
        7: lambda: (return_halo(0), step_c(kDown[1])),
        8: lambda: (step_b(kUp[2]), step_e(kUp[1])),
        9: lambda: step_b(kDown[2]),
        10: lambda: (step_c(kUp[2]), step_e(kDown[1])),
        11: lambda: (give_half(1), step_c(kDown[2])),
    }
    back_near_plan = {
        2: lambda: return_halo(1),
        5: lambda: (give_own(0), step_e(kUp[2])),
        8: lambda: step_e(kDown[2]),
        11: lambda: give_own(1),
    }
    lax.fori_loop(0, M * heads, backward_far, 0)
    lax.fori_loop(0, M * heads, backward_near, 0)

    for m in range(M):
        ms = slice(m * n, (m + 1) * n)
        rows = dqT[m * heads : (m + 1) * heads] * scale
        low = spin(rows, cos[:, ms], -sine[:, ms]).astype(BF16)
        dql[ms, :] = low.reshape(hq, n).T
    put_grad(kQ, n1T, dql)
    vec[5:6, 0:hq] = jnp.sum(dql[...].astype(F32), axis=0, keepdims=True)

    for m in range(M):
        ms = slice(m * n, (m + 1) * n)
        own_copy(m).wait_recv()
        dko = dkvT[m, :, own : own + n] + hxr[m, :, own : own + n].astype(F32)
        kvo[...] = dko
        for s in range(1, REACH + 1):
            @pl.when(me + s < count)
            def _(s=s, m=m):
                back_copy(s, m).wait_recv()
                kvo[...] += hr[s - 1, m].astype(F32)
        low = keyval_spin(kvo[...], m, -1.0).astype(BF16)
        dkl[ms, :] = jnp.concatenate([low, jnp.zeros((KV - HDIM, n), BF16)], axis=0).T
    put_grad(kKV, n1T, dkl)
    vec[5:6, hq : hq + KV] = jnp.sum(dkl[...].astype(F32), axis=0, keepdims=True)

    def d1_copy(i):
        rows = pl.ds(pl.multiple_of(i * R, R), R)
        return send(gbuf.at[rows, pl.ds(0, D)], n2.at[rows], ts.at[i], tr.at[i], t_id)

    def first_tile(i, _):
        rows = pl.ds(pl.multiple_of(i * R, R), R)
        gbuf[rows, 0:D] = (nt(dql[rows, :], weight(kQ)) + nt(dkl[rows, :], weight(kKV))).astype(BF16)
        d1_copy(i).start()
        return 0

    lax.fori_loop(0, T // R, first_tile, 0)
    step_b(kQ)
    step_b(kKV)

    y_copy.wait_recv()
    both_bias = row(b_out) + row(b_down)

    def out_tile(i, _):
        rows = pl.ds(pl.multiple_of(i * R, R), R)
        both = (yp[rows, :].astype(F32) + yr[rows, :].astype(F32)) + both_bias
        layer_out[rows, :] = (x[rows, :].astype(F32) + both).astype(BF16)
        return 0

    lax.fori_loop(0, T // R, out_tile, 0)
    d2_copy.wait_recv()
    step_c(kQ)

    def last_tile(i, _):
        rows = pl.ds(pl.multiple_of(i * R, R), R)
        _, xh, rstd = xhat_of(rows)
        d1_copy(i).wait_recv()
        dn1 = gbuf[rows, 0:D].astype(F32) + n2[rows, :].astype(F32)
        dn2 = d2p[rows, :].astype(F32) + d2r[rows, :].astype(F32)
        vec[0:1, :] += jnp.sum(dn1 * xh, axis=0, keepdims=True)
        vec[1:2, :] += jnp.sum(dn1, axis=0, keepdims=True)
        vec[2:3, :] += jnp.sum(dn2 * xh, axis=0, keepdims=True)
        vec[3:4, :] += jnp.sum(dn2, axis=0, keepdims=True)
        a = dn1 * g1v + dn2 * g2v
        back = a - jnp.mean(a, axis=-1, keepdims=True) - xh * jnp.mean(a * xh, axis=-1, keepdims=True)
        input_grad[rows, :] = (dy[rows, :].astype(F32) + rstd * back).astype(BF16)
        return 0

    lax.fori_loop(0, T // R, last_tile, 0)

    flat = y * 2 + xx
    vp[flat] = vec[...]
    plane = [send(vp.at[flat], vp.at[flat], vs.at[j], vr.at[j], to) for j, to in enumerate((x_id, y_id, d_id))]
    for c in plane:
        c.start()
    step_c(kKV)
    for c in plane:
        c.wait_recv()
    vz[z] = (vp[0] + vp[1]) + (vp[2] + vp[3])
    along = [send(vz.at[z], vz.at[z], vs.at[3 + j], vr.at[3 + j], z_ids[j]) for j in range(3)]
    for c in along:
        c.start()
    step_e(kQ)
    step_e(kKV)
    for c in along:
        c.wait_recv()
    vec_out[...] = (vz[0] + vz[1]) + (vz[2] + vz[3])

    for k in range(n_chunks):
        for c in gather_z(k) + gather_col(k) + gather_far(k) + red1(k) + red2(k) + red3(k):
            c.wait_send()
    across(0).wait_send()
    for s in range(1, REACH + 1):
        @pl.when(me + s < count)
        def _(s=s):
            halo(s).wait_send()

        @pl.when(me >= s)
        def _(s=s):
            across(s).wait_send()
            for m in range(M):
                back_copy(s, m).wait_send()
    for m in range(M):
        half_copy(m).wait_send()
        own_copy(m).wait_send()
    for i in range(T // R):
        d1_copy(i).wait_send()
    for c in [y_copy, d2_copy] + plane + along:
        c.wait_send()


def finish_kernel(
    chunks, pieces, grads, vec, n1g, n1b, n2g, n2b, wq, bq, wkv, bkv, wo, bo, wu, bu, wd, bd
):
    hq, half, piece, D = wq.shape[1], wkv.shape[1], chunks[3][1], vec.shape[1]
    for out, r in ((n1g, 0), (n1b, 1), (n2g, 2), (n2b, 3), (bo, 4), (bd, 4)):
        out[...] = vec[r].reshape(D)
    q0, o0 = chunks[1][0], chunks[2][0]
    wq[...] = grads[:, q0 : q0 + hq]
    wkv[...] = grads[:, 0:half]
    wo[...] = grads[:, o0 : o0 + hq]
    for c in range(pieces):
        u0, d0 = chunks[3 + 2 * c][0], chunks[4 + 2 * c][0]
        wu[:, c * piece : (c + 1) * piece] = grads[:, u0 : u0 + piece]
        wd[:, c * piece : (c + 1) * piece] = grads[:, d0 : d0 + piece]
    bq[...] = vec[5:6, 0:hq].reshape(hq)
    bkv[...] = vec[5:6, hq : hq + half].reshape(half)
    for r in range(bu.shape[0] // D):
        bu[r * D : (r + 1) * D] = vec[6 + r].reshape(D)


def fused_layer(arguments, pieces):
    (hidden_in, positions, out_grad, g1, b1, g2, b2, w_query, b_query, w_keyval, b_keyval,
     w_out, b_out, w_up, b_up, w_down, b_down) = arguments
    M, n, D = hidden_in.shape
    T = M * n
    hq, F, half, rows = b_query.shape[0], b_up.shape[0], b_keyval.shape[0], w_query.shape[0]
    heads, KV, piece = hq // HDIM, 2 * half, F // pieces
    chunks = chunk_list(hq, KV, F, pieces)
    C = chunks[-1][0] + chunks[-1][1]
    k = len(chunks)
    Wn = (REACH + 1) * n
    V = pltpu.VMEM
    S = pltpu.SemaphoreType.DMA
    sds = jax.ShapeDtypeStruct
    vm = pl.BlockSpec(memory_space=pltpu.VMEM)
    mh = M * heads
    scratch = [
        V((4, 2, 2, rows, C), BF16), V((4, 2, 2, rows, C), BF16),
        V((D, T), BF16), V((T, D), BF16), V((D, T), BF16), V((D, T), BF16),
        V((hq, D), BF16), V((mh, HDIM, n), BF16), V((mh, HDIM, n), BF16), V((mh, HDIM, n), BF16),
        V((T, hq), BF16), V((mh, 1, n), F32), V((mh, 1, n), F32),
        V((M, Wn, KV), BF16), V((M, KV, Wn), BF16), V((M, HDIM, n), BF16),
        V((ROT // 2, T), F32), V((ROT // 2, T), F32), V((M, 1, n), jnp.int32),
        V((1, n), F32), V((1, n), F32), V((HDIM, n), F32),
        V((T, F), BF16), V((pieces, T, piece), BF16),
        V((mh, HDIM, n), F32), V((M, Wn, KV), F32), V((M, HDIM, Wn), F32), V((KV, n), F32),
        V((REACH, M, HDIM, n), BF16), V((REACH, M, HDIM, n), BF16),
        V((M, HDIM, Wn), BF16), V((M, HDIM, Wn), BF16), V((HDIM, n), F32),
        V((T, D), BF16), V((T, D), BF16), V((T, D), BF16), V((T, D), BF16),
        V((4, 2, rows, C), BF16), V((4, rows, C), BF16), V((3, rows, C), BF16),
        V((8, D), F32), V((4, 8, D), F32), V((4, 8, D), F32),
        V((T, hq), BF16), V((T, KV), BF16),
        S((k, 3)), S((k, 3)), S((k, 2)), S((k, 2)), S((k, 2)), S((k, 2)),
        S((k, 2)), S((k, 2)), S((k, 2)), S((k, 2)), S((k, 3)), S((k, 3)),
        S((REACH,)), S((REACH,)), S((REACH, M)), S((REACH, M)), S((REACH + 1,)), S((REACH + 1,)),
        S((2 + 2 * M,)), S((2 + 2 * M,)), S((T // 256,)), S((T // 256,)), S((6,)), S((6,)),
    ]
    y_out, kv_out, x_out, grads, vec = pl.pallas_call(
        functools.partial(fused_kernel, chunks, pieces),
        out_shape=(
            sds((T, D), BF16), sds((M, n, KV), BF16), sds((T, D), BF16), sds((rows, C), F32), sds((8, D), F32),
        ),
        in_specs=[vm] * 17,
        out_specs=(vm,) * 5,
        scratch_shapes=scratch,
        compiler_params=pltpu.CompilerParams(
            collective_id=0, has_side_effects=True, vmem_limit_bytes=62 << 20
        ),
        name="fused_layer",
    )(hidden_in.reshape(T, D), out_grad.reshape(T, D), positions, g1, b1, g2, b2, w_query, b_query,
      w_keyval, b_keyval, w_out.T, b_out, w_up, b_up, w_down.T, b_down)
    vector = sds((D,), F32)
    out_shape = (
        vector, vector, vector, vector,
        sds(w_query.shape, F32), sds(b_query.shape, F32), sds(w_keyval.shape, F32), sds(b_keyval.shape, F32),
        sds(w_out.shape[::-1], F32), vector, sds(w_up.shape, F32), sds(b_up.shape, F32), sds(w_down.shape[::-1], F32), vector,
    )
    outs = pl.pallas_call(
        functools.partial(finish_kernel, chunks, pieces),
        out_shape=out_shape,
        in_specs=[vm] * 2,
        out_specs=(vm,) * 14,
        compiler_params=pltpu.CompilerParams(vmem_limit_bytes=60 << 20),
        name="finish_layer",
    )(grads, vec)
    outs = [y_out.reshape(hidden_in.shape), kv_out, x_out.reshape(hidden_in.shape)] + list(outs)
    outs[11], outs[15] = outs[11].T, outs[15].T
    return tuple(outs)


PIECES = 3


def fits_fused(hidden_in, query_weight, up_weight):
    rows, hq = query_weight.shape
    return (
        lax.axis_size("dp") == 16
        and rows % 16 == 0
        and hq % 384 == 0
        and up_weight.shape[1] % (PIECES * 256) == 0
        and up_weight.shape[1] >= hidden_in.shape[2]
        and hidden_in.shape[1] % 256 == 0
    )


def on_device(*arguments):
    if fits_fused(arguments[0], arguments[7], arguments[13]):
        return fused_layer(arguments, PIECES)
    return plain_layer(*arguments)


def solution(mesh):
    return jax.shard_map(
        on_device,
        mesh=mesh,
        in_specs=(
            P(None, "dp", None),
            P(None, "dp"),
            P(None, "dp", None),
            P(),
            P(),
            P(),
            P(),
            P("dp", "tensor"),
            P("tensor"),
            P("dp", "tensor"),
            P("tensor"),
            P("tensor", "dp"),
            P(),
            P("dp", "tensor"),
            P("tensor"),
            P("tensor", "dp"),
            P(),
        ),
        out_specs=(
            P(None, "dp", None),
            P(None, "dp", None),
            P(None, "dp", None),
            P(),
            P(),
            P(),
            P(),
            P("dp", "tensor"),
            P("tensor"),
            P("dp", "tensor"),
            P("tensor"),
            P("tensor", "dp"),
            P(),
            P("dp", "tensor"),
            P("tensor"),
            P("tensor", "dp"),
            P(),
        ),
        check_vma=False,
    )
```

```python
import functools
import jax
import jax.numpy as jnp
from jax import lax
from jax.experimental import pallas as pl
from jax.experimental.pallas import tpu as pltpu
from jax.sharding import PartitionSpec as P

HDIM = 64
ROT = 16
REACH = 4
epsilon = 1e-05
MESH = pl.DeviceIdType.MESH
LOW = -1e30
F32 = jnp.float32
BF16 = jnp.bfloat16


SCHEDULE = {
    "pro": (("z", 0), ("z", 1), ("col", 0), ("z", 3),),
    "norm": (("far", 0),),
    "cos": (("col", 1), ("z", 2),),
    "kv": (("far", 1),),
    "q": (("col", 3),),
    "near0": (("z", 4),),
    "near5": (("z", 5), ("col", 2),),
    "halow": (("col", 4),),
    "acw": (("z", 7),),
    "far0": (("z", 6), ("far", 4), ("far", 3),),
    "far1": (("z", 8), ("col", 5),),
    "far2": (("col", 7), ("col", 6),),
    "far3": (("far", 2),),
    "far4": (("col", 8),),
    "far5": (("far", 5),),
    "bfar1": (("far", 6),),
    "bfar2": (("b", 3), ("b", 4),),
    "bfar3": (("far", 7), ("b", 2),),
    "ffn1": (("c", 3), ("c", 4), ("c", 2),),
    "bfar5": (("far", 8),),
    "bfar6": (("b", 6), ("b", 5), ("ret", 0),),
    "ffn2": (("c", 5), ("c", 6),),
    "bfar7": (("e", 4),),
    "bfar8": (("b", 7),),
    "bfar9": (("b", 8), ("e", 2),),
    "bfar10": (("c", 7), ("c", 8),),
    "bnear1": (("e", 6),),
    "bnear4": (("ret", 1),),
    "bnear6": (("e", 5), ("e", 7),),
    "bnear8": (("e", 3),),
    "bnear11": (("e", 8),),
    "t3": (("b", 0), ("b", 1),),
    "t4": (("c", 0), ("c", 1), ("e", 0),),
    "t5": (("e", 1),),
}
FEED_AT = (4, 7)


def shifted(value, axis, steps):
    count = lax.axis_size(axis)
    initial, last = (max(0, -steps), min(count, count - steps))
    return lax.ppermute(value, axis, [(source, source + steps) for source in range(initial, last)])


def norm_forward(stream):
    average = jnp.mean(stream, axis=-1, keepdims=True)
    centered = stream - average
    spread = jnp.mean(centered * centered, axis=-1, keepdims=True)
    scaling = lax.rsqrt(spread + epsilon)
    normed = centered * scaling
    return (normed, scaling)


def norm_backward(upstream, normed, scaling, norm_gain):
    weighted = upstream * norm_gain
    return scaling * (
        weighted
        - jnp.mean(weighted, axis=-1, keepdims=True)
        - normed * jnp.mean(weighted * normed, axis=-1, keepdims=True)
    )


def rotary_tables(places):
    inverse = 10000.0 ** (-(jnp.arange(ROT // 2, dtype=jnp.float32) * 2.0) / ROT)
    angles = places.astype(jnp.float32)[:, None] * inverse[None, :]
    angles = jnp.concatenate([angles, angles], axis=-1)
    return (jnp.cos(angles), jnp.sin(angles))


def rotate(values, cos_table, sine_table):
    head_part = values[..., :ROT]
    first_half = head_part[..., : ROT // 2]
    second_half = head_part[..., ROT // 2 :]
    turned = jnp.concatenate([-second_half, first_half], axis=-1)
    spun_part = head_part * cos_table[:, None, :] + turned * sine_table[:, None, :]
    return jnp.concatenate([spun_part, values[..., ROT:]], axis=-1)


def gelu_exact(values):
    return jax.nn.gelu(values, approximate=False)


def fetch_weights(shard_weights):
    return (
        lax.all_gather(shard_weights[0], "dp", axis=0, tiled=True),
        lax.all_gather(shard_weights[1], "dp", axis=0, tiled=True),
        lax.all_gather(shard_weights[2], "dp", axis=1, tiled=True),
        lax.all_gather(shard_weights[3], "dp", axis=0, tiled=True),
        lax.all_gather(shard_weights[4], "dp", axis=1, tiled=True),
    )


def score_block(queries, key_rows, places, reach_step):
    tokens_here = queries.shape[1]
    scores = jnp.einsum("htd,kd->htk", queries, key_rows, preferred_element_type=jnp.float32)
    row_ids = jnp.arange(tokens_here, dtype=jnp.int32)
    offsets = reach_step * tokens_here + row_ids[:, None] - row_ids[None, :]
    visible = (offsets >= 0) & (offsets <= places[:, None])
    return (scores, visible[None])


def attend_forward(queries, blocks, places):
    heads_here, tokens_here = (queries.shape[0], queries.shape[1])
    top_score = jnp.full((heads_here, tokens_here), -1e30, jnp.float32)
    totals = jnp.zeros((heads_here, tokens_here), jnp.float32)
    for reach_step, kv_block in enumerate(blocks):
        scores, visible = score_block(queries, kv_block[:, :HDIM], places, reach_step)
        masked = jnp.where(visible, scores, -1e30)
        new_top = jnp.maximum(top_score, jnp.max(masked, axis=-1))
        totals = totals * jnp.exp(top_score - new_top) + jnp.sum(
            jnp.where(visible, jnp.exp(masked - new_top[..., None]), 0.0), axis=-1
        )
        top_score = new_top
    log_sum = top_score + jnp.log(totals)
    mixture = jnp.zeros((heads_here, tokens_here, HDIM), jnp.float32)
    for reach_step, kv_block in enumerate(blocks):
        scores, visible = score_block(queries, kv_block[:, :HDIM], places, reach_step)
        weights_low = jnp.where(visible, jnp.exp(scores - log_sum[..., None]), 0.0).astype(
            jnp.bfloat16
        )
        mixture = mixture + jnp.einsum(
            "htk,kd->htd", weights_low, kv_block[:, HDIM:], preferred_element_type=jnp.float32
        )
    return (mixture, log_sum)


def attend_backward(queries, blocks, places, log_sum, grad_mixture, row_dots):
    grad_queries = jnp.zeros(queries.shape, jnp.float32)
    key_terms = []
    for reach_step, kv_block in enumerate(blocks):
        key_rows = kv_block[:, :HDIM]
        value_rows = kv_block[:, HDIM:]
        scores, visible = score_block(queries, key_rows, places, reach_step)
        weights_full = jnp.where(visible, jnp.exp(scores - log_sum[..., None]), 0.0)
        weights_low = weights_full.astype(jnp.bfloat16)
        grad_weights = jnp.einsum(
            "htd,kd->htk", grad_mixture, value_rows, preferred_element_type=jnp.float32
        )
        grad_scores = (weights_full * (grad_weights - row_dots[..., None])).astype(jnp.bfloat16)
        grad_queries = grad_queries + jnp.einsum(
            "htk,kd->htd", grad_scores, key_rows, preferred_element_type=jnp.float32
        )
        grad_keys = jnp.einsum(
            "htk,htd->kd", grad_scores, queries, preferred_element_type=jnp.float32
        )
        grad_values = jnp.einsum(
            "htk,htd->kd", weights_low, grad_mixture, preferred_element_type=jnp.float32
        )
        key_terms.append(jnp.concatenate([grad_keys, grad_values], axis=-1))
    return (grad_queries, key_terms)


def plain_layer(
    hidden_in,
    positions,
    out_grad,
    norm1_gain,
    norm1_bias,
    norm2_gain,
    norm2_bias,
    query_weight,
    query_bias,
    keyval_weight,
    keyval_bias,
    attn_out_weight,
    attn_out_bias,
    up_weight,
    up_bias,
    down_weight,
    down_bias,
):
    micro_count = hidden_in.shape[0]
    tokens_here = hidden_in.shape[1]
    width = hidden_in.shape[2]
    dp_count = lax.axis_size("dp")
    first_core = lax.axis_index("tensor") == 0
    heads_here = query_bias.shape[0] // HDIM
    query_scale = HDIM ** (-0.5)
    shard_weights = (query_weight, keyval_weight, attn_out_weight, up_weight, down_weight)
    gathered = None
    grad_query_w = jnp.zeros((width, query_weight.shape[1]), jnp.float32)
    grad_keyval_w = jnp.zeros((width, keyval_weight.shape[1]), jnp.float32)
    grad_out_w = jnp.zeros(
        (attn_out_weight.shape[0], attn_out_weight.shape[1] * dp_count), jnp.float32
    )
    grad_up_w = jnp.zeros((width, up_weight.shape[1]), jnp.float32)
    grad_down_w = jnp.zeros((down_weight.shape[0], down_weight.shape[1] * dp_count), jnp.float32)
    grad_n1_gain = jnp.zeros((width,), jnp.float32)
    grad_n1_bias = jnp.zeros((width,), jnp.float32)
    grad_n2_gain = jnp.zeros((width,), jnp.float32)
    grad_n2_bias = jnp.zeros((width,), jnp.float32)
    grad_row_sum = jnp.zeros((width,), jnp.float32)
    grad_query_b = jnp.zeros(query_bias.shape, jnp.float32)
    grad_keyval_b = jnp.zeros(keyval_bias.shape, jnp.float32)
    grad_up_b = jnp.zeros(up_bias.shape, jnp.float32)
    layer_rows = []
    cache_rows = []
    input_rows = []
    for micro_step in range(micro_count):
        gathered = fetch_weights(shard_weights)
        w_query, w_keyval, w_out, w_up, w_down = gathered
        stream = hidden_in[micro_step].astype(jnp.float32)
        places = positions[micro_step]
        normed, scaling = norm_forward(stream)
        low_first = (normed * norm1_gain + norm1_bias).astype(jnp.bfloat16)
        low_second = (normed * norm2_gain + norm2_bias).astype(jnp.bfloat16)
        cos_table, sine_table = rotary_tables(places)
        query_lin = jnp.dot(low_first, w_query, preferred_element_type=jnp.float32) + query_bias
        queries = (
            rotate(query_lin.reshape(tokens_here, heads_here, HDIM), cos_table, sine_table)
            * query_scale
        ).astype(jnp.bfloat16)
        query_heads = jnp.transpose(queries, (1, 0, 2))
        half_lin = jnp.dot(low_first, w_keyval, preferred_element_type=jnp.float32) + keyval_bias
        spun_half = rotate(half_lin[:, None, :], cos_table, sine_table)[:, 0, :]
        half_low = jnp.where(first_core, spun_half, half_lin).astype(jnp.bfloat16)
        keyval = lax.all_gather(half_low, "tensor", axis=1, tiled=True)
        blocks = [keyval] + [
            shifted(keyval, "dp", reach_step) for reach_step in range(1, REACH + 1)
        ]
        mixture, log_sum = attend_forward(query_heads, blocks, places)
        mixture_low = (
            jnp.transpose(mixture, (1, 0, 2))
            .reshape(tokens_here, heads_here * HDIM)
            .astype(jnp.bfloat16)
        )
        up_lin = jnp.dot(low_second, w_up, preferred_element_type=jnp.float32) + up_bias
        active_low = gelu_exact(up_lin).astype(jnp.bfloat16)
        branch_part = jnp.dot(mixture_low, w_out, preferred_element_type=jnp.float32) + jnp.dot(
            active_low, w_down, preferred_element_type=jnp.float32
        )
        branches = lax.psum(branch_part.astype(jnp.bfloat16), "tensor").astype(jnp.float32)
        layer_rows.append((stream + branches + attn_out_bias + down_bias).astype(jnp.bfloat16))
        cache_rows.append(keyval)
        grad_low = out_grad[micro_step]
        grad_rows = grad_low.astype(jnp.float32)
        grad_row_sum = grad_row_sum + jnp.sum(grad_rows, axis=0)
        grad_out_w = grad_out_w + jnp.einsum(
            "th,td->hd", mixture_low, grad_low, preferred_element_type=jnp.float32
        )
        grad_down_w = grad_down_w + jnp.einsum(
            "tf,td->fd", active_low, grad_low, preferred_element_type=jnp.float32
        )
        grad_active = jnp.einsum("td,fd->tf", grad_low, w_down, preferred_element_type=jnp.float32)
        gelu_values, gelu_pull = jax.vjp(gelu_exact, up_lin)
        grad_up_low = gelu_pull(grad_active)[0].astype(jnp.bfloat16)
        grad_up_b = grad_up_b + jnp.sum(grad_up_low.astype(jnp.float32), axis=0)
        grad_up_w = grad_up_w + jnp.einsum(
            "td,tf->df", low_second, grad_up_low, preferred_element_type=jnp.float32
        )
        second_part = jnp.einsum("tf,df->td", grad_up_low, w_up, preferred_element_type=jnp.float32)
        grad_mix_low = jnp.einsum(
            "td,hd->th", grad_low, w_out, preferred_element_type=jnp.float32
        ).astype(jnp.bfloat16)
        grad_mixture = jnp.transpose(grad_mix_low.reshape(tokens_here, heads_here, HDIM), (1, 0, 2))
        row_dots = jnp.sum(grad_mixture.astype(jnp.float32) * mixture, axis=-1)
        grad_queries, key_terms = attend_backward(
            query_heads, blocks, places, log_sum, grad_mixture, row_dots
        )
        keyval_grad = key_terms[0]
        for reach_step in range(1, REACH + 1):
            keyval_grad = keyval_grad + shifted(
                key_terms[reach_step].astype(jnp.bfloat16), "dp", -reach_step
            ).astype(jnp.float32)
        half_grad = lax.psum_scatter(
            keyval_grad.astype(jnp.bfloat16), "tensor", scatter_dimension=1, tiled=True
        ).astype(jnp.float32)
        unspun_half = rotate(half_grad[:, None, :], cos_table, -sine_table)[:, 0, :]
        half_grad_low = jnp.where(first_core, unspun_half, half_grad).astype(jnp.bfloat16)
        grad_keyval_b = grad_keyval_b + jnp.sum(half_grad_low.astype(jnp.float32), axis=0)
        grad_keyval_w = grad_keyval_w + jnp.einsum(
            "td,tk->dk", low_first, half_grad_low, preferred_element_type=jnp.float32
        )
        query_rows = jnp.transpose(grad_queries, (1, 0, 2)) * query_scale
        grad_query_low = (
            rotate(query_rows, cos_table, -sine_table)
            .reshape(tokens_here, heads_here * HDIM)
            .astype(jnp.bfloat16)
        )
        grad_query_b = grad_query_b + jnp.sum(grad_query_low.astype(jnp.float32), axis=0)
        grad_query_w = grad_query_w + jnp.einsum(
            "td,tq->dq", low_first, grad_query_low, preferred_element_type=jnp.float32
        )
        first_part = jnp.einsum(
            "tq,dq->td", grad_query_low, w_query, preferred_element_type=jnp.float32
        ) + jnp.einsum("tk,dk->td", half_grad_low, w_keyval, preferred_element_type=jnp.float32)
        grad_first, grad_second = (
            lax.psum(first_part.astype(jnp.bfloat16), "tensor").astype(jnp.float32),
            lax.psum(second_part.astype(jnp.bfloat16), "tensor").astype(jnp.float32),
        )
        grad_n1_gain = grad_n1_gain + jnp.sum(grad_first * normed, axis=0)
        grad_n1_bias = grad_n1_bias + jnp.sum(grad_first, axis=0)
        grad_n2_gain = grad_n2_gain + jnp.sum(grad_second * normed, axis=0)
        grad_n2_bias = grad_n2_bias + jnp.sum(grad_second, axis=0)
        input_total = (
            grad_rows
            + norm_backward(grad_first, normed, scaling, norm1_gain)
            + norm_backward(grad_second, normed, scaling, norm2_gain)
        )
        input_rows.append(input_total.astype(jnp.bfloat16))
    summed_query, summed_keyval, summed_out, summed_up, summed_down = (
        lax.psum_scatter(grad_query_w, "dp", scatter_dimension=0, tiled=True),
        lax.psum_scatter(grad_keyval_w, "dp", scatter_dimension=0, tiled=True),
        lax.psum_scatter(grad_out_w, "dp", scatter_dimension=1, tiled=True),
        lax.psum_scatter(grad_up_w, "dp", scatter_dimension=0, tiled=True),
        lax.psum_scatter(grad_down_w, "dp", scatter_dimension=1, tiled=True),
    )
    vector_sums = lax.psum(
        (
            grad_n1_gain,
            grad_n1_bias,
            grad_n2_gain,
            grad_n2_bias,
            grad_row_sum,
            grad_query_b,
            grad_keyval_b,
            grad_up_b,
        ),
        "dp",
    )
    (
        sum_n1_gain,
        sum_n1_bias,
        sum_n2_gain,
        sum_n2_bias,
        sum_rows,
        sum_query_b,
        sum_keyval_b,
        sum_up_b,
    ) = vector_sums
    return (
        jnp.stack(layer_rows),
        jnp.stack(cache_rows),
        jnp.stack(input_rows),
        sum_n1_gain,
        sum_n1_bias,
        sum_n2_gain,
        sum_n2_bias,
        summed_query,
        sum_query_b,
        summed_keyval,
        sum_keyval_b,
        summed_out,
        sum_rows,
        summed_up,
        sum_up_b,
        summed_down,
        sum_rows,
    )


def nn(a, b):
    return jnp.dot(a, b, preferred_element_type=F32)


def nt(a, b):
    return lax.dot_general(a, b, (((1,), (1,)), ((), ())), preferred_element_type=F32)


def chunk_list(q_cols, kv_cols, ff_cols, pieces):
    sizes = [kv_cols, q_cols, q_cols] + [ff_cols // pieces] * (2 * pieces)
    at = 0
    out = []
    for size in sizes:
        out.append((at, size))
        at += size
    return out


def near_tiles(n, half):
    own = REACH * n
    return [(own + a, half, a, n - a, True) for a in range(0, n, half)]


def far_tiles(n, half):
    own = REACH * n
    out = [(own - j * n, n, 0, n, False) for j in range(1, REACH)]
    return out + [(a, half, 0, min(n, a + half), False) for a in range(0, n, half)]


def spin(rows, cos, sine):
    h = ROT // 2
    a, b, rest = rows[..., :h, :], rows[..., h:ROT, :], rows[..., ROT:, :]
    return jnp.concatenate([a * cos - b * sine, b * cos + a * sine, rest], axis=-2)


def fused_kernel(
    chunks, pieces,
    x, dy, positions, g1, b1, g2, b2, w_query, b_query, w_keyval, b_keyval, w_out, b_out, w_up, b_up, w_down, b_down,
    layer_out, keyval_out, input_grad, grads_out, vec_out,
    W, G, n1T, n2, n2T, dyT, wqT, qT, doT, o_nat, lse, dvec, kvwin, kvTwin, low_kv,
    cos, sine, start, m_s, l_s, acc, gbuf, dubuf, dqT, dkv, dkvT, turned, hs, hr, hx, hxr, kvo, yr, d2r,
    r1, r2, r3, vec, vp, vz, dql, dkl,
    gzs, gzr, g2s, g2r, g3s, g3r, a1s, a1r, a2s, a2r, azs, azr,
    hfs, hfr, hbs, hbr, fws, fwr, xs, xr, ts, tr, vs, vr,
):
    T, D = x.shape
    M, W_rows, KV = kvwin.shape
    n = T // M
    heads = qT.shape[0] // M
    pairs = heads // 2
    hq = heads * HDIM
    own = REACH * n
    piece = dubuf.shape[2]
    scale = HDIM ** (-0.5)
    me = lax.axis_index("dp")
    core = lax.axis_index("tensor")
    count = lax.axis_size("dp")
    z, y, xx = me // 4, (me // 2) % 2, me % 2
    shard_rows = w_query.shape[0]
    n_chunks = len(chunks)
    kKV, kQ, kO = 0, 1, 2
    kUp = [3 + 2 * c for c in range(pieces)]
    kDown = [4 + 2 * c for c in range(pieces)]
    mine = pl.ds(pl.multiple_of(core * HDIM, HDIM), HDIM)
    other = pl.ds(pl.multiple_of((1 - core) * HDIM, HDIM), HDIM)

    def at(zz, yy, xo):
        return {"dp": zz * 4 + yy * 2 + xo}

    z_ids = [at((z + d) % 4, y, xx) for d in (1, 2, 3)]
    y_id, x_id, d_id = at(z, 1 - y, xx), at(z, y, 1 - xx), at(z, 1 - y, 1 - xx)
    t_id = {"tensor": 1 - core}

    def send(src, dst, ss, rs, to):
        return pltpu.make_async_remote_copy(
            src_ref=src, dst_ref=dst, send_sem=ss, recv_sem=rs, device_id=to, device_id_type=MESH
        )

    bar = pltpu.get_barrier_semaphore()
    peers = z_ids + [y_id, x_id, d_id, t_id]
    peers += [{"dp": (me + s) % count} for s in range(1, REACH + 1)]
    peers += [{"dp": (me + count - s) % count} for s in range(1, REACH + 1)]
    for p in peers:
        pl.semaphore_signal(bar, inc=1, device_id=p, device_id_type=MESH)
    pl.semaphore_wait(bar, len(peers))

    def cols(k):
        return pl.ds(chunks[k][0], chunks[k][1])

    def halves(k):
        c0, cn = chunks[k]
        if cn < 256:
            return pl.ds(c0, cn), None
        first = cn // 256 * 128
        return pl.ds(c0, first), pl.ds(c0 + first, cn - first)

    def gather_z(k):
        r = W.at[z, y, xx, :, cols(k)]
        return [send(r, r, gzs.at[k, j], gzr.at[k, j], z_ids[j]) for j in range(3)]

    def gather_col(k):
        r = W.at[:, y, xx, :, cols(k)]
        return [send(r, r, g2s.at[k, 0], g2r.at[k, 0], x_id), send(r, r, g2s.at[k, 1], g2r.at[k, 1], y_id)]

    def gather_far(k):
        first, second = halves(k)
        r = W.at[:, y, 1 - xx, :, first]
        out = [send(r, r, g3s.at[k, 0], g3r.at[k, 0], y_id)]
        if second is not None:
            r = W.at[:, 1 - y, xx, :, second]
            out.append(send(r, r, g3s.at[k, 1], g3r.at[k, 1], x_id))
        return out

    def start1(k):
        for c in gather_z(k):
            c.start()

    def step2(k):
        for c in gather_z(k):
            c.wait_recv()
        for c in gather_col(k):
            c.start()

    def step3(k):
        for c in gather_col(k):
            c.wait_recv()
        for c in gather_far(k):
            c.start()

    def arrived(k):
        for c in gather_far(k):
            c.wait_recv()

    def weight(k):
        c0, cn = chunks[k]
        return W[:, :, :, :, c0 : c0 + cn].reshape(D, cn)

    def red1(k):
        first, second = halves(k)
        out = [send(G.at[:, :, 1 - xx, :, first], r1.at[:, :, :, first], a1s.at[k, 0], a1r.at[k, 0], x_id)]
        if second is not None:
            out.append(send(G.at[:, 1 - y, :, :, second], r1.at[:, :, :, second], a1s.at[k, 1], a1r.at[k, 1], y_id))
        return out

    def red2(k):
        first, second = halves(k)
        out = [send(r1.at[:, 1 - y, :, first], r2.at[:, :, first], a2s.at[k, 0], a2r.at[k, 0], y_id)]
        if second is not None:
            out.append(send(r1.at[:, 1 - xx, :, second], r2.at[:, :, second], a2s.at[k, 1], a2r.at[k, 1], x_id))
        return out

    def red3(k):
        return [
            send(r2.at[(z + j + 1) % 4, :, cols(k)], r3.at[j, :, cols(k)], azs.at[k, j], azr.at[k, j], z_ids[j])
            for j in range(3)
        ]

    def step_a(k):
        for c in red1(k):
            c.start()

    def step_b(k):
        first, second = halves(k)
        for c in red1(k):
            c.wait_recv()

        def add(i, _):
            zz, o = i // 2, i % 2
            r1[zz, o, :, first] = r1[zz, o, :, first] + G[zz, o, xx, :, first]
            if second is not None:
                r1[zz, o, :, second] = r1[zz, o, :, second] + G[zz, y, o, :, second]
            return 0

        lax.fori_loop(0, 8, add, 0)
        for c in red2(k):
            c.start()

    def step_c(k):
        first, second = halves(k)
        for c in red2(k):
            c.wait_recv()

        def add(i, _):
            r2[i, :, first] = r2[i, :, first] + r1[i, y, :, first]
            if second is not None:
                r2[i, :, second] = r2[i, :, second] + r1[i, xx, :, second]
            return 0

        lax.fori_loop(0, 4, add, 0)
        for c in red3(k):
            c.start()

    def step_e(k):
        for c in red3(k):
            c.wait_recv()
        total = r2[z, :, cols(k)].astype(F32)
        for j in range(3):
            total = total + r3[j, :, cols(k)].astype(F32)
        grads_out[:, cols(k)] = total

    def act(place_name):
        for move, k in SCHEDULE.get(place_name, ()):
            if move == "z":
                start1(k)
            elif move == "col":
                step2(k)
            elif move == "far":
                step3(k)
            elif move == "b":
                step_b(k)
            elif move == "c":
                step_c(k)
            elif move == "e":
                step_e(k)
            else:
                return_halo(k)

    def act_in(loop_name, i):
        for j in range(M * heads):
            if loop_name + str(j) in SCHEDULE:
                pl.when(i == j)(functools.partial(act, loop_name + str(j)))

    def place(k, block):
        c0 = chunks[k][0]
        W[z, y, xx, :, c0 : c0 + block.shape[1]] = block

    place(kKV, jnp.concatenate([w_keyval[...], jnp.zeros((shard_rows, HDIM), BF16)], axis=1))
    place(kQ, w_query[...])
    place(kO, w_out[...])
    for c in range(pieces):
        place(kUp[c], w_up[:, c * piece : (c + 1) * piece])
        place(kDown[c], w_down[:, c * piece : (c + 1) * piece])
    act("pro")

    R = 256
    vec[...] = jnp.zeros_like(vec)

    def row(ref):
        return ref[...].reshape(1, ref.shape[0])

    g1v, b1v, g2v, b2v = row(g1), row(b1), row(g2), row(b2)

    def xhat_of(rows):
        v = x[rows, :].astype(F32)
        c = v - jnp.mean(v, axis=-1, keepdims=True)
        rstd = lax.rsqrt(jnp.mean(c * c, axis=-1, keepdims=True) + epsilon)
        return v, c * rstd, rstd

    def norm_tile(i, _):
        rows = pl.ds(pl.multiple_of(i * R, R), R)
        _, xh, _ = xhat_of(rows)
        n1v = (xh * g1v + b1v).astype(BF16)
        n2v = (xh * g2v + b2v).astype(BF16)
        n2[rows, :] = n2v
        n1T[:, rows] = n1v.T
        n2T[:, rows] = n2v.T
        d = dy[rows, :]
        dyT[:, rows] = d.T
        vec[4:5, :] += jnp.sum(d.astype(F32), axis=0, keepdims=True)
        return 0

    lax.fori_loop(0, T // R, norm_tile, 0)
    act("norm")
    h = ROT // 2
    index = lax.broadcasted_iota(jnp.int32, (h, 1), 0)
    inverse = jnp.zeros((h, 1), F32)
    for i in range(h):
        inverse = jnp.where(index == i, 10000.0 ** (-(2.0 * i) / ROT), inverse)
    for m in range(M):
        ms = slice(m * n, (m + 1) * n)
        place_row = positions[m : m + 1, :]
        angle = inverse * place_row.astype(F32)
        cos[:, ms] = jnp.cos(angle)
        sine[:, ms] = jnp.sin(angle)
        start[m] = lax.broadcasted_iota(jnp.int32, (1, n), 1) + own - place_row

    def keyval_spin(rows, m, sign):
        ms = slice(m * n, (m + 1) * n)
        return spin(rows, jnp.where(core == 0, cos[:, ms], 1.0), jnp.where(core == 0, sign * sine[:, ms], 0.0))

    def column(ref):
        size = ref.shape[0]
        return jnp.broadcast_to(ref[...].reshape(1, size), (8, size)).T[:, 0:1]

    act("cos")
    arrived(kKV)
    wkvT = weight(kKV).T[0:HDIM]
    bkv = column(b_keyval)
    for m in range(M):
        ms = slice(m * n, (m + 1) * n)
        low_kv[m] = keyval_spin(nn(wkvT, n1T[:, ms]) + bkv, m, 1.0).astype(BF16)
    kvTwin[:, mine, own : own + n] = low_kv[...]

    def block(s):
        return pl.ds((REACH - s) * n, n)

    def halo(s):
        return send(
            low_kv, kvTwin.at[:, mine, block(s)], hfs.at[s - 1], hfr.at[s - 1], {"dp": (me + s) % count}
        )

    def across(s):
        part = kvTwin.at[:, mine, block(s)]
        return send(part, part, fws.at[s], fwr.at[s], t_id)

    for s in range(1, REACH + 1):
        @pl.when(me + s < count)
        def _(s=s):
            halo(s).start()
    across(0).start()

    act("kv")
    across(0).wait_recv()
    for m in range(M):
        natural = kvTwin[m, :, own : own + n].T
        kvwin[m, own : own + n, :] = natural
        keyval_out[m] = natural
    act("own")
    arrived(kQ)
    wqT[...] = weight(kQ).T
    bq = column(b_query)
    for m in range(M):
        ms = slice(m * n, (m + 1) * n)
        lin = nn(wqT[...], n1T[:, ms]) + bq
        spun = spin(lin.reshape(heads, HDIM, n), cos[:, ms], sine[:, ms]) * scale
        qT[m * heads : (m + 1) * heads] = spun.astype(BF16)
    act("q")

    near, far = near_tiles(n, n // 2), far_tiles(n, n // 2)
    tops, totals, sums = lse, dvec, dqT

    def visible(w0, kn, q0, qn, first, causal):
        key = lax.broadcasted_iota(jnp.int32, (kn, 1), 0) + w0
        seen = key >= first
        if causal:
            query = lax.broadcasted_iota(jnp.int32, (1, qn), 1) + (q0 + own)
            seen = seen & (key <= query)
        return seen

    def padded_query(i):
        return jnp.concatenate([qT[i], jnp.zeros((KV - HDIM, n), BF16)], axis=0)

    def forward_tiles(i, tiles):
        m = i // pairs
        first = start[m]
        queries = [padded_query(2 * i + t) for t in range(2)]

        def scores(t, tile):
            w0, kn, q0, qn, causal = tile
            qs = slice(q0, q0 + qn)
            sc = nn(kvwin[m, w0 : w0 + kn, :], queries[t][:, qs])
            return jnp.where(visible(w0, kn, q0, qn, first[:, qs], causal), sc, LOW)

        def take(t, tile, sc):
            w0, kn, q0, qn, _ = tile
            qs = slice(q0, q0 + qn)
            before = m_s[t, :, qs]
            top = jnp.maximum(before, jnp.max(sc, axis=0, keepdims=True))
            p = jnp.exp(sc - top)
            shrink = jnp.exp(before - top)
            l_s[t, :, qs] = l_s[t, :, qs] * shrink + jnp.sum(p, axis=0, keepdims=True)
            m_s[t, :, qs] = top
            acc[t, :, qs] = acc[t, :, qs] * shrink + nn(kvTwin[m, HDIM:KV, w0 : w0 + kn], p.astype(BF16))

        ready = [scores(t, tiles[0]) for t in range(2)]
        for at_tile, tile in enumerate(tiles):
            ahead = None
            if at_tile + 1 < len(tiles):
                ahead = [scores(t, tiles[at_tile + 1]) for t in range(2)]
            for t in range(2):
                take(t, tile, ready[t])
            ready = ahead

    def forward_near(i, _):
        m_s[...] = jnp.full_like(m_s, LOW)
        l_s[...] = jnp.zeros_like(l_s)
        acc[...] = jnp.zeros_like(acc)
        forward_tiles(i, near)
        both = pl.ds(2 * i, 2)
        tops[both], totals[both], sums[both] = m_s[...], l_s[...], acc[...]
        return 0

    def forward_far(i, _):
        m = i // pairs
        both = pl.ds(2 * i, 2)
        m_s[...], l_s[...], acc[...] = tops[both], totals[both], sums[both]
        forward_tiles(i, far)
        o = acc[...] / l_s[...]
        sums[both] = o
        lse[both] = m_s[...] + jnp.log(l_s[...])
        rows = pl.ds(pl.multiple_of(m * n, n), n)
        lanes = pl.ds(pl.multiple_of((i % pairs) * 2 * HDIM, 2 * HDIM), 2 * HDIM)
        o_nat[rows, lanes] = o.astype(BF16).reshape(2 * HDIM, n).T
        act_in("far", i)
        return 0

    def near_step(i, _):
        forward_near(i, 0)
        act_in("near", i)
        return 0

    lax.fori_loop(0, M * pairs, near_step, 0)
    for s in range(1, REACH + 1):
        @pl.when(me >= s)
        def _(s=s):
            halo(s).wait_recv()
            across(s).start()

        @pl.when(me < s)
        def _(s=s):
            kvTwin[:, :, block(s)] = jnp.zeros((M, KV, n), BF16)

    act("halow")
    for s in range(1, REACH + 1):
        @pl.when(me >= s)
        def _(s=s):
            across(s).wait_recv()

        for m in range(M):
            kvwin[m, block(s), :] = kvTwin[m, :, block(s)].T

    act("acw")
    lax.fori_loop(0, M * pairs, forward_far, 0)

    arrived(kO)
    wo = weight(kO).T
    for m in range(M):
        ms = slice(m * n, (m + 1) * n)
        doT[m * heads : (m + 1) * heads] = nn(wo, dyT[:, ms]).astype(BF16).reshape(heads, HDIM, n)

    def mix_dots(i, _):
        dvec[i] = jnp.sum(doT[i].astype(F32) * sums[i], axis=0, keepdims=True)
        return 0

    lax.fori_loop(0, M * heads, mix_dots, 0)

    def put_grad(k, leftT, right):
        c0, cn = chunks[k]

        def half(i, _):
            rows = pl.ds(pl.multiple_of(i * (D // 2), 128), D // 2)
            part = nn(leftT[rows, :], right[...]).astype(BF16)
            G[pl.ds(i * 2, 2), :, :, :, c0 : c0 + cn] = part.reshape(2, 2, 2, shard_rows, cn)
            return 0

        lax.fori_loop(0, 2, half, 0)
        step_a(k)

    put_grad(kO, dyT, o_nat)
    act("mix")

    def feed_forward(c):
        ku, kd = kUp[c], kDown[c]
        arrived(ku)
        arrived(kd)
        (u0, _), (d0, _) = chunks[ku], chunks[kd]
        up_bias = b_up[c * piece : (c + 1) * piece].reshape(1, piece)

        def rows_tile(i, _):
            rows = pl.ds(pl.multiple_of(i * R, R), R)
            u = nn(n2[rows, :], W[:, :, :, :, u0 : u0 + piece].reshape(D, piece)) + up_bias
            phi = 0.5 * (1.0 + lax.erf(u * 0.7071067811865476))
            slope = phi + u * (jnp.exp(-0.5 * u * u) * 0.3989422804014327)
            gbuf[rows, c * piece : (c + 1) * piece] = (u * phi).astype(BF16)
            dg = nn(dy[rows, :], W[:, :, :, :, d0 : d0 + piece].reshape(D, piece))
            dubuf[c, rows, :] = (slope * dg).astype(BF16)
            return 0

        lax.fori_loop(0, T // R, rows_tile, 0)
        put_grad(ku, n2T, dubuf.at[c])
        put_grad(kd, dyT, gbuf.at[:, c * piece : (c + 1) * piece])

    def branch_tile(i, _):
        rows = pl.ds(pl.multiple_of(i * R, R), R)
        total = nt(o_nat[rows, :], weight(kO))
        back = jnp.zeros((R, D), F32)
        for c in range(pieces):
            total = total + nt(gbuf[rows, c * piece : (c + 1) * piece], weight(kDown[c]))
            back = back + nt(dubuf[c, rows, :], weight(kUp[c]))
        layer_out[rows, :] = total.astype(BF16)
        input_grad[rows, :] = back.astype(BF16)
        return 0

    y_copy = send(layer_out, yr, xs.at[0], xr.at[0], t_id)
    d2_copy = send(input_grad, d2r, xs.at[1], xr.at[1], t_id)

    def branches():
        lax.fori_loop(0, T // R, branch_tile, 0)
        y_copy.start()
        d2_copy.start()
        for c in range(pieces):
            part = jnp.sum(dubuf[c].astype(F32), axis=0, keepdims=True)
            done = 0
            while done < piece:
                flat = c * piece + done
                line, col = flat // D, flat % D
                width = min(piece - done, D - col)
                vec[6 + line : 7 + line, col : col + width] = part[:, done : done + width]
                done += width

    feed_forward(0)
    act("ffn0")

    dkv[...] = jnp.zeros_like(dkv)

    def backward_tiles(i, tiles):
        m = i // heads
        zero = jnp.zeros((HDIM, n), BF16)
        query = jnp.concatenate([qT[i], zero], axis=0)
        cotangent = jnp.concatenate([zero, doT[i]], axis=0)
        natural = jnp.concatenate([qT[i], doT[i]], axis=0).T
        first, ls, dots = start[m], lse[i], dvec[i]
        step = n // 2
        pieces_of = [(w0 + a, step, q0, qn, c) for w0, kn, q0, qn, c in tiles for a in range(0, kn, step)]

        def products(tile):
            w0, kn, q0, qn, causal = tile
            qs = slice(q0, q0 + qn)
            rows = kvwin[m, w0 : w0 + kn, :]
            sc = nn(rows, query[:, qs])
            sc = jnp.where(visible(w0, kn, q0, qn, first[:, qs], causal), sc, LOW)
            return sc, nn(rows, cotangent[:, qs])

        ready = products(pieces_of[0])
        for at_tile, tile in enumerate(pieces_of):
            ahead = products(pieces_of[at_tile + 1]) if at_tile + 1 < len(pieces_of) else None
            w0, kn, q0, qn, _ = tile
            qs = slice(q0, q0 + qn)
            sc, dp = ready
            p = jnp.exp(sc - ls[:, qs])
            ds = (p * (dp - dots[:, qs])).astype(BF16)
            for_k = nn(ds, natural[qs])
            for_v = nn(p.astype(BF16), natural[qs])
            lane = lax.broadcasted_iota(jnp.int32, for_k.shape, 1)
            dkv[m, w0 : w0 + kn, :] += jnp.where(lane < HDIM, for_k, for_v)
            dqT[i, :, qs] += nn(kvTwin[m, 0:HDIM, w0 : w0 + kn], ds)
            ready = ahead

    def backward_far(i, _):
        @pl.when(i == FEED_AT[0])
        def _():
            feed_forward(1)
            act("ffn1")

        @pl.when(i == FEED_AT[1])
        def _():
            feed_forward(2)
            branches()
            act("ffn2")

        dqT[i] = jnp.zeros((HDIM, n), F32)
        backward_tiles(i, far)
        for m in range(M):
            pl.when(i == (m + 1) * heads - 1)(functools.partial(give_half, m))
        act_in("bfar", i)
        return 0

    def backward_near(i, _):
        backward_tiles(i, near)
        for m in range(M):
            pl.when(i == (m + 1) * heads - 1)(functools.partial(give_own, m))
        act_in("bnear", i)
        return 0

    def back_copy(s, m):
        return send(
            hs.at[s - 1, m], hr.at[s - 1, m], hbs.at[s - 1, m], hbr.at[s - 1, m],
            {"dp": (me + count - s) % count},
        )

    def half_copy(m):
        part = pl.ds(0, own)
        return send(hx.at[m, :, part], hxr.at[m, :, part], xs.at[2 + m], xr.at[2 + m], t_id)

    def own_copy(m):
        part = pl.ds(own, n)
        return send(hx.at[m, :, part], hxr.at[m, :, part], xs.at[2 + M + m], xr.at[2 + M + m], t_id)

    def split(m, j):
        js = slice(j * n, (j + 1) * n)
        turned[...] = dkv[m, js, :].T
        dkvT[m, :, js] = turned[mine, :]
        hx[m, :, js] = turned[other, :].astype(BF16)

    def give_half(m):
        for j in range(REACH):
            split(m, j)
        half_copy(m).start()

    def return_halo(m):
        half_copy(m).wait_recv()
        for j in range(REACH):
            js = slice(j * n, (j + 1) * n)
            hs[REACH - j - 1, m] = (dkvT[m, :, js] + hxr[m, :, js].astype(F32)).astype(BF16)
        for s in range(1, REACH + 1):
            @pl.when(me >= s)
            def _(s=s):
                back_copy(s, m).start()

    def give_own(m):
        split(m, REACH)
        own_copy(m).start()

    lax.fori_loop(0, M * heads, backward_far, 0)
    lax.fori_loop(0, M * heads, backward_near, 0)

    for m in range(M):
        ms = slice(m * n, (m + 1) * n)
        rows = dqT[m * heads : (m + 1) * heads] * scale
        low = spin(rows, cos[:, ms], -sine[:, ms]).astype(BF16)
        dql[ms, :] = low.reshape(hq, n).T
    put_grad(kQ, n1T, dql)
    vec[5:6, 0:hq] = jnp.sum(dql[...].astype(F32), axis=0, keepdims=True)
    act("t0")

    for m in range(M):
        ms = slice(m * n, (m + 1) * n)
        own_copy(m).wait_recv()
        dko = dkvT[m, :, own : own + n] + hxr[m, :, own : own + n].astype(F32)
        kvo[...] = dko
        for s in range(1, REACH + 1):
            @pl.when(me + s < count)
            def _(s=s, m=m):
                back_copy(s, m).wait_recv()
                kvo[...] += hr[s - 1, m].astype(F32)
        low = keyval_spin(kvo[...], m, -1.0).astype(BF16)
        dkl[ms, :] = jnp.concatenate([low, jnp.zeros((KV - HDIM, n), BF16)], axis=0).T
    put_grad(kKV, n1T, dkl)
    vec[5:6, hq : hq + KV] = jnp.sum(dkl[...].astype(F32), axis=0, keepdims=True)
    act("t1")

    def d1_copy(i):
        rows = pl.ds(pl.multiple_of(i * R, R), R)
        return send(gbuf.at[rows, pl.ds(0, D)], n2.at[rows], ts.at[i], tr.at[i], t_id)

    def first_tile(i, _):
        rows = pl.ds(pl.multiple_of(i * R, R), R)
        gbuf[rows, 0:D] = (nt(dql[rows, :], weight(kQ)) + nt(dkl[rows, :], weight(kKV))).astype(BF16)
        d1_copy(i).start()
        return 0

    lax.fori_loop(0, T // R, first_tile, 0)
    act("t2")

    y_copy.wait()
    both_bias = row(b_out) + row(b_down)

    def out_tile(i, _):
        rows = pl.ds(pl.multiple_of(i * R, R), R)
        both = (layer_out[rows, :].astype(F32) + yr[rows, :].astype(F32)) + both_bias
        layer_out[rows, :] = (x[rows, :].astype(F32) + both).astype(BF16)
        return 0

    lax.fori_loop(0, T // R, out_tile, 0)
    act("t3")
    d2_copy.wait()

    def last_tile(i, _):
        rows = pl.ds(pl.multiple_of(i * R, R), R)
        _, xh, rstd = xhat_of(rows)
        d1_copy(i).wait_recv()
        dn1 = gbuf[rows, 0:D].astype(F32) + n2[rows, :].astype(F32)
        dn2 = input_grad[rows, :].astype(F32) + d2r[rows, :].astype(F32)
        vec[0:1, :] += jnp.sum(dn1 * xh, axis=0, keepdims=True)
        vec[1:2, :] += jnp.sum(dn1, axis=0, keepdims=True)
        vec[2:3, :] += jnp.sum(dn2 * xh, axis=0, keepdims=True)
        vec[3:4, :] += jnp.sum(dn2, axis=0, keepdims=True)
        a = dn1 * g1v + dn2 * g2v
        back = a - jnp.mean(a, axis=-1, keepdims=True) - xh * jnp.mean(a * xh, axis=-1, keepdims=True)
        input_grad[rows, :] = (dy[rows, :].astype(F32) + rstd * back).astype(BF16)
        return 0

    lax.fori_loop(0, T // R, last_tile, 0)

    flat = y * 2 + xx
    vp[flat] = vec[...]
    plane = [send(vp.at[flat], vp.at[flat], vs.at[j], vr.at[j], to) for j, to in enumerate((x_id, y_id, d_id))]
    for c in plane:
        c.start()
    act("t4")
    for c in plane:
        c.wait_recv()
    vz[z] = (vp[0] + vp[1]) + (vp[2] + vp[3])
    along = [send(vz.at[z], vz.at[z], vs.at[3 + j], vr.at[3 + j], z_ids[j]) for j in range(3)]
    for c in along:
        c.start()
    act("t5")
    for c in along:
        c.wait_recv()
    act("t6")
    vec_out[...] = (vz[0] + vz[1]) + (vz[2] + vz[3])

    for k in range(n_chunks):
        for c in gather_z(k) + gather_col(k) + gather_far(k) + red1(k) + red2(k) + red3(k):
            c.wait_send()
    across(0).wait_send()
    for s in range(1, REACH + 1):
        @pl.when(me + s < count)
        def _(s=s):
            halo(s).wait_send()

        @pl.when(me >= s)
        def _(s=s):
            across(s).wait_send()
            for m in range(M):
                back_copy(s, m).wait_send()
    for m in range(M):
        half_copy(m).wait_send()
        own_copy(m).wait_send()
    for i in range(T // R):
        d1_copy(i).wait_send()
    for c in plane + along:
        c.wait_send()


def finish_kernel(
    chunks, pieces, grads, vec, n1g, n1b, n2g, n2b, wq, bq, wkv, bkv, wo, bo, wu, bu, wd, bd
):
    hq, half, piece, D = wq.shape[1], wkv.shape[1], chunks[3][1], vec.shape[1]
    for out, r in ((n1g, 0), (n1b, 1), (n2g, 2), (n2b, 3), (bo, 4), (bd, 4)):
        out[...] = vec[r].reshape(D)
    q0, o0 = chunks[1][0], chunks[2][0]
    wq[...] = grads[:, q0 : q0 + hq]
    wkv[...] = grads[:, 0:half]
    wo[...] = grads[:, o0 : o0 + hq]
    for c in range(pieces):
        u0, d0 = chunks[3 + 2 * c][0], chunks[4 + 2 * c][0]
        wu[:, c * piece : (c + 1) * piece] = grads[:, u0 : u0 + piece]
        wd[:, c * piece : (c + 1) * piece] = grads[:, d0 : d0 + piece]
    bq[...] = vec[5:6, 0:hq].reshape(hq)
    bkv[...] = vec[5:6, hq : hq + half].reshape(half)
    for r in range(bu.shape[0] // D):
        bu[r * D : (r + 1) * D] = vec[6 + r].reshape(D)


def fused_layer(arguments, pieces):
    (hidden_in, positions, out_grad, g1, b1, g2, b2, w_query, b_query, w_keyval, b_keyval,
     w_out, b_out, w_up, b_up, w_down, b_down) = arguments
    M, n, D = hidden_in.shape
    T = M * n
    hq, F, half, rows = b_query.shape[0], b_up.shape[0], b_keyval.shape[0], w_query.shape[0]
    heads, KV, piece = hq // HDIM, 2 * half, F // pieces
    chunks = chunk_list(hq, KV, F, pieces)
    C = chunks[-1][0] + chunks[-1][1]
    k = len(chunks)
    Wn = (REACH + 1) * n
    V = pltpu.VMEM
    S = pltpu.SemaphoreType.DMA
    sds = jax.ShapeDtypeStruct
    vm = pl.BlockSpec(memory_space=pltpu.VMEM)
    mh = M * heads
    scratch = [
        V((4, 2, 2, rows, C), BF16), V((4, 2, 2, rows, C), BF16),
        V((D, T), BF16), V((T, D), BF16), V((D, T), BF16), V((D, T), BF16),
        V((hq, D), BF16), V((mh, HDIM, n), BF16), V((mh, HDIM, n), BF16),
        V((T, hq), BF16), V((mh, 1, n), F32), V((mh, 1, n), F32),
        V((M, Wn, KV), BF16), V((M, KV, Wn), BF16), V((M, HDIM, n), BF16),
        V((ROT // 2, T), F32), V((ROT // 2, T), F32), V((M, 1, n), jnp.int32),
        V((2, 1, n), F32), V((2, 1, n), F32), V((2, HDIM, n), F32),
        V((T, F), BF16), V((pieces, T, piece), BF16),
        V((mh, HDIM, n), F32), V((M, Wn, KV), F32), V((M, HDIM, Wn), F32), V((KV, n), F32),
        V((REACH, M, HDIM, n), BF16), V((REACH, M, HDIM, n), BF16),
        V((M, HDIM, Wn), BF16), V((M, HDIM, Wn), BF16), V((HDIM, n), F32),
        V((T, D), BF16), V((T, D), BF16),
        V((4, 2, rows, C), BF16), V((4, rows, C), BF16), V((3, rows, C), BF16),
        V((8, D), F32), V((4, 8, D), F32), V((4, 8, D), F32),
        V((T, hq), BF16), V((T, KV), BF16),
        S((k, 3)), S((k, 3)), S((k, 2)), S((k, 2)), S((k, 2)), S((k, 2)),
        S((k, 2)), S((k, 2)), S((k, 2)), S((k, 2)), S((k, 3)), S((k, 3)),
        S((REACH,)), S((REACH,)), S((REACH, M)), S((REACH, M)), S((REACH + 1,)), S((REACH + 1,)),
        S((2 + 2 * M,)), S((2 + 2 * M,)), S((T // 256,)), S((T // 256,)), S((6,)), S((6,)),
    ]
    y_out, kv_out, x_out, grads, vec = pl.pallas_call(
        functools.partial(fused_kernel, chunks, pieces),
        out_shape=(
            sds((T, D), BF16), sds((M, n, KV), BF16), sds((T, D), BF16), sds((rows, C), F32), sds((8, D), F32),
        ),
        in_specs=[vm] * 17,
        out_specs=(vm,) * 5,
        scratch_shapes=scratch,
        compiler_params=pltpu.CompilerParams(
            collective_id=0, has_side_effects=True, vmem_limit_bytes=62 << 20
        ),
        name="fused_layer",
    )(hidden_in.reshape(T, D), out_grad.reshape(T, D), positions, g1, b1, g2, b2, w_query, b_query,
      w_keyval, b_keyval, w_out.T, b_out, w_up, b_up, w_down.T, b_down)
    vector = sds((D,), F32)
    out_shape = (
        vector, vector, vector, vector,
        sds(w_query.shape, F32), sds(b_query.shape, F32), sds(w_keyval.shape, F32), sds(b_keyval.shape, F32),
        sds(w_out.shape[::-1], F32), vector, sds(w_up.shape, F32), sds(b_up.shape, F32), sds(w_down.shape[::-1], F32), vector,
    )
    outs = pl.pallas_call(
        functools.partial(finish_kernel, chunks, pieces),
        out_shape=out_shape,
        in_specs=[vm] * 2,
        out_specs=(vm,) * 14,
        compiler_params=pltpu.CompilerParams(vmem_limit_bytes=60 << 20),
        name="finish_layer",
    )(grads, vec)
    outs = [y_out.reshape(hidden_in.shape), kv_out, x_out.reshape(hidden_in.shape)] + list(outs)
    outs[11], outs[15] = outs[11].T, outs[15].T
    return tuple(outs)


PIECES = 3


def fits_fused(hidden_in, query_weight, up_weight):
    rows, hq = query_weight.shape
    return (
        lax.axis_size("dp") == 16
        and rows % 16 == 0
        and hq % 384 == 0
        and up_weight.shape[1] % (PIECES * 256) == 0
        and up_weight.shape[1] >= hidden_in.shape[2]
        and hidden_in.shape[1] % 256 == 0
    )


def on_device(*arguments):
    if fits_fused(arguments[0], arguments[7], arguments[13]):
        return fused_layer(arguments, PIECES)
    return plain_layer(*arguments)


def solution(mesh):
    return jax.shard_map(
        on_device,
        mesh=mesh,
        in_specs=(
            P(None, "dp", None),
            P(None, "dp"),
            P(None, "dp", None),
            P(),
            P(),
            P(),
            P(),
            P("dp", "tensor"),
            P("tensor"),
            P("dp", "tensor"),
            P("tensor"),
            P("tensor", "dp"),
            P(),
            P("dp", "tensor"),
            P("tensor"),
            P("tensor", "dp"),
            P(),
        ),
        out_specs=(
            P(None, "dp", None),
            P(None, "dp", None),
            P(None, "dp", None),
            P(),
            P(),
            P(),
            P(),
            P("dp", "tensor"),
            P("tensor"),
            P("dp", "tensor"),
            P("tensor"),
            P("tensor", "dp"),
            P(),
            P("dp", "tensor"),
            P("tensor"),
            P("tensor", "dp"),
            P(),
        ),
        check_vma=False,
    )
```

```python
import functools
import jax
import jax.numpy as jnp
from jax import lax
from jax.experimental import pallas as pl
from jax.experimental.pallas import tpu as pltpu
from jax.sharding import PartitionSpec as P

HDIM = 64
ROT = 16
REACH = 4
epsilon = 1e-05
MESH = pl.DeviceIdType.MESH
LOW = -1e30
F32 = jnp.float32
BF16 = jnp.bfloat16


SCHEDULE = {
    "pro": (("z", 0), ("z", 1), ("col", 0), ("z", 3),),
    "norm": (("far", 0),),
    "cos": (("col", 1), ("z", 2),),
    "kv": (("far", 1),),
    "q": (("col", 3),),
    "near0": (("z", 4),),
    "near5": (("z", 5), ("col", 2),),
    "halow": (("col", 4),),
    "acw": (("z", 7),),
    "far0": (("z", 6), ("far", 4), ("far", 3),),
    "far1": (("z", 8), ("col", 5),),
    "far2": (("col", 7), ("col", 6),),
    "far3": (("far", 2),),
    "far4": (("col", 8),),
    "far5": (("far", 5),),
    "bfar1": (("far", 6),),
    "bfar2": (("b", 3), ("b", 4),),
    "bfar3": (("far", 7), ("b", 2),),
    "ffn1": (("c", 3), ("c", 4), ("c", 2),),
    "bfar5": (("far", 8),),
    "bfar6": (("b", 6), ("b", 5), ("ret", 0),),
    "ffn2": (("c", 5), ("c", 6),),
    "bfar7": (("e", 4),),
    "bfar8": (("b", 7),),
    "bfar9": (("b", 8), ("e", 2),),
    "bfar10": (("c", 7), ("c", 8),),
    "bnear1": (("e", 6),),
    "bnear4": (("ret", 1),),
    "bnear6": (("e", 7),),
    "bnear8": (("e", 3),),
    "bnear11": (("e", 8),),
    "t0": (("e", 5),),
    "t3": (("b", 0), ("b", 1),),
    "t4": (("c", 0), ("c", 1), ("e", 0),),
    "t5": (("e", 1),),
}
FEED_AT = (4, 7)


def shifted(value, axis, steps):
    count = lax.axis_size(axis)
    initial, last = (max(0, -steps), min(count, count - steps))
    return lax.ppermute(value, axis, [(source, source + steps) for source in range(initial, last)])


def norm_forward(stream):
    average = jnp.mean(stream, axis=-1, keepdims=True)
    centered = stream - average
    spread = jnp.mean(centered * centered, axis=-1, keepdims=True)
    scaling = lax.rsqrt(spread + epsilon)
    normed = centered * scaling
    return (normed, scaling)


def norm_backward(upstream, normed, scaling, norm_gain):
    weighted = upstream * norm_gain
    return scaling * (
        weighted
        - jnp.mean(weighted, axis=-1, keepdims=True)
        - normed * jnp.mean(weighted * normed, axis=-1, keepdims=True)
    )


def rotary_tables(places):
    inverse = 10000.0 ** (-(jnp.arange(ROT // 2, dtype=jnp.float32) * 2.0) / ROT)
    angles = places.astype(jnp.float32)[:, None] * inverse[None, :]
    angles = jnp.concatenate([angles, angles], axis=-1)
    return (jnp.cos(angles), jnp.sin(angles))


def rotate(values, cos_table, sine_table):
    head_part = values[..., :ROT]
    first_half = head_part[..., : ROT // 2]
    second_half = head_part[..., ROT // 2 :]
    turned = jnp.concatenate([-second_half, first_half], axis=-1)
    spun_part = head_part * cos_table[:, None, :] + turned * sine_table[:, None, :]
    return jnp.concatenate([spun_part, values[..., ROT:]], axis=-1)


def gelu_exact(values):
    return jax.nn.gelu(values, approximate=False)


def fetch_weights(shard_weights):
    return (
        lax.all_gather(shard_weights[0], "dp", axis=0, tiled=True),
        lax.all_gather(shard_weights[1], "dp", axis=0, tiled=True),
        lax.all_gather(shard_weights[2], "dp", axis=1, tiled=True),
        lax.all_gather(shard_weights[3], "dp", axis=0, tiled=True),
        lax.all_gather(shard_weights[4], "dp", axis=1, tiled=True),
    )


def score_block(queries, key_rows, places, reach_step):
    tokens_here = queries.shape[1]
    scores = jnp.einsum("htd,kd->htk", queries, key_rows, preferred_element_type=jnp.float32)
    row_ids = jnp.arange(tokens_here, dtype=jnp.int32)
    offsets = reach_step * tokens_here + row_ids[:, None] - row_ids[None, :]
    visible = (offsets >= 0) & (offsets <= places[:, None])
    return (scores, visible[None])


def attend_forward(queries, blocks, places):
    heads_here, tokens_here = (queries.shape[0], queries.shape[1])
    top_score = jnp.full((heads_here, tokens_here), -1e30, jnp.float32)
    totals = jnp.zeros((heads_here, tokens_here), jnp.float32)
    for reach_step, kv_block in enumerate(blocks):
        scores, visible = score_block(queries, kv_block[:, :HDIM], places, reach_step)
        masked = jnp.where(visible, scores, -1e30)
        new_top = jnp.maximum(top_score, jnp.max(masked, axis=-1))
        totals = totals * jnp.exp(top_score - new_top) + jnp.sum(
            jnp.where(visible, jnp.exp(masked - new_top[..., None]), 0.0), axis=-1
        )
        top_score = new_top
    log_sum = top_score + jnp.log(totals)
    mixture = jnp.zeros((heads_here, tokens_here, HDIM), jnp.float32)
    for reach_step, kv_block in enumerate(blocks):
        scores, visible = score_block(queries, kv_block[:, :HDIM], places, reach_step)
        weights_low = jnp.where(visible, jnp.exp(scores - log_sum[..., None]), 0.0).astype(
            jnp.bfloat16
        )
        mixture = mixture + jnp.einsum(
            "htk,kd->htd", weights_low, kv_block[:, HDIM:], preferred_element_type=jnp.float32
        )
    return (mixture, log_sum)


def attend_backward(queries, blocks, places, log_sum, grad_mixture, row_dots):
    grad_queries = jnp.zeros(queries.shape, jnp.float32)
    key_terms = []
    for reach_step, kv_block in enumerate(blocks):
        key_rows = kv_block[:, :HDIM]
        value_rows = kv_block[:, HDIM:]
        scores, visible = score_block(queries, key_rows, places, reach_step)
        weights_full = jnp.where(visible, jnp.exp(scores - log_sum[..., None]), 0.0)
        weights_low = weights_full.astype(jnp.bfloat16)
        grad_weights = jnp.einsum(
            "htd,kd->htk", grad_mixture, value_rows, preferred_element_type=jnp.float32
        )
        grad_scores = (weights_full * (grad_weights - row_dots[..., None])).astype(jnp.bfloat16)
        grad_queries = grad_queries + jnp.einsum(
            "htk,kd->htd", grad_scores, key_rows, preferred_element_type=jnp.float32
        )
        grad_keys = jnp.einsum(
            "htk,htd->kd", grad_scores, queries, preferred_element_type=jnp.float32
        )
        grad_values = jnp.einsum(
            "htk,htd->kd", weights_low, grad_mixture, preferred_element_type=jnp.float32
        )
        key_terms.append(jnp.concatenate([grad_keys, grad_values], axis=-1))
    return (grad_queries, key_terms)


def plain_layer(
    hidden_in,
    positions,
    out_grad,
    norm1_gain,
    norm1_bias,
    norm2_gain,
    norm2_bias,
    query_weight,
    query_bias,
    keyval_weight,
    keyval_bias,
    attn_out_weight,
    attn_out_bias,
    up_weight,
    up_bias,
    down_weight,
    down_bias,
):
    micro_count = hidden_in.shape[0]
    tokens_here = hidden_in.shape[1]
    width = hidden_in.shape[2]
    dp_count = lax.axis_size("dp")
    first_core = lax.axis_index("tensor") == 0
    heads_here = query_bias.shape[0] // HDIM
    query_scale = HDIM ** (-0.5)
    shard_weights = (query_weight, keyval_weight, attn_out_weight, up_weight, down_weight)
    gathered = None
    grad_query_w = jnp.zeros((width, query_weight.shape[1]), jnp.float32)
    grad_keyval_w = jnp.zeros((width, keyval_weight.shape[1]), jnp.float32)
    grad_out_w = jnp.zeros(
        (attn_out_weight.shape[0], attn_out_weight.shape[1] * dp_count), jnp.float32
    )
    grad_up_w = jnp.zeros((width, up_weight.shape[1]), jnp.float32)
    grad_down_w = jnp.zeros((down_weight.shape[0], down_weight.shape[1] * dp_count), jnp.float32)
    grad_n1_gain = jnp.zeros((width,), jnp.float32)
    grad_n1_bias = jnp.zeros((width,), jnp.float32)
    grad_n2_gain = jnp.zeros((width,), jnp.float32)
    grad_n2_bias = jnp.zeros((width,), jnp.float32)
    grad_row_sum = jnp.zeros((width,), jnp.float32)
    grad_query_b = jnp.zeros(query_bias.shape, jnp.float32)
    grad_keyval_b = jnp.zeros(keyval_bias.shape, jnp.float32)
    grad_up_b = jnp.zeros(up_bias.shape, jnp.float32)
    layer_rows = []
    cache_rows = []
    input_rows = []
    for micro_step in range(micro_count):
        gathered = fetch_weights(shard_weights)
        w_query, w_keyval, w_out, w_up, w_down = gathered
        stream = hidden_in[micro_step].astype(jnp.float32)
        places = positions[micro_step]
        normed, scaling = norm_forward(stream)
        low_first = (normed * norm1_gain + norm1_bias).astype(jnp.bfloat16)
        low_second = (normed * norm2_gain + norm2_bias).astype(jnp.bfloat16)
        cos_table, sine_table = rotary_tables(places)
        query_lin = jnp.dot(low_first, w_query, preferred_element_type=jnp.float32) + query_bias
        queries = (
            rotate(query_lin.reshape(tokens_here, heads_here, HDIM), cos_table, sine_table)
            * query_scale
        ).astype(jnp.bfloat16)
        query_heads = jnp.transpose(queries, (1, 0, 2))
        half_lin = jnp.dot(low_first, w_keyval, preferred_element_type=jnp.float32) + keyval_bias
        spun_half = rotate(half_lin[:, None, :], cos_table, sine_table)[:, 0, :]
        half_low = jnp.where(first_core, spun_half, half_lin).astype(jnp.bfloat16)
        keyval = lax.all_gather(half_low, "tensor", axis=1, tiled=True)
        blocks = [keyval] + [
            shifted(keyval, "dp", reach_step) for reach_step in range(1, REACH + 1)
        ]
        mixture, log_sum = attend_forward(query_heads, blocks, places)
        mixture_low = (
            jnp.transpose(mixture, (1, 0, 2))
            .reshape(tokens_here, heads_here * HDIM)
            .astype(jnp.bfloat16)
        )
        up_lin = jnp.dot(low_second, w_up, preferred_element_type=jnp.float32) + up_bias
        active_low = gelu_exact(up_lin).astype(jnp.bfloat16)
        branch_part = jnp.dot(mixture_low, w_out, preferred_element_type=jnp.float32) + jnp.dot(
            active_low, w_down, preferred_element_type=jnp.float32
        )
        branches = lax.psum(branch_part.astype(jnp.bfloat16), "tensor").astype(jnp.float32)
        layer_rows.append((stream + branches + attn_out_bias + down_bias).astype(jnp.bfloat16))
        cache_rows.append(keyval)
        grad_low = out_grad[micro_step]
        grad_rows = grad_low.astype(jnp.float32)
        grad_row_sum = grad_row_sum + jnp.sum(grad_rows, axis=0)
        grad_out_w = grad_out_w + jnp.einsum(
            "th,td->hd", mixture_low, grad_low, preferred_element_type=jnp.float32
        )
        grad_down_w = grad_down_w + jnp.einsum(
            "tf,td->fd", active_low, grad_low, preferred_element_type=jnp.float32
        )
        grad_active = jnp.einsum("td,fd->tf", grad_low, w_down, preferred_element_type=jnp.float32)
        gelu_values, gelu_pull = jax.vjp(gelu_exact, up_lin)
        grad_up_low = gelu_pull(grad_active)[0].astype(jnp.bfloat16)
        grad_up_b = grad_up_b + jnp.sum(grad_up_low.astype(jnp.float32), axis=0)
        grad_up_w = grad_up_w + jnp.einsum(
            "td,tf->df", low_second, grad_up_low, preferred_element_type=jnp.float32
        )
        second_part = jnp.einsum("tf,df->td", grad_up_low, w_up, preferred_element_type=jnp.float32)
        grad_mix_low = jnp.einsum(
            "td,hd->th", grad_low, w_out, preferred_element_type=jnp.float32
        ).astype(jnp.bfloat16)
        grad_mixture = jnp.transpose(grad_mix_low.reshape(tokens_here, heads_here, HDIM), (1, 0, 2))
        row_dots = jnp.sum(grad_mixture.astype(jnp.float32) * mixture, axis=-1)
        grad_queries, key_terms = attend_backward(
            query_heads, blocks, places, log_sum, grad_mixture, row_dots
        )
        keyval_grad = key_terms[0]
        for reach_step in range(1, REACH + 1):
            keyval_grad = keyval_grad + shifted(
                key_terms[reach_step].astype(jnp.bfloat16), "dp", -reach_step
            ).astype(jnp.float32)
        half_grad = lax.psum_scatter(
            keyval_grad.astype(jnp.bfloat16), "tensor", scatter_dimension=1, tiled=True
        ).astype(jnp.float32)
        unspun_half = rotate(half_grad[:, None, :], cos_table, -sine_table)[:, 0, :]
        half_grad_low = jnp.where(first_core, unspun_half, half_grad).astype(jnp.bfloat16)
        grad_keyval_b = grad_keyval_b + jnp.sum(half_grad_low.astype(jnp.float32), axis=0)
        grad_keyval_w = grad_keyval_w + jnp.einsum(
            "td,tk->dk", low_first, half_grad_low, preferred_element_type=jnp.float32
        )
        query_rows = jnp.transpose(grad_queries, (1, 0, 2)) * query_scale
        grad_query_low = (
            rotate(query_rows, cos_table, -sine_table)
            .reshape(tokens_here, heads_here * HDIM)
            .astype(jnp.bfloat16)
        )
        grad_query_b = grad_query_b + jnp.sum(grad_query_low.astype(jnp.float32), axis=0)
        grad_query_w = grad_query_w + jnp.einsum(
            "td,tq->dq", low_first, grad_query_low, preferred_element_type=jnp.float32
        )
        first_part = jnp.einsum(
            "tq,dq->td", grad_query_low, w_query, preferred_element_type=jnp.float32
        ) + jnp.einsum("tk,dk->td", half_grad_low, w_keyval, preferred_element_type=jnp.float32)
        grad_first, grad_second = (
            lax.psum(first_part.astype(jnp.bfloat16), "tensor").astype(jnp.float32),
            lax.psum(second_part.astype(jnp.bfloat16), "tensor").astype(jnp.float32),
        )
        grad_n1_gain = grad_n1_gain + jnp.sum(grad_first * normed, axis=0)
        grad_n1_bias = grad_n1_bias + jnp.sum(grad_first, axis=0)
        grad_n2_gain = grad_n2_gain + jnp.sum(grad_second * normed, axis=0)
        grad_n2_bias = grad_n2_bias + jnp.sum(grad_second, axis=0)
        input_total = (
            grad_rows
            + norm_backward(grad_first, normed, scaling, norm1_gain)
            + norm_backward(grad_second, normed, scaling, norm2_gain)
        )
        input_rows.append(input_total.astype(jnp.bfloat16))
    summed_query, summed_keyval, summed_out, summed_up, summed_down = (
        lax.psum_scatter(grad_query_w, "dp", scatter_dimension=0, tiled=True),
        lax.psum_scatter(grad_keyval_w, "dp", scatter_dimension=0, tiled=True),
        lax.psum_scatter(grad_out_w, "dp", scatter_dimension=1, tiled=True),
        lax.psum_scatter(grad_up_w, "dp", scatter_dimension=0, tiled=True),
        lax.psum_scatter(grad_down_w, "dp", scatter_dimension=1, tiled=True),
    )
    vector_sums = lax.psum(
        (
            grad_n1_gain,
            grad_n1_bias,
            grad_n2_gain,
            grad_n2_bias,
            grad_row_sum,
            grad_query_b,
            grad_keyval_b,
            grad_up_b,
        ),
        "dp",
    )
    (
        sum_n1_gain,
        sum_n1_bias,
        sum_n2_gain,
        sum_n2_bias,
        sum_rows,
        sum_query_b,
        sum_keyval_b,
        sum_up_b,
    ) = vector_sums
    return (
        jnp.stack(layer_rows),
        jnp.stack(cache_rows),
        jnp.stack(input_rows),
        sum_n1_gain,
        sum_n1_bias,
        sum_n2_gain,
        sum_n2_bias,
        summed_query,
        sum_query_b,
        summed_keyval,
        sum_keyval_b,
        summed_out,
        sum_rows,
        summed_up,
        sum_up_b,
        summed_down,
        sum_rows,
    )


def nn(a, b):
    return jnp.dot(a, b, preferred_element_type=F32)


def nt(a, b):
    return lax.dot_general(a, b, (((1,), (1,)), ((), ())), preferred_element_type=F32)


def chunk_list(q_cols, kv_cols, ff_cols, pieces):
    sizes = [kv_cols, q_cols, q_cols] + [ff_cols // pieces] * (2 * pieces)
    at = 0
    out = []
    for size in sizes:
        out.append((at, size))
        at += size
    return out


def near_tiles(n, half):
    own = REACH * n
    return [(own + a, half, a, n - a, True) for a in range(0, n, half)]


def far_tiles(n, half):
    own = REACH * n
    out = [(own - j * n, n, 0, n, False) for j in range(1, REACH)]
    return out + [(a, half, 0, min(n, a + half), False) for a in range(0, n, half)]


def spin(rows, cos, sine):
    h = ROT // 2
    a, b, rest = rows[..., :h, :], rows[..., h:ROT, :], rows[..., ROT:, :]
    return jnp.concatenate([a * cos - b * sine, b * cos + a * sine, rest], axis=-2)


def fused_kernel(
    chunks, pieces,
    x_in, dy_in, positions, g1, b1, g2, b2, w_query, b_query, w_keyval, b_keyval, w_out, b_out, w_up, b_up, w_down, b_down,
    layer_hbm, keyval_hbm, grad_hbm, grads_out, vec_out,
    x, dy, layer_out, keyval_out, input_grad, in_sem, out_sem,
    W, G, n1T, n2, n2T, dyT, wqT, qT, doT, o_nat, lse, dvec, kvwin, kvTwin, low_kv,
    cos, sine, start, m_s, l_s, acc, gbuf, dubuf, dqT, dkv, dkvT, turned, hs, hr, hx, hxr, kvo, yr, d2r,
    r1, r2, r3, vec, vp, vz, dql, dkl,
    gzs, gzr, g2s, g2r, g3s, g3r, a1s, a1r, a2s, a2r, azs, azr,
    hfs, hfr, hbs, hbr, fws, fwr, xs, xr, ts, tr, vs, vr,
):
    T, D = x.shape
    M, W_rows, KV = kvwin.shape
    n = T // M
    heads = qT.shape[0] // M
    pairs = heads // 2
    hq = heads * HDIM
    own = REACH * n
    piece = dubuf.shape[2]
    scale = HDIM ** (-0.5)
    me = lax.axis_index("dp")
    core = lax.axis_index("tensor")
    count = lax.axis_size("dp")
    z, y, xx = me // 4, (me // 2) % 2, me % 2
    shard_rows = w_query.shape[0]
    n_chunks = len(chunks)
    kKV, kQ, kO = 0, 1, 2
    kUp = [3 + 2 * c for c in range(pieces)]
    kDown = [4 + 2 * c for c in range(pieces)]
    mine = pl.ds(pl.multiple_of(core * HDIM, HDIM), HDIM)
    other = pl.ds(pl.multiple_of((1 - core) * HDIM, HDIM), HDIM)

    def at(zz, yy, xo):
        return {"dp": zz * 4 + yy * 2 + xo}

    z_ids = [at((z + d) % 4, y, xx) for d in (1, 2, 3)]
    y_id, x_id, d_id = at(z, 1 - y, xx), at(z, y, 1 - xx), at(z, 1 - y, 1 - xx)
    t_id = {"tensor": 1 - core}

    def send(src, dst, ss, rs, to):
        return pltpu.make_async_remote_copy(
            src_ref=src, dst_ref=dst, send_sem=ss, recv_sem=rs, device_id=to, device_id_type=MESH
        )

    loads = [pltpu.make_async_copy(a, b, in_sem.at[j]) for j, (a, b) in enumerate(((x_in, x), (dy_in, dy)))]
    for c in loads:
        c.start()

    bar = pltpu.get_barrier_semaphore()
    peers = z_ids + [y_id, x_id, d_id, t_id]
    peers += [{"dp": (me + s) % count} for s in range(1, REACH + 1)]
    peers += [{"dp": (me + count - s) % count} for s in range(1, REACH + 1)]
    for p in peers:
        pl.semaphore_signal(bar, inc=1, device_id=p, device_id_type=MESH)
    pl.semaphore_wait(bar, len(peers))

    def cols(k):
        return pl.ds(chunks[k][0], chunks[k][1])

    def halves(k):
        c0, cn = chunks[k]
        if cn < 256:
            return pl.ds(c0, cn), None
        first = cn // 256 * 128
        return pl.ds(c0, first), pl.ds(c0 + first, cn - first)

    def gather_z(k):
        r = W.at[z, y, xx, :, cols(k)]
        return [send(r, r, gzs.at[k, j], gzr.at[k, j], z_ids[j]) for j in range(3)]

    def gather_col(k):
        r = W.at[:, y, xx, :, cols(k)]
        return [send(r, r, g2s.at[k, 0], g2r.at[k, 0], x_id), send(r, r, g2s.at[k, 1], g2r.at[k, 1], y_id)]

    def gather_far(k):
        first, second = halves(k)
        r = W.at[:, y, 1 - xx, :, first]
        out = [send(r, r, g3s.at[k, 0], g3r.at[k, 0], y_id)]
        if second is not None:
            r = W.at[:, 1 - y, xx, :, second]
            out.append(send(r, r, g3s.at[k, 1], g3r.at[k, 1], x_id))
        return out

    def start1(k):
        for c in gather_z(k):
            c.start()

    def step2(k):
        for c in gather_z(k):
            c.wait_recv()
        for c in gather_col(k):
            c.start()

    def step3(k):
        for c in gather_col(k):
            c.wait_recv()
        for c in gather_far(k):
            c.start()

    def arrived(k):
        for c in gather_far(k):
            c.wait_recv()

    def weight(k):
        c0, cn = chunks[k]
        return W[:, :, :, :, c0 : c0 + cn].reshape(D, cn)

    def red1(k):
        first, second = halves(k)
        out = [send(G.at[:, :, 1 - xx, :, first], r1.at[:, :, :, first], a1s.at[k, 0], a1r.at[k, 0], x_id)]
        if second is not None:
            out.append(send(G.at[:, 1 - y, :, :, second], r1.at[:, :, :, second], a1s.at[k, 1], a1r.at[k, 1], y_id))
        return out

    def red2(k):
        first, second = halves(k)
        out = [send(r1.at[:, 1 - y, :, first], r2.at[:, :, first], a2s.at[k, 0], a2r.at[k, 0], y_id)]
        if second is not None:
            out.append(send(r1.at[:, 1 - xx, :, second], r2.at[:, :, second], a2s.at[k, 1], a2r.at[k, 1], x_id))
        return out

    def red3(k):
        return [
            send(r2.at[(z + j + 1) % 4, :, cols(k)], r3.at[j, :, cols(k)], azs.at[k, j], azr.at[k, j], z_ids[j])
            for j in range(3)
        ]

    def step_a(k):
        for c in red1(k):
            c.start()

    def step_b(k):
        first, second = halves(k)
        for c in red1(k):
            c.wait_recv()

        def add(i, _):
            zz, o = i // 2, i % 2
            r1[zz, o, :, first] = r1[zz, o, :, first] + G[zz, o, xx, :, first]
            if second is not None:
                r1[zz, o, :, second] = r1[zz, o, :, second] + G[zz, y, o, :, second]
            return 0

        lax.fori_loop(0, 8, add, 0)
        for c in red2(k):
            c.start()

    def step_c(k):
        first, second = halves(k)
        for c in red2(k):
            c.wait_recv()

        def add(i, _):
            r2[i, :, first] = r2[i, :, first] + r1[i, y, :, first]
            if second is not None:
                r2[i, :, second] = r2[i, :, second] + r1[i, xx, :, second]
            return 0

        lax.fori_loop(0, 4, add, 0)
        for c in red3(k):
            c.start()

    def step_e(k):
        for c in red3(k):
            c.wait_recv()
        total = r2[z, :, cols(k)].astype(F32)
        for j in range(3):
            total = total + r3[j, :, cols(k)].astype(F32)
        grads_out[:, cols(k)] = total

    def act(place_name):
        for move, k in SCHEDULE.get(place_name, ()):
            if move == "z":
                start1(k)
            elif move == "col":
                step2(k)
            elif move == "far":
                step3(k)
            elif move == "b":
                step_b(k)
            elif move == "c":
                step_c(k)
            elif move == "e":
                step_e(k)
            else:
                return_halo(k)

    def act_in(loop_name, i):
        for j in range(M * heads):
            if loop_name + str(j) in SCHEDULE:
                pl.when(i == j)(functools.partial(act, loop_name + str(j)))

    def place(k, block):
        c0 = chunks[k][0]
        W[z, y, xx, :, c0 : c0 + block.shape[1]] = block

    place(kKV, jnp.concatenate([w_keyval[...], jnp.zeros((shard_rows, HDIM), BF16)], axis=1))
    place(kQ, w_query[...])
    place(kO, w_out[...])
    for c in range(pieces):
        place(kUp[c], w_up[:, c * piece : (c + 1) * piece])
        place(kDown[c], w_down[:, c * piece : (c + 1) * piece])
    act("pro")

    R = 256
    vec[...] = jnp.zeros_like(vec)

    def row(ref):
        return ref[...].reshape(1, ref.shape[0])

    g1v, b1v, g2v, b2v = row(g1), row(b1), row(g2), row(b2)

    def xhat_of(rows):
        v = x[rows, :].astype(F32)
        c = v - jnp.mean(v, axis=-1, keepdims=True)
        rstd = lax.rsqrt(jnp.mean(c * c, axis=-1, keepdims=True) + epsilon)
        return v, c * rstd, rstd

    def norm_tile(i, _):
        rows = pl.ds(pl.multiple_of(i * R, R), R)
        _, xh, _ = xhat_of(rows)
        n1v = (xh * g1v + b1v).astype(BF16)
        n2v = (xh * g2v + b2v).astype(BF16)
        n2[rows, :] = n2v
        n1T[:, rows] = n1v.T
        n2T[:, rows] = n2v.T
        d = dy[rows, :]
        dyT[:, rows] = d.T
        vec[4:5, :] += jnp.sum(d.astype(F32), axis=0, keepdims=True)
        return 0

    for c in loads:
        c.wait()
    lax.fori_loop(0, T // R, norm_tile, 0)
    act("norm")
    h = ROT // 2
    index = lax.broadcasted_iota(jnp.int32, (h, 1), 0)
    inverse = jnp.zeros((h, 1), F32)
    for i in range(h):
        inverse = jnp.where(index == i, 10000.0 ** (-(2.0 * i) / ROT), inverse)
    for m in range(M):
        ms = slice(m * n, (m + 1) * n)
        place_row = positions[m : m + 1, :]
        angle = inverse * place_row.astype(F32)
        cos[:, ms] = jnp.cos(angle)
        sine[:, ms] = jnp.sin(angle)
        start[m] = lax.broadcasted_iota(jnp.int32, (1, n), 1) + own - place_row

    def keyval_spin(rows, m, sign):
        ms = slice(m * n, (m + 1) * n)
        return spin(rows, jnp.where(core == 0, cos[:, ms], 1.0), jnp.where(core == 0, sign * sine[:, ms], 0.0))

    def column(ref):
        size = ref.shape[0]
        return jnp.broadcast_to(ref[...].reshape(1, size), (8, size)).T[:, 0:1]

    act("cos")
    arrived(kKV)
    wkvT = weight(kKV).T[0:HDIM]
    bkv = column(b_keyval)
    for m in range(M):
        ms = slice(m * n, (m + 1) * n)
        low_kv[m] = keyval_spin(nn(wkvT, n1T[:, ms]) + bkv, m, 1.0).astype(BF16)
    kvTwin[:, mine, own : own + n] = low_kv[...]

    def block(s):
        return pl.ds((REACH - s) * n, n)

    def halo(s):
        return send(
            low_kv, kvTwin.at[:, mine, block(s)], hfs.at[s - 1], hfr.at[s - 1], {"dp": (me + s) % count}
        )

    def across(s):
        part = kvTwin.at[:, mine, block(s)]
        return send(part, part, fws.at[s], fwr.at[s], t_id)

    for s in range(1, REACH + 1):
        @pl.when(me + s < count)
        def _(s=s):
            halo(s).start()
    across(0).start()

    act("kv")
    across(0).wait_recv()
    for m in range(M):
        natural = kvTwin[m, :, own : own + n].T
        kvwin[m, own : own + n, :] = natural
        keyval_out[m] = natural
    stores = [
        pltpu.make_async_copy(a, b, out_sem.at[j])
        for j, (a, b) in enumerate(((keyval_out, keyval_hbm), (layer_out, layer_hbm)))
    ]
    stores[0].start()
    act("own")
    arrived(kQ)
    wqT[...] = weight(kQ).T
    bq = column(b_query)
    for m in range(M):
        ms = slice(m * n, (m + 1) * n)
        lin = nn(wqT[...], n1T[:, ms]) + bq
        spun = spin(lin.reshape(heads, HDIM, n), cos[:, ms], sine[:, ms]) * scale
        qT[m * heads : (m + 1) * heads] = spun.astype(BF16)
    act("q")

    near, far = near_tiles(n, n // 2), far_tiles(n, n // 2)
    tops, totals, sums = lse, dvec, dqT

    def visible(w0, kn, q0, qn, first, causal):
        key = lax.broadcasted_iota(jnp.int32, (kn, 1), 0) + w0
        seen = key >= first
        if causal:
            query = lax.broadcasted_iota(jnp.int32, (1, qn), 1) + (q0 + own)
            seen = seen & (key <= query)
        return seen

    def padded_query(i):
        return jnp.concatenate([qT[i], jnp.zeros((KV - HDIM, n), BF16)], axis=0)

    def forward_tiles(i, tiles):
        m = i // pairs
        first = start[m]
        queries = [padded_query(2 * i + t) for t in range(2)]

        def scores(t, tile):
            w0, kn, q0, qn, causal = tile
            qs = slice(q0, q0 + qn)
            sc = nn(kvwin[m, w0 : w0 + kn, :], queries[t][:, qs])
            return jnp.where(visible(w0, kn, q0, qn, first[:, qs], causal), sc, LOW)

        def take(t, tile, sc):
            w0, kn, q0, qn, _ = tile
            qs = slice(q0, q0 + qn)
            before = m_s[t, :, qs]
            top = jnp.maximum(before, jnp.max(sc, axis=0, keepdims=True))
            p = jnp.exp(sc - top)
            shrink = jnp.exp(before - top)
            l_s[t, :, qs] = l_s[t, :, qs] * shrink + jnp.sum(p, axis=0, keepdims=True)
            m_s[t, :, qs] = top
            acc[t, :, qs] = acc[t, :, qs] * shrink + nn(kvTwin[m, HDIM:KV, w0 : w0 + kn], p.astype(BF16))

        ready = [scores(t, tiles[0]) for t in range(2)]
        for at_tile, tile in enumerate(tiles):
            ahead = None
            if at_tile + 1 < len(tiles):
                ahead = [scores(t, tiles[at_tile + 1]) for t in range(2)]
            for t in range(2):
                take(t, tile, ready[t])
            ready = ahead

    def forward_near(i, _):
        m_s[...] = jnp.full_like(m_s, LOW)
        l_s[...] = jnp.zeros_like(l_s)
        acc[...] = jnp.zeros_like(acc)
        forward_tiles(i, near)
        both = pl.ds(2 * i, 2)
        tops[both], totals[both], sums[both] = m_s[...], l_s[...], acc[...]
        return 0

    def forward_far(i, _):
        m = i // pairs
        both = pl.ds(2 * i, 2)
        m_s[...], l_s[...], acc[...] = tops[both], totals[both], sums[both]
        forward_tiles(i, far)
        o = acc[...] / l_s[...]
        sums[both] = o
        lse[both] = m_s[...] + jnp.log(l_s[...])
        rows = pl.ds(pl.multiple_of(m * n, n), n)
        lanes = pl.ds(pl.multiple_of((i % pairs) * 2 * HDIM, 2 * HDIM), 2 * HDIM)
        o_nat[rows, lanes] = o.astype(BF16).reshape(2 * HDIM, n).T
        act_in("far", i)
        return 0

    def near_step(i, _):
        forward_near(i, 0)
        act_in("near", i)
        return 0

    lax.fori_loop(0, M * pairs, near_step, 0)
    for s in range(1, REACH + 1):
        @pl.when(me >= s)
        def _(s=s):
            halo(s).wait_recv()
            across(s).start()

        @pl.when(me < s)
        def _(s=s):
            kvTwin[:, :, block(s)] = jnp.zeros((M, KV, n), BF16)

    act("halow")
    for s in range(1, REACH + 1):
        @pl.when(me >= s)
        def _(s=s):
            across(s).wait_recv()

        for m in range(M):
            kvwin[m, block(s), :] = kvTwin[m, :, block(s)].T

    act("acw")
    lax.fori_loop(0, M * pairs, forward_far, 0)

    arrived(kO)
    wo = weight(kO).T
    for m in range(M):
        ms = slice(m * n, (m + 1) * n)
        doT[m * heads : (m + 1) * heads] = nn(wo, dyT[:, ms]).astype(BF16).reshape(heads, HDIM, n)

    def mix_dots(i, _):
        dvec[i] = jnp.sum(doT[i].astype(F32) * sums[i], axis=0, keepdims=True)
        return 0

    lax.fori_loop(0, M * heads, mix_dots, 0)

    def put_grad(k, leftT, right):
        c0, cn = chunks[k]

        def half(i, _):
            rows = pl.ds(pl.multiple_of(i * (D // 2), 128), D // 2)
            part = nn(leftT[rows, :], right[...]).astype(BF16)
            G[pl.ds(i * 2, 2), :, :, :, c0 : c0 + cn] = part.reshape(2, 2, 2, shard_rows, cn)
            return 0

        lax.fori_loop(0, 2, half, 0)
        step_a(k)

    put_grad(kO, dyT, o_nat)
    act("mix")

    def feed_forward(c):
        ku, kd = kUp[c], kDown[c]
        arrived(ku)
        arrived(kd)
        (u0, _), (d0, _) = chunks[ku], chunks[kd]
        up_bias = b_up[c * piece : (c + 1) * piece].reshape(1, piece)

        def rows_tile(i, _):
            rows = pl.ds(pl.multiple_of(i * R, R), R)
            u = nn(n2[rows, :], W[:, :, :, :, u0 : u0 + piece].reshape(D, piece)) + up_bias
            phi = 0.5 * (1.0 + lax.erf(u * 0.7071067811865476))
            slope = phi + u * (jnp.exp(-0.5 * u * u) * 0.3989422804014327)
            gbuf[rows, c * piece : (c + 1) * piece] = (u * phi).astype(BF16)
            dg = nn(dy[rows, :], W[:, :, :, :, d0 : d0 + piece].reshape(D, piece))
            dubuf[c, rows, :] = (slope * dg).astype(BF16)
            return 0

        lax.fori_loop(0, T // R, rows_tile, 0)
        put_grad(ku, n2T, dubuf.at[c])
        put_grad(kd, dyT, gbuf.at[:, c * piece : (c + 1) * piece])

    def branch_tile(i, _):
        rows = pl.ds(pl.multiple_of(i * R, R), R)
        total = nt(o_nat[rows, :], weight(kO))
        back = jnp.zeros((R, D), F32)
        for c in range(pieces):
            total = total + nt(gbuf[rows, c * piece : (c + 1) * piece], weight(kDown[c]))
            back = back + nt(dubuf[c, rows, :], weight(kUp[c]))
        layer_out[rows, :] = total.astype(BF16)
        input_grad[rows, :] = back.astype(BF16)
        return 0

    y_copy = send(layer_out, yr, xs.at[0], xr.at[0], t_id)
    d2_copy = send(input_grad, d2r, xs.at[1], xr.at[1], t_id)

    def branches():
        lax.fori_loop(0, T // R, branch_tile, 0)
        y_copy.start()
        d2_copy.start()
        for c in range(pieces):
            part = jnp.sum(dubuf[c].astype(F32), axis=0, keepdims=True)
            done = 0
            while done < piece:
                flat = c * piece + done
                line, col = flat // D, flat % D
                width = min(piece - done, D - col)
                vec[6 + line : 7 + line, col : col + width] = part[:, done : done + width]
                done += width

    feed_forward(0)
    act("ffn0")

    dkv[...] = jnp.zeros_like(dkv)

    def backward_tiles(i, tiles):
        m = i // heads
        zero = jnp.zeros((HDIM, n), BF16)
        query = jnp.concatenate([qT[i], zero], axis=0)
        cotangent = jnp.concatenate([zero, doT[i]], axis=0)
        natural = jnp.concatenate([qT[i], doT[i]], axis=0).T
        first, ls, dots = start[m], lse[i], dvec[i]
        step = n // 2
        pieces_of = [(w0 + a, step, q0, qn, c) for w0, kn, q0, qn, c in tiles for a in range(0, kn, step)]

        def products(tile):
            w0, kn, q0, qn, causal = tile
            qs = slice(q0, q0 + qn)
            rows = kvwin[m, w0 : w0 + kn, :]
            sc = nn(rows, query[:, qs])
            sc = jnp.where(visible(w0, kn, q0, qn, first[:, qs], causal), sc, LOW)
            return sc, nn(rows, cotangent[:, qs])

        ready = products(pieces_of[0])
        for at_tile, tile in enumerate(pieces_of):
            ahead = products(pieces_of[at_tile + 1]) if at_tile + 1 < len(pieces_of) else None
            w0, kn, q0, qn, _ = tile
            qs = slice(q0, q0 + qn)
            sc, dp = ready
            p = jnp.exp(sc - ls[:, qs])
            ds = (p * (dp - dots[:, qs])).astype(BF16)
            for_k = nn(ds, natural[qs])
            for_v = nn(p.astype(BF16), natural[qs])
            lane = lax.broadcasted_iota(jnp.int32, for_k.shape, 1)
            dkv[m, w0 : w0 + kn, :] += jnp.where(lane < HDIM, for_k, for_v)
            dqT[i, :, qs] += nn(kvTwin[m, 0:HDIM, w0 : w0 + kn], ds)
            ready = ahead

    def backward_far(i, _):
        @pl.when(i == FEED_AT[0])
        def _():
            feed_forward(1)
            act("ffn1")

        @pl.when(i == FEED_AT[1])
        def _():
            feed_forward(2)
            branches()
            act("ffn2")

        dqT[i] = jnp.zeros((HDIM, n), F32)
        backward_tiles(i, far)
        for m in range(M):
            pl.when(i == (m + 1) * heads - 1)(functools.partial(give_half, m))
        act_in("bfar", i)
        return 0

    def backward_near(i, _):
        backward_tiles(i, near)
        for m in range(M):
            pl.when(i == (m + 1) * heads - 1)(functools.partial(give_own, m))
        act_in("bnear", i)
        return 0

    def back_copy(s, m):
        return send(
            hs.at[s - 1, m], hr.at[s - 1, m], hbs.at[s - 1, m], hbr.at[s - 1, m],
            {"dp": (me + count - s) % count},
        )

    def half_copy(m):
        part = pl.ds(0, own)
        return send(hx.at[m, :, part], hxr.at[m, :, part], xs.at[2 + m], xr.at[2 + m], t_id)

    def own_copy(m):
        part = pl.ds(own, n)
        return send(hx.at[m, :, part], hxr.at[m, :, part], xs.at[2 + M + m], xr.at[2 + M + m], t_id)

    def split(m, j):
        js = slice(j * n, (j + 1) * n)
        turned[...] = dkv[m, js, :].T
        dkvT[m, :, js] = turned[mine, :]
        hx[m, :, js] = turned[other, :].astype(BF16)

    def give_half(m):
        for j in range(REACH):
            split(m, j)
        half_copy(m).start()

    def return_halo(m):
        half_copy(m).wait_recv()
        for j in range(REACH):
            js = slice(j * n, (j + 1) * n)
            hs[REACH - j - 1, m] = (dkvT[m, :, js] + hxr[m, :, js].astype(F32)).astype(BF16)
        for s in range(1, REACH + 1):
            @pl.when(me >= s)
            def _(s=s):
                back_copy(s, m).start()

    def give_own(m):
        split(m, REACH)
        own_copy(m).start()

    lax.fori_loop(0, M * heads, backward_far, 0)
    lax.fori_loop(0, M * heads, backward_near, 0)

    for m in range(M):
        ms = slice(m * n, (m + 1) * n)
        rows = dqT[m * heads : (m + 1) * heads] * scale
        low = spin(rows, cos[:, ms], -sine[:, ms]).astype(BF16)
        dql[ms, :] = low.reshape(hq, n).T
    put_grad(kQ, n1T, dql)
    vec[5:6, 0:hq] = jnp.sum(dql[...].astype(F32), axis=0, keepdims=True)
    act("t0")

    for m in range(M):
        ms = slice(m * n, (m + 1) * n)
        own_copy(m).wait_recv()
        dko = dkvT[m, :, own : own + n] + hxr[m, :, own : own + n].astype(F32)
        kvo[...] = dko
        for s in range(1, REACH + 1):
            @pl.when(me + s < count)
            def _(s=s, m=m):
                back_copy(s, m).wait_recv()
                kvo[...] += hr[s - 1, m].astype(F32)
        low = keyval_spin(kvo[...], m, -1.0).astype(BF16)
        dkl[ms, :] = jnp.concatenate([low, jnp.zeros((KV - HDIM, n), BF16)], axis=0).T
    put_grad(kKV, n1T, dkl)
    vec[5:6, hq : hq + KV] = jnp.sum(dkl[...].astype(F32), axis=0, keepdims=True)
    act("t1")

    def d1_copy(i):
        rows = pl.ds(pl.multiple_of(i * R, R), R)
        return send(gbuf.at[rows, pl.ds(0, D)], n2.at[rows], ts.at[i], tr.at[i], t_id)

    def first_tile(i, _):
        rows = pl.ds(pl.multiple_of(i * R, R), R)
        gbuf[rows, 0:D] = (nt(dql[rows, :], weight(kQ)) + nt(dkl[rows, :], weight(kKV))).astype(BF16)
        d1_copy(i).start()
        return 0

    lax.fori_loop(0, T // R, first_tile, 0)
    act("t2")

    y_copy.wait()
    both_bias = row(b_out) + row(b_down)

    def out_tile(i, _):
        rows = pl.ds(pl.multiple_of(i * R, R), R)
        both = (layer_out[rows, :].astype(F32) + yr[rows, :].astype(F32)) + both_bias
        layer_out[rows, :] = (x[rows, :].astype(F32) + both).astype(BF16)
        return 0

    lax.fori_loop(0, T // R, out_tile, 0)
    stores[1].start()
    act("t3")
    d2_copy.wait()

    def grad_store(i):
        rows = pl.ds(pl.multiple_of(i * R, R), R)
        return pltpu.make_async_copy(input_grad.at[rows], grad_hbm.at[rows], out_sem.at[2 + i])

    def last_tile(i, _):
        rows = pl.ds(pl.multiple_of(i * R, R), R)
        _, xh, rstd = xhat_of(rows)
        d1_copy(i).wait_recv()
        dn1 = gbuf[rows, 0:D].astype(F32) + n2[rows, :].astype(F32)
        dn2 = input_grad[rows, :].astype(F32) + d2r[rows, :].astype(F32)
        vec[0:1, :] += jnp.sum(dn1 * xh, axis=0, keepdims=True)
        vec[1:2, :] += jnp.sum(dn1, axis=0, keepdims=True)
        vec[2:3, :] += jnp.sum(dn2 * xh, axis=0, keepdims=True)
        vec[3:4, :] += jnp.sum(dn2, axis=0, keepdims=True)
        a = dn1 * g1v + dn2 * g2v
        back = a - jnp.mean(a, axis=-1, keepdims=True) - xh * jnp.mean(a * xh, axis=-1, keepdims=True)
        input_grad[rows, :] = (dy[rows, :].astype(F32) + rstd * back).astype(BF16)
        grad_store(i).start()
        return 0

    lax.fori_loop(0, T // R, last_tile, 0)

    flat = y * 2 + xx
    vp[flat] = vec[...]
    plane = [send(vp.at[flat], vp.at[flat], vs.at[j], vr.at[j], to) for j, to in enumerate((x_id, y_id, d_id))]
    for c in plane:
        c.start()
    act("t4")
    for c in plane:
        c.wait_recv()
    vz[z] = (vp[0] + vp[1]) + (vp[2] + vp[3])
    along = [send(vz.at[z], vz.at[z], vs.at[3 + j], vr.at[3 + j], z_ids[j]) for j in range(3)]
    for c in along:
        c.start()
    act("t5")
    for c in along:
        c.wait_recv()
    act("t6")
    vec_out[...] = (vz[0] + vz[1]) + (vz[2] + vz[3])

    for k in range(n_chunks):
        for c in gather_z(k) + gather_col(k) + gather_far(k) + red1(k) + red2(k) + red3(k):
            c.wait_send()
    across(0).wait_send()
    for s in range(1, REACH + 1):
        @pl.when(me + s < count)
        def _(s=s):
            halo(s).wait_send()

        @pl.when(me >= s)
        def _(s=s):
            across(s).wait_send()
            for m in range(M):
                back_copy(s, m).wait_send()
    for m in range(M):
        half_copy(m).wait_send()
        own_copy(m).wait_send()
    for i in range(T // R):
        d1_copy(i).wait_send()
        grad_store(i).wait()
    for c in stores:
        c.wait()
    for c in plane + along:
        c.wait_send()


def finish_kernel(
    chunks, pieces,
    y_in, kv_in, x_in, grads, vec,
    y_out, kv_out, x_out, n1g, n1b, n2g, n2b, wq, bq, wkv, bkv, wo, bo, wu, bu, wd, bd,
    y_buf, kv_buf, x_buf, in_sem, out_sem,
):
    loads, stores = [], []
    half_rows = pl.ds(0, y_in.shape[0] // 2), pl.ds(y_in.shape[0] // 2, y_in.shape[0] // 2)
    for a, buf, b in (
        (y_in.at[half_rows[0]], y_buf.at[half_rows[0]], y_out.at[half_rows[0]]),
        (y_in.at[half_rows[1]], y_buf.at[half_rows[1]], y_out.at[half_rows[1]]),
        (x_in.at[half_rows[0]], x_buf.at[half_rows[0]], x_out.at[half_rows[0]]),
        (x_in.at[half_rows[1]], x_buf.at[half_rows[1]], x_out.at[half_rows[1]]),
        (kv_in, kv_buf, kv_out),
    ):
        loads.append(pltpu.make_async_copy(a, buf, in_sem.at[len(loads)]))
        stores.append(pltpu.make_async_copy(buf, b, out_sem.at[len(stores)]))
    for c in loads:
        c.start()
    for load, store in zip(loads, stores):
        load.wait()
        store.start()
    hq, half, piece, D = wq.shape[1], wkv.shape[1], chunks[3][1], vec.shape[1]
    for out, r in ((n1g, 0), (n1b, 1), (n2g, 2), (n2b, 3), (bo, 4), (bd, 4)):
        out[...] = vec[r].reshape(D)
    q0, o0 = chunks[1][0], chunks[2][0]
    wq[...] = grads[:, q0 : q0 + hq]
    wkv[...] = grads[:, 0:half]
    wo[...] = grads[:, o0 : o0 + hq]
    for c in range(pieces):
        u0, d0 = chunks[3 + 2 * c][0], chunks[4 + 2 * c][0]
        wu[:, c * piece : (c + 1) * piece] = grads[:, u0 : u0 + piece]
        wd[:, c * piece : (c + 1) * piece] = grads[:, d0 : d0 + piece]
    bq[...] = vec[5:6, 0:hq].reshape(hq)
    bkv[...] = vec[5:6, hq : hq + half].reshape(half)
    for r in range(bu.shape[0] // D):
        bu[r * D : (r + 1) * D] = vec[6 + r].reshape(D)
    for c in stores:
        c.wait()


def fused_layer(arguments, pieces):
    (hidden_in, positions, out_grad, g1, b1, g2, b2, w_query, b_query, w_keyval, b_keyval,
     w_out, b_out, w_up, b_up, w_down, b_down) = arguments
    M, n, D = hidden_in.shape
    T = M * n
    hq, F, half, rows = b_query.shape[0], b_up.shape[0], b_keyval.shape[0], w_query.shape[0]
    heads, KV, piece = hq // HDIM, 2 * half, F // pieces
    chunks = chunk_list(hq, KV, F, pieces)
    C = chunks[-1][0] + chunks[-1][1]
    k = len(chunks)
    Wn = (REACH + 1) * n
    V = pltpu.VMEM
    S = pltpu.SemaphoreType.DMA
    sds = jax.ShapeDtypeStruct
    vm = pl.BlockSpec(memory_space=pltpu.VMEM)
    mh = M * heads
    hbm = pl.BlockSpec(memory_space=pl.ANY)
    scratch = [
        V((T, D), BF16), V((T, D), BF16), V((T, D), BF16), V((M, n, KV), BF16), V((T, D), BF16),
        S((2,)), S((2 + T // 256,)),
        V((4, 2, 2, rows, C), BF16), V((4, 2, 2, rows, C), BF16),
        V((D, T), BF16), V((T, D), BF16), V((D, T), BF16), V((D, T), BF16),
        V((hq, D), BF16), V((mh, HDIM, n), BF16), V((mh, HDIM, n), BF16),
        V((T, hq), BF16), V((mh, 1, n), F32), V((mh, 1, n), F32),
        V((M, Wn, KV), BF16), V((M, KV, Wn), BF16), V((M, HDIM, n), BF16),
        V((ROT // 2, T), F32), V((ROT // 2, T), F32), V((M, 1, n), jnp.int32),
        V((2, 1, n), F32), V((2, 1, n), F32), V((2, HDIM, n), F32),
        V((T, F), BF16), V((pieces, T, piece), BF16),
        V((mh, HDIM, n), F32), V((M, Wn, KV), F32), V((M, HDIM, Wn), F32), V((KV, n), F32),
        V((REACH, M, HDIM, n), BF16), V((REACH, M, HDIM, n), BF16),
        V((M, HDIM, Wn), BF16), V((M, HDIM, Wn), BF16), V((HDIM, n), F32),
        V((T, D), BF16), V((T, D), BF16),
        V((4, 2, rows, C), BF16), V((4, rows, C), BF16), V((3, rows, C), BF16),
        V((8, D), F32), V((4, 8, D), F32), V((4, 8, D), F32),
        V((T, hq), BF16), V((T, KV), BF16),
        S((k, 3)), S((k, 3)), S((k, 2)), S((k, 2)), S((k, 2)), S((k, 2)),
        S((k, 2)), S((k, 2)), S((k, 2)), S((k, 2)), S((k, 3)), S((k, 3)),
        S((REACH,)), S((REACH,)), S((REACH, M)), S((REACH, M)), S((REACH + 1,)), S((REACH + 1,)),
        S((2 + 2 * M,)), S((2 + 2 * M,)), S((T // 256,)), S((T // 256,)), S((6,)), S((6,)),
    ]
    y_out, kv_out, x_out, grads, vec = pl.pallas_call(
        functools.partial(fused_kernel, chunks, pieces),
        out_shape=(
            sds((T, D), BF16), sds((M, n, KV), BF16), sds((T, D), BF16), sds((rows, C), F32), sds((8, D), F32),
        ),
        in_specs=[hbm] * 2 + [vm] * 15,
        out_specs=(hbm,) * 3 + (vm,) * 2,
        scratch_shapes=scratch,
        compiler_params=pltpu.CompilerParams(
            collective_id=0, has_side_effects=True, vmem_limit_bytes=62 << 20
        ),
        name="fused_layer",
    )(hidden_in.reshape(T, D), out_grad.reshape(T, D), positions, g1, b1, g2, b2, w_query, b_query,
      w_keyval, b_keyval, w_out.T, b_out, w_up, b_up, w_down.T, b_down)
    vector = sds((D,), F32)
    out_shape = (
        sds((T, D), BF16), sds((M, n, KV), BF16), sds((T, D), BF16), vector, vector, vector, vector,
        sds(w_query.shape, F32), sds(b_query.shape, F32), sds(w_keyval.shape, F32), sds(b_keyval.shape, F32),
        sds(w_out.shape[::-1], F32), vector, sds(w_up.shape, F32), sds(b_up.shape, F32), sds(w_down.shape[::-1], F32), vector,
    )
    outs = pl.pallas_call(
        functools.partial(finish_kernel, chunks, pieces),
        out_shape=out_shape,
        in_specs=[hbm] * 3 + [vm] * 2,
        out_specs=(hbm,) * 3 + (vm,) * 14,
        scratch_shapes=[V((T, D), BF16), V((M, n, KV), BF16), V((T, D), BF16), S((5,)), S((5,))],
        compiler_params=pltpu.CompilerParams(vmem_limit_bytes=60 << 20),
        name="finish_layer",
    )(y_out, kv_out, x_out, grads, vec)
    outs = list(outs)
    outs[0], outs[2] = outs[0].reshape(hidden_in.shape), outs[2].reshape(hidden_in.shape)
    outs[11], outs[15] = outs[11].T, outs[15].T
    return tuple(outs)


PIECES = 3


def fits_fused(hidden_in, query_weight, up_weight):
    rows, hq = query_weight.shape
    return (
        lax.axis_size("dp") == 16
        and rows % 16 == 0
        and hq % 384 == 0
        and up_weight.shape[1] % (PIECES * 256) == 0
        and up_weight.shape[1] >= hidden_in.shape[2]
        and hidden_in.shape[1] % 256 == 0
    )


def on_device(*arguments):
    if fits_fused(arguments[0], arguments[7], arguments[13]):
        return fused_layer(arguments, PIECES)
    return plain_layer(*arguments)


def solution(mesh):
    return jax.shard_map(
        on_device,
        mesh=mesh,
        in_specs=(
            P(None, "dp", None),
            P(None, "dp"),
            P(None, "dp", None),
            P(),
            P(),
            P(),
            P(),
            P("dp", "tensor"),
            P("tensor"),
            P("dp", "tensor"),
            P("tensor"),
            P("tensor", "dp"),
            P(),
            P("dp", "tensor"),
            P("tensor"),
            P("tensor", "dp"),
            P(),
        ),
        out_specs=(
            P(None, "dp", None),
            P(None, "dp", None),
            P(None, "dp", None),
            P(),
            P(),
            P(),
            P(),
            P("dp", "tensor"),
            P("tensor"),
            P("dp", "tensor"),
            P("tensor"),
            P("tensor", "dp"),
            P(),
            P("dp", "tensor"),
            P("tensor"),
            P("tensor", "dp"),
            P(),
        ),
        check_vma=False,
    )
```

```python
import functools
import jax
import jax.numpy as jnp
from jax import lax
from jax.experimental import pallas as pl
from jax.experimental.pallas import tpu as pltpu
from jax.sharding import PartitionSpec as P

HDIM = 64
ROT = 16
REACH = 4
epsilon = 1e-05
MESH = pl.DeviceIdType.MESH
LOW = -1e30
F32 = jnp.float32
BF16 = jnp.bfloat16


SCHEDULE = {
    "pro": (("z", 0), ("z", 2), ("col", 2), ("z", 1), ("col", 0), ("z", 3),),
    "norm": (("z", 5), ("col", 1), ("far", 0),),
    "cos": (("z", 4), ("far", 1), ("col", 3),),
    "kv": (("col", 4), ("far", 3),),
    "own": (("far", 2),),
    "near2": (("z", 6),),
    "near5": (("col", 5),),
    "halow": (("z", 7),),
    "acw": (("far", 4), ("z", 9),),
    "far0": (("col", 6),),
    "far1": (("z", 8), ("col", 7), ("z", 10),),
    "far2": (("far", 5), ("col", 9),),
    "far4": (("far", 6),),
    "far5": (("col", 8),),
    "ffn0": (("far", 8), ("far", 7), ("far", 9), ("col", 10),),
    "bfar4": (("b", 4),),
    "ffn1": (("c", 4),),
    "bfar5": (("far", 10),),
    "bfar6": (("b", 8), ("ret", 0),),
    "bfar7": (("b", 6),),
    "ffn2": (("c", 8),),
    "bfar8": (("c", 6),),
    "bfar9": (("b", 9),),
    "bfar10": (("b", 5), ("c", 9),),
    "bfar11": (("c", 5), ("b", 7),),
    "bnear0": (("e", 4),),
    "bnear1": (("b", 10),),
    "bnear4": (("ret", 1), ("e", 9),),
    "bnear7": (("e", 5), ("e", 6),),
    "bnear11": (("c", 7),),
    "t2": (("c", 10), ("b", 2), ("b", 1),),
    "t3": (("b", 0), ("b", 3),),
    "t4": (("c", 0), ("c", 3), ("e", 8),),
    "t5": (("c", 1), ("e", 3), ("c", 2), ("e", 0), ("e", 7), ("e", 2), ("e", 10), ("e", 1),),
}
FEED_AT = (5, 8)


def shifted(value, axis, steps):
    count = lax.axis_size(axis)
    initial, last = (max(0, -steps), min(count, count - steps))
    return lax.ppermute(value, axis, [(source, source + steps) for source in range(initial, last)])


def norm_forward(stream):
    average = jnp.mean(stream, axis=-1, keepdims=True)
    centered = stream - average
    spread = jnp.mean(centered * centered, axis=-1, keepdims=True)
    scaling = lax.rsqrt(spread + epsilon)
    normed = centered * scaling
    return (normed, scaling)


def norm_backward(upstream, normed, scaling, norm_gain):
    weighted = upstream * norm_gain
    return scaling * (
        weighted
        - jnp.mean(weighted, axis=-1, keepdims=True)
        - normed * jnp.mean(weighted * normed, axis=-1, keepdims=True)
    )


def rotary_tables(places):
    inverse = 10000.0 ** (-(jnp.arange(ROT // 2, dtype=jnp.float32) * 2.0) / ROT)
    angles = places.astype(jnp.float32)[:, None] * inverse[None, :]
    angles = jnp.concatenate([angles, angles], axis=-1)
    return (jnp.cos(angles), jnp.sin(angles))


def rotate(values, cos_table, sine_table):
    head_part = values[..., :ROT]
    first_half = head_part[..., : ROT // 2]
    second_half = head_part[..., ROT // 2 :]
    turned = jnp.concatenate([-second_half, first_half], axis=-1)
    spun_part = head_part * cos_table[:, None, :] + turned * sine_table[:, None, :]
    return jnp.concatenate([spun_part, values[..., ROT:]], axis=-1)


def gelu_exact(values):
    return jax.nn.gelu(values, approximate=False)


def fetch_weights(shard_weights):
    return (
        lax.all_gather(shard_weights[0], "dp", axis=0, tiled=True),
        lax.all_gather(shard_weights[1], "dp", axis=0, tiled=True),
        lax.all_gather(shard_weights[2], "dp", axis=1, tiled=True),
        lax.all_gather(shard_weights[3], "dp", axis=0, tiled=True),
        lax.all_gather(shard_weights[4], "dp", axis=1, tiled=True),
    )


def score_block(queries, key_rows, places, reach_step):
    tokens_here = queries.shape[1]
    scores = jnp.einsum("htd,kd->htk", queries, key_rows, preferred_element_type=jnp.float32)
    row_ids = jnp.arange(tokens_here, dtype=jnp.int32)
    offsets = reach_step * tokens_here + row_ids[:, None] - row_ids[None, :]
    visible = (offsets >= 0) & (offsets <= places[:, None])
    return (scores, visible[None])


def attend_forward(queries, blocks, places):
    heads_here, tokens_here = (queries.shape[0], queries.shape[1])
    top_score = jnp.full((heads_here, tokens_here), -1e30, jnp.float32)
    totals = jnp.zeros((heads_here, tokens_here), jnp.float32)
    for reach_step, kv_block in enumerate(blocks):
        scores, visible = score_block(queries, kv_block[:, :HDIM], places, reach_step)
        masked = jnp.where(visible, scores, -1e30)
        new_top = jnp.maximum(top_score, jnp.max(masked, axis=-1))
        totals = totals * jnp.exp(top_score - new_top) + jnp.sum(
            jnp.where(visible, jnp.exp(masked - new_top[..., None]), 0.0), axis=-1
        )
        top_score = new_top
    log_sum = top_score + jnp.log(totals)
    mixture = jnp.zeros((heads_here, tokens_here, HDIM), jnp.float32)
    for reach_step, kv_block in enumerate(blocks):
        scores, visible = score_block(queries, kv_block[:, :HDIM], places, reach_step)
        weights_low = jnp.where(visible, jnp.exp(scores - log_sum[..., None]), 0.0).astype(
            jnp.bfloat16
        )
        mixture = mixture + jnp.einsum(
            "htk,kd->htd", weights_low, kv_block[:, HDIM:], preferred_element_type=jnp.float32
        )
    return (mixture, log_sum)


def attend_backward(queries, blocks, places, log_sum, grad_mixture, row_dots):
    grad_queries = jnp.zeros(queries.shape, jnp.float32)
    key_terms = []
    for reach_step, kv_block in enumerate(blocks):
        key_rows = kv_block[:, :HDIM]
        value_rows = kv_block[:, HDIM:]
        scores, visible = score_block(queries, key_rows, places, reach_step)
        weights_full = jnp.where(visible, jnp.exp(scores - log_sum[..., None]), 0.0)
        weights_low = weights_full.astype(jnp.bfloat16)
        grad_weights = jnp.einsum(
            "htd,kd->htk", grad_mixture, value_rows, preferred_element_type=jnp.float32
        )
        grad_scores = (weights_full * (grad_weights - row_dots[..., None])).astype(jnp.bfloat16)
        grad_queries = grad_queries + jnp.einsum(
            "htk,kd->htd", grad_scores, key_rows, preferred_element_type=jnp.float32
        )
        grad_keys = jnp.einsum(
            "htk,htd->kd", grad_scores, queries, preferred_element_type=jnp.float32
        )
        grad_values = jnp.einsum(
            "htk,htd->kd", weights_low, grad_mixture, preferred_element_type=jnp.float32
        )
        key_terms.append(jnp.concatenate([grad_keys, grad_values], axis=-1))
    return (grad_queries, key_terms)


def plain_layer(
    hidden_in,
    positions,
    out_grad,
    norm1_gain,
    norm1_bias,
    norm2_gain,
    norm2_bias,
    query_weight,
    query_bias,
    keyval_weight,
    keyval_bias,
    attn_out_weight,
    attn_out_bias,
    up_weight,
    up_bias,
    down_weight,
    down_bias,
):
    micro_count = hidden_in.shape[0]
    tokens_here = hidden_in.shape[1]
    width = hidden_in.shape[2]
    dp_count = lax.axis_size("dp")
    first_core = lax.axis_index("tensor") == 0
    heads_here = query_bias.shape[0] // HDIM
    query_scale = HDIM ** (-0.5)
    shard_weights = (query_weight, keyval_weight, attn_out_weight, up_weight, down_weight)
    gathered = None
    grad_query_w = jnp.zeros((width, query_weight.shape[1]), jnp.float32)
    grad_keyval_w = jnp.zeros((width, keyval_weight.shape[1]), jnp.float32)
    grad_out_w = jnp.zeros(
        (attn_out_weight.shape[0], attn_out_weight.shape[1] * dp_count), jnp.float32
    )
    grad_up_w = jnp.zeros((width, up_weight.shape[1]), jnp.float32)
    grad_down_w = jnp.zeros((down_weight.shape[0], down_weight.shape[1] * dp_count), jnp.float32)
    grad_n1_gain = jnp.zeros((width,), jnp.float32)
    grad_n1_bias = jnp.zeros((width,), jnp.float32)
    grad_n2_gain = jnp.zeros((width,), jnp.float32)
    grad_n2_bias = jnp.zeros((width,), jnp.float32)
    grad_row_sum = jnp.zeros((width,), jnp.float32)
    grad_query_b = jnp.zeros(query_bias.shape, jnp.float32)
    grad_keyval_b = jnp.zeros(keyval_bias.shape, jnp.float32)
    grad_up_b = jnp.zeros(up_bias.shape, jnp.float32)
    layer_rows = []
    cache_rows = []
    input_rows = []
    for micro_step in range(micro_count):
        gathered = fetch_weights(shard_weights)
        w_query, w_keyval, w_out, w_up, w_down = gathered
        stream = hidden_in[micro_step].astype(jnp.float32)
        places = positions[micro_step]
        normed, scaling = norm_forward(stream)
        low_first = (normed * norm1_gain + norm1_bias).astype(jnp.bfloat16)
        low_second = (normed * norm2_gain + norm2_bias).astype(jnp.bfloat16)
        cos_table, sine_table = rotary_tables(places)
        query_lin = jnp.dot(low_first, w_query, preferred_element_type=jnp.float32) + query_bias
        queries = (
            rotate(query_lin.reshape(tokens_here, heads_here, HDIM), cos_table, sine_table)
            * query_scale
        ).astype(jnp.bfloat16)
        query_heads = jnp.transpose(queries, (1, 0, 2))
        half_lin = jnp.dot(low_first, w_keyval, preferred_element_type=jnp.float32) + keyval_bias
        spun_half = rotate(half_lin[:, None, :], cos_table, sine_table)[:, 0, :]
        half_low = jnp.where(first_core, spun_half, half_lin).astype(jnp.bfloat16)
        keyval = lax.all_gather(half_low, "tensor", axis=1, tiled=True)
        blocks = [keyval] + [
            shifted(keyval, "dp", reach_step) for reach_step in range(1, REACH + 1)
        ]
        mixture, log_sum = attend_forward(query_heads, blocks, places)
        mixture_low = (
            jnp.transpose(mixture, (1, 0, 2))
            .reshape(tokens_here, heads_here * HDIM)
            .astype(jnp.bfloat16)
        )
        up_lin = jnp.dot(low_second, w_up, preferred_element_type=jnp.float32) + up_bias
        active_low = gelu_exact(up_lin).astype(jnp.bfloat16)
        branch_part = jnp.dot(mixture_low, w_out, preferred_element_type=jnp.float32) + jnp.dot(
            active_low, w_down, preferred_element_type=jnp.float32
        )
        branches = lax.psum(branch_part.astype(jnp.bfloat16), "tensor").astype(jnp.float32)
        layer_rows.append((stream + branches + attn_out_bias + down_bias).astype(jnp.bfloat16))
        cache_rows.append(keyval)
        grad_low = out_grad[micro_step]
        grad_rows = grad_low.astype(jnp.float32)
        grad_row_sum = grad_row_sum + jnp.sum(grad_rows, axis=0)
        grad_out_w = grad_out_w + jnp.einsum(
            "th,td->hd", mixture_low, grad_low, preferred_element_type=jnp.float32
        )
        grad_down_w = grad_down_w + jnp.einsum(
            "tf,td->fd", active_low, grad_low, preferred_element_type=jnp.float32
        )
        grad_active = jnp.einsum("td,fd->tf", grad_low, w_down, preferred_element_type=jnp.float32)
        gelu_values, gelu_pull = jax.vjp(gelu_exact, up_lin)
        grad_up_low = gelu_pull(grad_active)[0].astype(jnp.bfloat16)
        grad_up_b = grad_up_b + jnp.sum(grad_up_low.astype(jnp.float32), axis=0)
        grad_up_w = grad_up_w + jnp.einsum(
            "td,tf->df", low_second, grad_up_low, preferred_element_type=jnp.float32
        )
        second_part = jnp.einsum("tf,df->td", grad_up_low, w_up, preferred_element_type=jnp.float32)
        grad_mix_low = jnp.einsum(
            "td,hd->th", grad_low, w_out, preferred_element_type=jnp.float32
        ).astype(jnp.bfloat16)
        grad_mixture = jnp.transpose(grad_mix_low.reshape(tokens_here, heads_here, HDIM), (1, 0, 2))
        row_dots = jnp.sum(grad_mixture.astype(jnp.float32) * mixture, axis=-1)
        grad_queries, key_terms = attend_backward(
            query_heads, blocks, places, log_sum, grad_mixture, row_dots
        )
        keyval_grad = key_terms[0]
        for reach_step in range(1, REACH + 1):
            keyval_grad = keyval_grad + shifted(
                key_terms[reach_step].astype(jnp.bfloat16), "dp", -reach_step
            ).astype(jnp.float32)
        half_grad = lax.psum_scatter(
            keyval_grad.astype(jnp.bfloat16), "tensor", scatter_dimension=1, tiled=True
        ).astype(jnp.float32)
        unspun_half = rotate(half_grad[:, None, :], cos_table, -sine_table)[:, 0, :]
        half_grad_low = jnp.where(first_core, unspun_half, half_grad).astype(jnp.bfloat16)
        grad_keyval_b = grad_keyval_b + jnp.sum(half_grad_low.astype(jnp.float32), axis=0)
        grad_keyval_w = grad_keyval_w + jnp.einsum(
            "td,tk->dk", low_first, half_grad_low, preferred_element_type=jnp.float32
        )
        query_rows = jnp.transpose(grad_queries, (1, 0, 2)) * query_scale
        grad_query_low = (
            rotate(query_rows, cos_table, -sine_table)
            .reshape(tokens_here, heads_here * HDIM)
            .astype(jnp.bfloat16)
        )
        grad_query_b = grad_query_b + jnp.sum(grad_query_low.astype(jnp.float32), axis=0)
        grad_query_w = grad_query_w + jnp.einsum(
            "td,tq->dq", low_first, grad_query_low, preferred_element_type=jnp.float32
        )
        first_part = jnp.einsum(
            "tq,dq->td", grad_query_low, w_query, preferred_element_type=jnp.float32
        ) + jnp.einsum("tk,dk->td", half_grad_low, w_keyval, preferred_element_type=jnp.float32)
        grad_first, grad_second = (
            lax.psum(first_part.astype(jnp.bfloat16), "tensor").astype(jnp.float32),
            lax.psum(second_part.astype(jnp.bfloat16), "tensor").astype(jnp.float32),
        )
        grad_n1_gain = grad_n1_gain + jnp.sum(grad_first * normed, axis=0)
        grad_n1_bias = grad_n1_bias + jnp.sum(grad_first, axis=0)
        grad_n2_gain = grad_n2_gain + jnp.sum(grad_second * normed, axis=0)
        grad_n2_bias = grad_n2_bias + jnp.sum(grad_second, axis=0)
        input_total = (
            grad_rows
            + norm_backward(grad_first, normed, scaling, norm1_gain)
            + norm_backward(grad_second, normed, scaling, norm2_gain)
        )
        input_rows.append(input_total.astype(jnp.bfloat16))
    summed_query, summed_keyval, summed_out, summed_up, summed_down = (
        lax.psum_scatter(grad_query_w, "dp", scatter_dimension=0, tiled=True),
        lax.psum_scatter(grad_keyval_w, "dp", scatter_dimension=0, tiled=True),
        lax.psum_scatter(grad_out_w, "dp", scatter_dimension=1, tiled=True),
        lax.psum_scatter(grad_up_w, "dp", scatter_dimension=0, tiled=True),
        lax.psum_scatter(grad_down_w, "dp", scatter_dimension=1, tiled=True),
    )
    vector_sums = lax.psum(
        (
            grad_n1_gain,
            grad_n1_bias,
            grad_n2_gain,
            grad_n2_bias,
            grad_row_sum,
            grad_query_b,
            grad_keyval_b,
            grad_up_b,
        ),
        "dp",
    )
    (
        sum_n1_gain,
        sum_n1_bias,
        sum_n2_gain,
        sum_n2_bias,
        sum_rows,
        sum_query_b,
        sum_keyval_b,
        sum_up_b,
    ) = vector_sums
    return (
        jnp.stack(layer_rows),
        jnp.stack(cache_rows),
        jnp.stack(input_rows),
        sum_n1_gain,
        sum_n1_bias,
        sum_n2_gain,
        sum_n2_bias,
        summed_query,
        sum_query_b,
        summed_keyval,
        sum_keyval_b,
        summed_out,
        sum_rows,
        summed_up,
        sum_up_b,
        summed_down,
        sum_rows,
    )


def nn(a, b):
    return jnp.dot(a, b, preferred_element_type=F32)


def nt(a, b):
    return lax.dot_general(a, b, (((1,), (1,)), ((), ())), preferred_element_type=F32)


def chunk_list(q_cols, kv_cols, ff_cols, pieces):
    sizes = [kv_cols] + [q_cols // 3] * 3 + [q_cols] + [ff_cols // pieces] * (2 * pieces)
    at = 0
    out = []
    for size in sizes:
        out.append((at, size))
        at += size
    return out


def near_tiles(n, half):
    own = REACH * n
    return [(own + a, half, a, n - a, True) for a in range(0, n, half)]


def far_tiles(n, half):
    own = REACH * n
    out = [(own - j * n, n, 0, n, False) for j in range(1, REACH)]
    return out + [(a, half, 0, min(n, a + half), False) for a in range(0, n, half)]


def spin(rows, cos, sine):
    h = ROT // 2
    a, b, rest = rows[..., :h, :], rows[..., h:ROT, :], rows[..., ROT:, :]
    return jnp.concatenate([a * cos - b * sine, b * cos + a * sine, rest], axis=-2)


def fused_kernel(
    chunks, pieces,
    x_in, dy_in, positions, g1, b1, g2, b2, w_query, b_query, w_keyval, b_keyval, w_out, b_out, w_up, b_up, w_down, b_down,
    layer_hbm, keyval_hbm, grad_hbm, grads_out, vec_out,
    x, dy, layer_out, keyval_out, input_grad, in_sem, out_sem,
    W, G, n1T, n2, n2T, dyT, wqT, qT, doT, o_nat, lse, dvec, kvwin, kvTwin, low_kv,
    cos, sine, start, m_s, l_s, acc, gbuf, dubuf, dqT, dkv, dkvT, turned, hs, hr, hx, hxr, kvo, yr, d2r,
    r1, r2, r3, vec, vp, vz, dql, dkl,
    gzs, gzr, g2s, g2r, g3s, g3r, a1s, a1r, a2s, a2r, azs, azr,
    hfs, hfr, hbs, hbr, fws, fwr, xs, xr, ts, tr, vs, vr,
):
    T, D = x.shape
    M, W_rows, KV = kvwin.shape
    n = T // M
    heads = qT.shape[0] // M
    pairs = heads // 2
    hq = heads * HDIM
    own = REACH * n
    piece = dubuf.shape[2]
    scale = HDIM ** (-0.5)
    me = lax.axis_index("dp")
    core = lax.axis_index("tensor")
    count = lax.axis_size("dp")
    z, y, xx = me // 4, (me // 2) % 2, me % 2
    shard_rows = w_query.shape[0]
    n_chunks = len(chunks)
    kKV, kQ, kO = 0, (1, 2, 3), 4
    kUp = [5 + 2 * c for c in range(pieces)]
    kDown = [6 + 2 * c for c in range(pieces)]
    mine = pl.ds(pl.multiple_of(core * HDIM, HDIM), HDIM)
    other = pl.ds(pl.multiple_of((1 - core) * HDIM, HDIM), HDIM)

    def at(zz, yy, xo):
        return {"dp": zz * 4 + yy * 2 + xo}

    z_ids = [at((z + d) % 4, y, xx) for d in (1, 2, 3)]
    y_id, x_id, d_id = at(z, 1 - y, xx), at(z, y, 1 - xx), at(z, 1 - y, 1 - xx)
    t_id = {"tensor": 1 - core}

    def send(src, dst, ss, rs, to):
        return pltpu.make_async_remote_copy(
            src_ref=src, dst_ref=dst, send_sem=ss, recv_sem=rs, device_id=to, device_id_type=MESH
        )

    loads = [pltpu.make_async_copy(a, b, in_sem.at[j]) for j, (a, b) in enumerate(((x_in, x), (dy_in, dy)))]
    for c in loads:
        c.start()

    bar = pltpu.get_barrier_semaphore()
    peers = z_ids + [y_id, x_id, d_id, t_id]
    peers += [{"dp": (me + s) % count} for s in range(1, REACH + 1)]
    peers += [{"dp": (me + count - s) % count} for s in range(1, REACH + 1)]
    for p in peers:
        pl.semaphore_signal(bar, inc=1, device_id=p, device_id_type=MESH)
    pl.semaphore_wait(bar, len(peers))

    def cols(k):
        return pl.ds(chunks[k][0], chunks[k][1])

    def halves(k):
        c0, cn = chunks[k]
        if cn < 256:
            return (pl.ds(c0, cn), None) if k % 2 == 0 else (None, pl.ds(c0, cn))
        first = cn // 256 * 128
        return pl.ds(c0, first), pl.ds(c0 + first, cn - first)

    def gather_z(k):
        r = W.at[z, y, xx, :, cols(k)]
        return [send(r, r, gzs.at[k, j], gzr.at[k, j], z_ids[j]) for j in range(3)]

    def gather_col(k):
        r = W.at[:, y, xx, :, cols(k)]
        return [send(r, r, g2s.at[k, 0], g2r.at[k, 0], x_id), send(r, r, g2s.at[k, 1], g2r.at[k, 1], y_id)]

    def gather_far(k):
        first, second = halves(k)
        out = []
        if first is not None:
            r = W.at[:, y, 1 - xx, :, first]
            out.append(send(r, r, g3s.at[k, 0], g3r.at[k, 0], y_id))
        if second is not None:
            r = W.at[:, 1 - y, xx, :, second]
            out.append(send(r, r, g3s.at[k, 1], g3r.at[k, 1], x_id))
        return out

    def start1(k):
        for c in gather_z(k):
            c.start()

    def step2(k):
        for c in gather_z(k):
            c.wait_recv()
        for c in gather_col(k):
            c.start()

    def step3(k):
        for c in gather_col(k):
            c.wait_recv()
        for c in gather_far(k):
            c.start()

    def arrived(k):
        for c in gather_far(k):
            c.wait_recv()

    def span(ks):
        ks = ks if isinstance(ks, tuple) else (ks,)
        return ks, chunks[ks[0]][0], sum(chunks[k][1] for k in ks)

    def weight(k):
        _, c0, cn = span(k)
        return W[:, :, :, :, c0 : c0 + cn].reshape(D, cn)

    def red1(k):
        first, second = halves(k)
        out = []
        if first is not None:
            out.append(send(G.at[:, :, 1 - xx, :, first], r1.at[:, :, :, first], a1s.at[k, 0], a1r.at[k, 0], x_id))
        if second is not None:
            out.append(send(G.at[:, 1 - y, :, :, second], r1.at[:, :, :, second], a1s.at[k, 1], a1r.at[k, 1], y_id))
        return out

    def red2(k):
        first, second = halves(k)
        out = []
        if first is not None:
            out.append(send(r1.at[:, 1 - y, :, first], r2.at[:, :, first], a2s.at[k, 0], a2r.at[k, 0], y_id))
        if second is not None:
            out.append(send(r1.at[:, 1 - xx, :, second], r2.at[:, :, second], a2s.at[k, 1], a2r.at[k, 1], x_id))
        return out

    def red3(k):
        return [
            send(r2.at[(z + j + 1) % 4, :, cols(k)], r3.at[j, :, cols(k)], azs.at[k, j], azr.at[k, j], z_ids[j])
            for j in range(3)
        ]

    def step_a(k):
        for c in red1(k):
            c.start()

    def step_b(k):
        first, second = halves(k)
        for c in red1(k):
            c.wait_recv()

        def add(i, _):
            zz, o = i // 2, i % 2
            if first is not None:
                r1[zz, o, :, first] = r1[zz, o, :, first] + G[zz, o, xx, :, first]
            if second is not None:
                r1[zz, o, :, second] = r1[zz, o, :, second] + G[zz, y, o, :, second]
            return 0

        lax.fori_loop(0, 8, add, 0)
        for c in red2(k):
            c.start()

    def step_c(k):
        first, second = halves(k)
        for c in red2(k):
            c.wait_recv()

        def add(i, _):
            if first is not None:
                r2[i, :, first] = r2[i, :, first] + r1[i, y, :, first]
            if second is not None:
                r2[i, :, second] = r2[i, :, second] + r1[i, xx, :, second]
            return 0

        lax.fori_loop(0, 4, add, 0)
        for c in red3(k):
            c.start()

    def step_e(k):
        for c in red3(k):
            c.wait_recv()
        total = r2[z, :, cols(k)].astype(F32)
        for j in range(3):
            total = total + r3[j, :, cols(k)].astype(F32)
        grads_out[:, cols(k)] = total

    def act(place_name):
        for move, k in SCHEDULE.get(place_name, ()):
            if move == "z":
                start1(k)
            elif move == "col":
                step2(k)
            elif move == "far":
                step3(k)
            elif move == "b":
                step_b(k)
            elif move == "c":
                step_c(k)
            elif move == "e":
                step_e(k)
            else:
                return_halo(k)

    def act_in(loop_name, i):
        for j in range(M * heads):
            if loop_name + str(j) in SCHEDULE:
                pl.when(i == j)(functools.partial(act, loop_name + str(j)))

    def place(k, block):
        _, c0, _ = span(k)
        W[z, y, xx, :, c0 : c0 + block.shape[1]] = block

    place(kKV, jnp.concatenate([w_keyval[...], jnp.zeros((shard_rows, HDIM), BF16)], axis=1))
    place(kQ, w_query[...])
    place(kO, w_out[...])
    for c in range(pieces):
        place(kUp[c], w_up[:, c * piece : (c + 1) * piece])
        place(kDown[c], w_down[:, c * piece : (c + 1) * piece])
    act("pro")

    R = 256
    vec[...] = jnp.zeros_like(vec)

    def row(ref):
        return ref[...].reshape(1, ref.shape[0])

    g1v, b1v, g2v, b2v = row(g1), row(b1), row(g2), row(b2)

    def xhat_of(rows):
        v = x[rows, :].astype(F32)
        c = v - jnp.mean(v, axis=-1, keepdims=True)
        rstd = lax.rsqrt(jnp.mean(c * c, axis=-1, keepdims=True) + epsilon)
        return v, c * rstd, rstd

    def norm_tile(i, _):
        rows = pl.ds(pl.multiple_of(i * R, R), R)
        _, xh, _ = xhat_of(rows)
        n1v = (xh * g1v + b1v).astype(BF16)
        n2v = (xh * g2v + b2v).astype(BF16)
        n2[rows, :] = n2v
        n1T[:, rows] = n1v.T
        n2T[:, rows] = n2v.T
        d = dy[rows, :]
        dyT[:, rows] = d.T
        vec[4:5, :] += jnp.sum(d.astype(F32), axis=0, keepdims=True)
        return 0

    for c in loads:
        c.wait()
    lax.fori_loop(0, T // R, norm_tile, 0)
    act("norm")
    h = ROT // 2
    index = lax.broadcasted_iota(jnp.int32, (h, 1), 0)
    inverse = jnp.zeros((h, 1), F32)
    for i in range(h):
        inverse = jnp.where(index == i, 10000.0 ** (-(2.0 * i) / ROT), inverse)
    for m in range(M):
        ms = slice(m * n, (m + 1) * n)
        place_row = positions[m : m + 1, :]
        angle = inverse * place_row.astype(F32)
        cos[:, ms] = jnp.cos(angle)
        sine[:, ms] = jnp.sin(angle)
        start[m] = lax.broadcasted_iota(jnp.int32, (1, n), 1) + own - place_row

    def keyval_spin(rows, m, sign):
        ms = slice(m * n, (m + 1) * n)
        return spin(rows, jnp.where(core == 0, cos[:, ms], 1.0), jnp.where(core == 0, sign * sine[:, ms], 0.0))

    def column(ref):
        size = ref.shape[0]
        return jnp.broadcast_to(ref[...].reshape(1, size), (8, size)).T[:, 0:1]

    act("cos")
    arrived(kKV)
    wkvT = weight(kKV).T[0:HDIM]
    bkv = column(b_keyval)
    for m in range(M):
        ms = slice(m * n, (m + 1) * n)
        low_kv[m] = keyval_spin(nn(wkvT, n1T[:, ms]) + bkv, m, 1.0).astype(BF16)
    kvTwin[:, mine, own : own + n] = low_kv[...]

    def block(s):
        return pl.ds((REACH - s) * n, n)

    def halo(s):
        return send(
            low_kv, kvTwin.at[:, mine, block(s)], hfs.at[s - 1], hfr.at[s - 1], {"dp": (me + s) % count}
        )

    def across(s):
        part = kvTwin.at[:, mine, block(s)]
        return send(part, part, fws.at[s], fwr.at[s], t_id)

    for s in range(1, REACH + 1):
        @pl.when(me + s < count)
        def _(s=s):
            halo(s).start()
    across(0).start()

    act("kv")
    across(0).wait_recv()
    for m in range(M):
        natural = kvTwin[m, :, own : own + n].T
        kvwin[m, own : own + n, :] = natural
        keyval_out[m] = natural
    stores = [
        pltpu.make_async_copy(a, b, out_sem.at[j])
        for j, (a, b) in enumerate(((keyval_out, keyval_hbm), (layer_out, layer_hbm)))
    ]
    stores[0].start()
    act("own")
    for k in kQ:
        arrived(k)
    wqT[...] = weight(kQ).T
    bq = column(b_query)
    for m in range(M):
        ms = slice(m * n, (m + 1) * n)
        lin = nn(wqT[...], n1T[:, ms]) + bq
        spun = spin(lin.reshape(heads, HDIM, n), cos[:, ms], sine[:, ms]) * scale
        qT[m * heads : (m + 1) * heads] = spun.astype(BF16)
    act("q")

    near, far = near_tiles(n, n // 2), far_tiles(n, n // 2)
    tops, totals, sums = lse, dvec, dqT

    def visible(w0, kn, q0, qn, first, causal):
        key = lax.broadcasted_iota(jnp.int32, (kn, 1), 0) + w0
        seen = key >= first
        if causal:
            query = lax.broadcasted_iota(jnp.int32, (1, qn), 1) + (q0 + own)
            seen = seen & (key <= query)
        return seen

    def padded_query(i):
        return jnp.concatenate([qT[i], jnp.zeros((KV - HDIM, n), BF16)], axis=0)

    def forward_tiles(i, tiles):
        m = i // pairs
        first = start[m]
        queries = [padded_query(2 * i + t) for t in range(2)]

        def scores(t, tile):
            w0, kn, q0, qn, causal = tile
            qs = slice(q0, q0 + qn)
            sc = nn(kvwin[m, w0 : w0 + kn, :], queries[t][:, qs])
            return jnp.where(visible(w0, kn, q0, qn, first[:, qs], causal), sc, LOW)

        def take(t, tile, sc):
            w0, kn, q0, qn, _ = tile
            qs = slice(q0, q0 + qn)
            before = m_s[t, :, qs]
            top = jnp.maximum(before, jnp.max(sc, axis=0, keepdims=True))
            p = jnp.exp(sc - top)
            shrink = jnp.exp(before - top)
            l_s[t, :, qs] = l_s[t, :, qs] * shrink + jnp.sum(p, axis=0, keepdims=True)
            m_s[t, :, qs] = top
            acc[t, :, qs] = acc[t, :, qs] * shrink + nn(kvTwin[m, HDIM:KV, w0 : w0 + kn], p.astype(BF16))

        ready = [scores(t, tiles[0]) for t in range(2)]
        for at_tile, tile in enumerate(tiles):
            ahead = None
            if at_tile + 1 < len(tiles):
                ahead = [scores(t, tiles[at_tile + 1]) for t in range(2)]
            for t in range(2):
                take(t, tile, ready[t])
            ready = ahead

    def forward_near(i, _):
        m_s[...] = jnp.full_like(m_s, LOW)
        l_s[...] = jnp.zeros_like(l_s)
        acc[...] = jnp.zeros_like(acc)
        forward_tiles(i, near)
        both = pl.ds(2 * i, 2)
        tops[both], totals[both], sums[both] = m_s[...], l_s[...], acc[...]
        return 0

    def forward_far(i, _):
        m = i // pairs
        both = pl.ds(2 * i, 2)
        m_s[...], l_s[...], acc[...] = tops[both], totals[both], sums[both]
        forward_tiles(i, far)
        o = acc[...] / l_s[...]
        sums[both] = o
        lse[both] = m_s[...] + jnp.log(l_s[...])
        rows = pl.ds(pl.multiple_of(m * n, n), n)
        lanes = pl.ds(pl.multiple_of((i % pairs) * 2 * HDIM, 2 * HDIM), 2 * HDIM)
        o_nat[rows, lanes] = o.astype(BF16).reshape(2 * HDIM, n).T
        act_in("far", i)
        return 0

    def near_step(i, _):
        forward_near(i, 0)
        act_in("near", i)
        return 0

    lax.fori_loop(0, M * pairs, near_step, 0)
    for s in range(1, REACH + 1):
        @pl.when(me >= s)
        def _(s=s):
            halo(s).wait_recv()
            across(s).start()

        @pl.when(me < s)
        def _(s=s):
            kvTwin[:, :, block(s)] = jnp.zeros((M, KV, n), BF16)

    act("halow")
    for s in range(1, REACH + 1):
        @pl.when(me >= s)
        def _(s=s):
            across(s).wait_recv()

        for m in range(M):
            kvwin[m, block(s), :] = kvTwin[m, :, block(s)].T

    act("acw")
    lax.fori_loop(0, M * pairs, forward_far, 0)

    arrived(kO)
    wo = weight(kO).T
    for m in range(M):
        ms = slice(m * n, (m + 1) * n)
        doT[m * heads : (m + 1) * heads] = nn(wo, dyT[:, ms]).astype(BF16).reshape(heads, HDIM, n)

    def mix_dots(i, _):
        dvec[i] = jnp.sum(doT[i].astype(F32) * sums[i], axis=0, keepdims=True)
        return 0

    lax.fori_loop(0, M * heads, mix_dots, 0)

    def put_grad(ks, leftT, right):
        ks, c0, cn = span(ks)

        part = nn(leftT[...], right[...]).astype(BF16)
        G[:, :, :, :, c0 : c0 + cn] = part.reshape(4, 2, 2, shard_rows, cn)
        for k in ks:
            step_a(k)

    put_grad(kO, dyT, o_nat)
    act("mix")

    def feed_forward(c):
        ku, kd = kUp[c], kDown[c]
        arrived(ku)
        arrived(kd)
        (u0, _), (d0, _) = chunks[ku], chunks[kd]
        up_bias = b_up[c * piece : (c + 1) * piece].reshape(1, piece)

        def rows_tile(i, _):
            rows = pl.ds(pl.multiple_of(i * 2 * R, 2 * R), 2 * R)
            u = nn(n2[rows, :], W[:, :, :, :, u0 : u0 + piece].reshape(D, piece)) + up_bias
            phi = 0.5 * (1.0 + lax.erf(u * 0.7071067811865476))
            slope = phi + u * (jnp.exp(-0.5 * u * u) * 0.3989422804014327)
            gbuf[rows, c * piece : (c + 1) * piece] = (u * phi).astype(BF16)
            dg = nn(dy[rows, :], W[:, :, :, :, d0 : d0 + piece].reshape(D, piece))
            dubuf[c, rows, :] = (slope * dg).astype(BF16)
            return 0

        lax.fori_loop(0, T // R // 2, rows_tile, 0)
        put_grad(ku, n2T, dubuf.at[c])
        put_grad(kd, dyT, gbuf.at[:, c * piece : (c + 1) * piece])

    def branch_tile(i, _):
        rows = pl.ds(pl.multiple_of(i * R, R), R)
        total = nt(o_nat[rows, :], weight(kO))
        back = jnp.zeros((R, D), F32)
        for c in range(pieces):
            total = total + nt(gbuf[rows, c * piece : (c + 1) * piece], weight(kDown[c]))
            back = back + nt(dubuf[c, rows, :], weight(kUp[c]))
        layer_out[rows, :] = total.astype(BF16)
        input_grad[rows, :] = back.astype(BF16)
        return 0

    y_copy = send(layer_out, yr, xs.at[0], xr.at[0], t_id)
    d2_copy = send(input_grad, d2r, xs.at[1], xr.at[1], t_id)

    def branches():
        lax.fori_loop(0, T // R, branch_tile, 0)
        y_copy.start()
        d2_copy.start()
        for c in range(pieces):
            part = jnp.sum(dubuf[c].astype(F32), axis=0, keepdims=True)
            done = 0
            while done < piece:
                flat = c * piece + done
                line, col = flat // D, flat % D
                width = min(piece - done, D - col)
                vec[6 + line : 7 + line, col : col + width] = part[:, done : done + width]
                done += width

    feed_forward(0)
    act("ffn0")

    dkv[...] = jnp.zeros_like(dkv)

    def backward_tiles(i, tiles):
        m = i // heads
        zero = jnp.zeros((HDIM, n), BF16)
        query = jnp.concatenate([qT[i], zero], axis=0)
        cotangent = jnp.concatenate([zero, doT[i]], axis=0)
        natural = jnp.concatenate([qT[i], doT[i]], axis=0).T
        first, ls, dots = start[m], lse[i], dvec[i]
        step = n // 2
        pieces_of = [(w0 + a, step, q0, qn, c) for w0, kn, q0, qn, c in tiles for a in range(0, kn, step)]

        def products(tile):
            w0, kn, q0, qn, causal = tile
            qs = slice(q0, q0 + qn)
            rows = kvwin[m, w0 : w0 + kn, :]
            sc = nn(rows, query[:, qs])
            sc = jnp.where(visible(w0, kn, q0, qn, first[:, qs], causal), sc, LOW)
            return sc, nn(rows, cotangent[:, qs])

        ready = products(pieces_of[0])
        for at_tile, tile in enumerate(pieces_of):
            ahead = products(pieces_of[at_tile + 1]) if at_tile + 1 < len(pieces_of) else None
            w0, kn, q0, qn, _ = tile
            qs = slice(q0, q0 + qn)
            sc, dp = ready
            p = jnp.exp(sc - ls[:, qs])
            ds = (p * (dp - dots[:, qs])).astype(BF16)
            for_k = nn(ds, natural[qs])
            for_v = nn(p.astype(BF16), natural[qs])
            lane = lax.broadcasted_iota(jnp.int32, for_k.shape, 1)
            dkv[m, w0 : w0 + kn, :] += jnp.where(lane < HDIM, for_k, for_v)
            dqT[i, :, qs] += nn(kvTwin[m, 0:HDIM, w0 : w0 + kn], ds)
            ready = ahead

    def backward_far(i, _):
        @pl.when(i == FEED_AT[0])
        def _():
            feed_forward(1)
            act("ffn1")

        @pl.when(i == FEED_AT[1])
        def _():
            feed_forward(2)
            branches()
            act("ffn2")

        dqT[i] = jnp.zeros((HDIM, n), F32)
        backward_tiles(i, far)
        for m in range(M):
            pl.when(i == (m + 1) * heads - 1)(functools.partial(give_half, m))
        act_in("bfar", i)
        return 0

    def backward_near(i, _):
        backward_tiles(i, near)
        for m in range(M):
            pl.when(i == (m + 1) * heads - 1)(functools.partial(give_own, m))
        act_in("bnear", i)
        return 0

    def back_copy(s, m):
        return send(
            hs.at[s - 1, m], hr.at[s - 1, m], hbs.at[s - 1, m], hbr.at[s - 1, m],
            {"dp": (me + count - s) % count},
        )

    def half_copy(m):
        part = pl.ds(0, own)
        return send(hx.at[m, :, part], hxr.at[m, :, part], xs.at[2 + m], xr.at[2 + m], t_id)

    def own_copy(m):
        part = pl.ds(own, n)
        return send(hx.at[m, :, part], hxr.at[m, :, part], xs.at[2 + M + m], xr.at[2 + M + m], t_id)

    def split(m, j):
        js = slice(j * n, (j + 1) * n)
        turned[...] = dkv[m, js, :].T
        dkvT[m, :, js] = turned[mine, :]
        hx[m, :, js] = turned[other, :].astype(BF16)

    def give_half(m):
        for j in range(REACH):
            split(m, j)
        half_copy(m).start()

    def return_halo(m):
        half_copy(m).wait_recv()
        for j in range(REACH):
            js = slice(j * n, (j + 1) * n)
            hs[REACH - j - 1, m] = (dkvT[m, :, js] + hxr[m, :, js].astype(F32)).astype(BF16)
        for s in range(1, REACH + 1):
            @pl.when(me >= s)
            def _(s=s):
                back_copy(s, m).start()

    def give_own(m):
        split(m, REACH)
        own_copy(m).start()

    lax.fori_loop(0, M * heads, backward_far, 0)
    lax.fori_loop(0, M * heads, backward_near, 0)

    for m in range(M):
        ms = slice(m * n, (m + 1) * n)
        rows = dqT[m * heads : (m + 1) * heads] * scale
        low = spin(rows, cos[:, ms], -sine[:, ms]).astype(BF16)
        dql[ms, :] = low.reshape(hq, n).T
    put_grad(kQ, n1T, dql)
    vec[5:6, 0:hq] = jnp.sum(dql[...].astype(F32), axis=0, keepdims=True)
    act("t0")

    for m in range(M):
        ms = slice(m * n, (m + 1) * n)
        own_copy(m).wait_recv()
        dko = dkvT[m, :, own : own + n] + hxr[m, :, own : own + n].astype(F32)
        kvo[...] = dko
        for s in range(1, REACH + 1):
            @pl.when(me + s < count)
            def _(s=s, m=m):
                back_copy(s, m).wait_recv()
                kvo[...] += hr[s - 1, m].astype(F32)
        low = keyval_spin(kvo[...], m, -1.0).astype(BF16)
        dkl[ms, :] = jnp.concatenate([low, jnp.zeros((KV - HDIM, n), BF16)], axis=0).T
    put_grad(kKV, n1T, dkl)
    vec[5:6, hq : hq + KV] = jnp.sum(dkl[...].astype(F32), axis=0, keepdims=True)
    act("t1")

    def d1_copy(i):
        rows = pl.ds(pl.multiple_of(i * R, R), R)
        return send(gbuf.at[rows, pl.ds(0, D)], n2.at[rows], ts.at[i], tr.at[i], t_id)

    def first_tile(i, _):
        rows = pl.ds(pl.multiple_of(i * R, R), R)
        gbuf[rows, 0:D] = (nt(dql[rows, :], weight(kQ)) + nt(dkl[rows, :], weight(kKV))).astype(BF16)
        d1_copy(i).start()
        return 0

    lax.fori_loop(0, T // R, first_tile, 0)
    act("t2")

    y_copy.wait()
    both_bias = row(b_out) + row(b_down)

    def out_tile(i, _):
        rows = pl.ds(pl.multiple_of(i * R, R), R)
        both = (layer_out[rows, :].astype(F32) + yr[rows, :].astype(F32)) + both_bias
        layer_out[rows, :] = (x[rows, :].astype(F32) + both).astype(BF16)
        return 0

    lax.fori_loop(0, T // R, out_tile, 0)
    stores[1].start()
    act("t3")
    d2_copy.wait()

    def grad_store(i):
        rows = pl.ds(pl.multiple_of(i * R, R), R)
        return pltpu.make_async_copy(input_grad.at[rows], grad_hbm.at[rows], out_sem.at[2 + i])

    def last_tile(i, _):
        rows = pl.ds(pl.multiple_of(i * R, R), R)
        _, xh, rstd = xhat_of(rows)
        d1_copy(i).wait_recv()
        dn1 = gbuf[rows, 0:D].astype(F32) + n2[rows, :].astype(F32)
        dn2 = input_grad[rows, :].astype(F32) + d2r[rows, :].astype(F32)
        vec[0:1, :] += jnp.sum(dn1 * xh, axis=0, keepdims=True)
        vec[1:2, :] += jnp.sum(dn1, axis=0, keepdims=True)
        vec[2:3, :] += jnp.sum(dn2 * xh, axis=0, keepdims=True)
        vec[3:4, :] += jnp.sum(dn2, axis=0, keepdims=True)
        a = dn1 * g1v + dn2 * g2v
        back = a - jnp.mean(a, axis=-1, keepdims=True) - xh * jnp.mean(a * xh, axis=-1, keepdims=True)
        input_grad[rows, :] = (dy[rows, :].astype(F32) + rstd * back).astype(BF16)
        grad_store(i).start()
        return 0

    lax.fori_loop(0, T // R, last_tile, 0)

    flat = y * 2 + xx
    vp[flat] = vec[...]
    plane = [send(vp.at[flat], vp.at[flat], vs.at[j], vr.at[j], to) for j, to in enumerate((x_id, y_id, d_id))]
    for c in plane:
        c.start()
    act("t4")
    for c in plane:
        c.wait_recv()
    vz[z] = (vp[0] + vp[1]) + (vp[2] + vp[3])
    along = [send(vz.at[z], vz.at[z], vs.at[3 + j], vr.at[3 + j], z_ids[j]) for j in range(3)]
    for c in along:
        c.start()
    act("t5")
    for c in along:
        c.wait_recv()
    act("t6")
    vec_out[...] = (vz[0] + vz[1]) + (vz[2] + vz[3])

    for k in range(n_chunks):
        for c in gather_z(k) + gather_col(k) + gather_far(k) + red1(k) + red2(k) + red3(k):
            c.wait_send()
    across(0).wait_send()
    for s in range(1, REACH + 1):
        @pl.when(me + s < count)
        def _(s=s):
            halo(s).wait_send()

        @pl.when(me >= s)
        def _(s=s):
            across(s).wait_send()
            for m in range(M):
                back_copy(s, m).wait_send()
    for m in range(M):
        half_copy(m).wait_send()
        own_copy(m).wait_send()
    for i in range(T // R):
        d1_copy(i).wait_send()
        grad_store(i).wait()
    for c in stores:
        c.wait()
    for c in plane + along:
        c.wait_send()


def finish_kernel(
    chunks, pieces,
    y_in, kv_in, x_in, grads, vec,
    y_out, kv_out, x_out, n1g, n1b, n2g, n2b, wq, bq, wkv, bkv, wo, bo, wu, bu, wd, bd,
    y_buf, kv_buf, x_buf, in_sem, out_sem,
):
    loads, stores = [], []
    half_rows = pl.ds(0, y_in.shape[0] // 2), pl.ds(y_in.shape[0] // 2, y_in.shape[0] // 2)
    for a, buf, b in (
        (y_in.at[half_rows[0]], y_buf.at[half_rows[0]], y_out.at[half_rows[0]]),
        (y_in.at[half_rows[1]], y_buf.at[half_rows[1]], y_out.at[half_rows[1]]),
        (x_in.at[half_rows[0]], x_buf.at[half_rows[0]], x_out.at[half_rows[0]]),
        (x_in.at[half_rows[1]], x_buf.at[half_rows[1]], x_out.at[half_rows[1]]),
        (kv_in, kv_buf, kv_out),
    ):
        loads.append(pltpu.make_async_copy(a, buf, in_sem.at[len(loads)]))
        stores.append(pltpu.make_async_copy(buf, b, out_sem.at[len(stores)]))
    for c in loads:
        c.start()
    for load, store in zip(loads, stores):
        load.wait()
        store.start()
    hq, half, piece, D = wq.shape[1], wkv.shape[1], chunks[5][1], vec.shape[1]
    for out, r in ((n1g, 0), (n1b, 1), (n2g, 2), (n2b, 3), (bo, 4), (bd, 4)):
        out[...] = vec[r].reshape(D)
    q0, o0 = chunks[1][0], chunks[4][0]
    wq[...] = grads[:, q0 : q0 + hq]
    wkv[...] = grads[:, 0:half]
    wo[...] = grads[:, o0 : o0 + hq]
    for c in range(pieces):
        u0, d0 = chunks[5 + 2 * c][0], chunks[6 + 2 * c][0]
        wu[:, c * piece : (c + 1) * piece] = grads[:, u0 : u0 + piece]
        wd[:, c * piece : (c + 1) * piece] = grads[:, d0 : d0 + piece]
    bq[...] = vec[5:6, 0:hq].reshape(hq)
    bkv[...] = vec[5:6, hq : hq + half].reshape(half)
    for r in range(bu.shape[0] // D):
        bu[r * D : (r + 1) * D] = vec[6 + r].reshape(D)
    for c in stores:
        c.wait()


def fused_layer(arguments, pieces):
    (hidden_in, positions, out_grad, g1, b1, g2, b2, w_query, b_query, w_keyval, b_keyval,
     w_out, b_out, w_up, b_up, w_down, b_down) = arguments
    M, n, D = hidden_in.shape
    T = M * n
    hq, F, half, rows = b_query.shape[0], b_up.shape[0], b_keyval.shape[0], w_query.shape[0]
    heads, KV, piece = hq // HDIM, 2 * half, F // pieces
    chunks = chunk_list(hq, KV, F, pieces)
    C = chunks[-1][0] + chunks[-1][1]
    k = len(chunks)
    Wn = (REACH + 1) * n
    V = pltpu.VMEM
    S = pltpu.SemaphoreType.DMA
    sds = jax.ShapeDtypeStruct
    vm = pl.BlockSpec(memory_space=pltpu.VMEM)
    mh = M * heads
    hbm = pl.BlockSpec(memory_space=pl.ANY)
    scratch = [
        V((T, D), BF16), V((T, D), BF16), V((T, D), BF16), V((M, n, KV), BF16), V((T, D), BF16),
        S((2,)), S((2 + T // 256,)),
        V((4, 2, 2, rows, C), BF16), V((4, 2, 2, rows, C), BF16),
        V((D, T), BF16), V((T, D), BF16), V((D, T), BF16), V((D, T), BF16),
        V((hq, D), BF16), V((mh, HDIM, n), BF16), V((mh, HDIM, n), BF16),
        V((T, hq), BF16), V((mh, 1, n), F32), V((mh, 1, n), F32),
        V((M, Wn, KV), BF16), V((M, KV, Wn), BF16), V((M, HDIM, n), BF16),
        V((ROT // 2, T), F32), V((ROT // 2, T), F32), V((M, 1, n), jnp.int32),
        V((2, 1, n), F32), V((2, 1, n), F32), V((2, HDIM, n), F32),
        V((T, F), BF16), V((pieces, T, piece), BF16),
        V((mh, HDIM, n), F32), V((M, Wn, KV), F32), V((M, HDIM, Wn), F32), V((KV, n), F32),
        V((REACH, M, HDIM, n), BF16), V((REACH, M, HDIM, n), BF16),
        V((M, HDIM, Wn), BF16), V((M, HDIM, Wn), BF16), V((HDIM, n), F32),
        V((T, D), BF16), V((T, D), BF16),
        V((4, 2, rows, C), BF16), V((4, rows, C), BF16), V((3, rows, C), BF16),
        V((8, D), F32), V((4, 8, D), F32), V((4, 8, D), F32),
        V((T, hq), BF16), V((T, KV), BF16),
        S((k, 3)), S((k, 3)), S((k, 2)), S((k, 2)), S((k, 2)), S((k, 2)),
        S((k, 2)), S((k, 2)), S((k, 2)), S((k, 2)), S((k, 3)), S((k, 3)),
        S((REACH,)), S((REACH,)), S((REACH, M)), S((REACH, M)), S((REACH + 1,)), S((REACH + 1,)),
        S((2 + 2 * M,)), S((2 + 2 * M,)), S((T // 256,)), S((T // 256,)), S((6,)), S((6,)),
    ]
    y_out, kv_out, x_out, grads, vec = pl.pallas_call(
        functools.partial(fused_kernel, chunks, pieces),
        out_shape=(
            sds((T, D), BF16), sds((M, n, KV), BF16), sds((T, D), BF16), sds((rows, C), F32), sds((8, D), F32),
        ),
        in_specs=[hbm] * 2 + [vm] * 15,
        out_specs=(hbm,) * 3 + (vm,) * 2,
        scratch_shapes=scratch,
        compiler_params=pltpu.CompilerParams(
            collective_id=0, has_side_effects=True, vmem_limit_bytes=62 << 20
        ),
        name="fused_layer",
    )(hidden_in.reshape(T, D), out_grad.reshape(T, D), positions, g1, b1, g2, b2, w_query, b_query,
      w_keyval, b_keyval, w_out.T, b_out, w_up, b_up, w_down.T, b_down)
    vector = sds((D,), F32)
    out_shape = (
        sds((T, D), BF16), sds((M, n, KV), BF16), sds((T, D), BF16), vector, vector, vector, vector,
        sds(w_query.shape, F32), sds(b_query.shape, F32), sds(w_keyval.shape, F32), sds(b_keyval.shape, F32),
        sds(w_out.shape[::-1], F32), vector, sds(w_up.shape, F32), sds(b_up.shape, F32), sds(w_down.shape[::-1], F32), vector,
    )
    outs = pl.pallas_call(
        functools.partial(finish_kernel, chunks, pieces),
        out_shape=out_shape,
        in_specs=[hbm] * 3 + [vm] * 2,
        out_specs=(hbm,) * 3 + (vm,) * 14,
        scratch_shapes=[V((T, D), BF16), V((M, n, KV), BF16), V((T, D), BF16), S((5,)), S((5,))],
        compiler_params=pltpu.CompilerParams(vmem_limit_bytes=60 << 20),
        name="finish_layer",
    )(y_out, kv_out, x_out, grads, vec)
    outs = list(outs)
    outs[0], outs[2] = outs[0].reshape(hidden_in.shape), outs[2].reshape(hidden_in.shape)
    outs[11], outs[15] = outs[11].T, outs[15].T
    return tuple(outs)


PIECES = 3


def fits_fused(hidden_in, query_weight, up_weight):
    rows, hq = query_weight.shape
    return (
        lax.axis_size("dp") == 16
        and rows % 16 == 0
        and hq % 384 == 0
        and up_weight.shape[1] % (PIECES * 256) == 0
        and up_weight.shape[1] >= hidden_in.shape[2]
        and hidden_in.shape[1] % 256 == 0
        and hidden_in.shape[0] * hidden_in.shape[1] % 512 == 0
    )


def on_device(*arguments):
    if fits_fused(arguments[0], arguments[7], arguments[13]):
        return fused_layer(arguments, PIECES)
    return plain_layer(*arguments)


def solution(mesh):
    return jax.shard_map(
        on_device,
        mesh=mesh,
        in_specs=(
            P(None, "dp", None),
            P(None, "dp"),
            P(None, "dp", None),
            P(),
            P(),
            P(),
            P(),
            P("dp", "tensor"),
            P("tensor"),
            P("dp", "tensor"),
            P("tensor"),
            P("tensor", "dp"),
            P(),
            P("dp", "tensor"),
            P("tensor"),
            P("tensor", "dp"),
            P(),
        ),
        out_specs=(
            P(None, "dp", None),
            P(None, "dp", None),
            P(None, "dp", None),
            P(),
            P(),
            P(),
            P(),
            P("dp", "tensor"),
            P("tensor"),
            P("dp", "tensor"),
            P("tensor"),
            P("tensor", "dp"),
            P(),
            P("dp", "tensor"),
            P("tensor"),
            P("tensor", "dp"),
            P(),
        ),
        check_vma=False,
    )
```
